128 devices in a mesh: row: 16 (over x, y), col: 8 (over z, core).
Axes of the slice: x: 4, y: 4, z: 4, core: 2. Of those that a mesh axis runs over, the one named last changes fastest.
Arguments:
- reduced_basis: bfloat16 [5, 96, 65536], P(None, None, ('row', 'col')), may hold values from -6 to 6
- cell_jacobian: float32 [5, 5, 65536], P(None, None, ('row', 'col')), may hold values from -4 to 4
- face_cells: int32 [2, 131072], P(None, ('row', 'col')), may hold values from 0 to 511, as said below
- face_jacobian: float32 [2, 5, 5, 131072], P(None, None, None, ('row', 'col')), may hold values from -3 to 3
- limiter_flags: int32 [131072], P(('row', 'col')), may hold values 0 or 1
- viscosity: float32 [5], replicated, may hold values from 0.1 to 1
- ghost_cells: int32 [20480], P(('row', 'col')), may hold values from 0 to 511
- ghost_jacobian: float32 [5, 5, 20480], P(None, None, ('row', 'col')), may hold values from -3 to 3
- ghost_counts: int32 [1024], P(('row', 'col')), may hold values from 4 to 32, as said below
- receive_cells: int32 [20480], P(('row', 'col')), may hold values from 0 to 511
- coordinates: float32 [96], replicated, may hold values from -5 to 5
- base_residual: float32 [5, 65536], P(None, ('row', 'col')), may hold values from -6 to 6
Outputs:
- test_basis: bfloat16 [5, 96, 65536], P(None, None, ('row', 'col'))
- triangular_factor: float32 [97, 97], replicated
- gauss_step: float32 [96], replicated
The draws below stay inside these ranges and needn't reach their ends.
Inputs may be any that keep to these rules, and one draw needn't show every extreme that they name: `face_cells`: the two cells of a face differ and lie at most 64 apart modulo 512. `ghost_counts`: entry 8 p + m counts the used slots of block m of partition p: from half of the block's size to all of it (32 for the first four blocks, 8 for the last four); in every draw some partition uses all slots of all its blocks.
All inputs are finite; a program needn't handle non-finite values. No bound on the sum of `limiter_flags` on one device may be relied on, other than what follows from the above.
Results may differ from the reference program's by a relative error of at most 0.0095.
Values may be sent and summed in bfloat16 or wider, within the bound.
No kernel may reach another device: no remote copies, remote signals or barrier semaphores. Data moves between devices by JAX's collectives and lax.ppermute only.
A program may use at most 64 MiB of HBM per device.

```python
import math
import jax
import jax.numpy as jnp
import numpy as np
from jax import lax

F = 5
K = 96
CELLS_DEV = 512
FACE_CAP = 32
EDGE_CAP = 8
NCELLS = 65536
FACES = 131072
SLOTS_ALL = 20480
N_ROW = 16
N_COL = 8
DEVICES = 128


def draw_face_cells(key, part):
    left_cells = jax.random.randint(jax.random.fold_in(key, 11), (FACES,), 0, CELLS_DEV)
    stride_offset = jax.random.randint(jax.random.fold_in(key, 12), (FACES,), 1, 65)
    right_cells = (left_cells + stride_offset) % CELLS_DEV
    return jnp.stack([left_cells, right_cells]).astype(jnp.int32)


def draw_ghost_counts(key, part):
    capacity = jnp.tile(jnp.array([FACE_CAP] * 4 + [EDGE_CAP] * 4, jnp.int32), DEVICES)
    lowest_count = capacity // 2
    sampled = jax.random.randint(jax.random.fold_in(key, 21), (8 * DEVICES,), 0, 1 << 20)
    counts = lowest_count + sampled % (capacity - lowest_count + 1)
    chosen = jax.random.randint(jax.random.fold_in(key, 22), (), 0, DEVICES)
    owning_device = jnp.arange(8 * DEVICES, dtype=jnp.int32) // 8
    return jnp.where(owning_device == chosen, capacity, counts).astype(jnp.int32)


def touch_ends(entries, own_key, least, high):
    longest = entries.shape.index(max(entries.shape))
    spots = []
    for shift in (0, 1):
        where = [jax.random.randint(jax.random.fold_in(own_key, axis), (), 0, length) for axis, length in enumerate(entries.shape)]
        where[longest] = (where[longest] + shift) % entries.shape[longest]
        spots.append(tuple(where))
    return entries.at[spots[0]].set(least).at[spots[1]].set(high)


def levels(key, dims, shards, least, largest):
    def one(dim, shards_of):
        draws = jax.random.uniform(jax.random.fold_in(jax.random.fold_in(key, 6), dim), (shards_of,), jnp.float32, least / len(shards), largest / len(shards))
        return jnp.repeat(jnp.exp(draws), dims[dim] // shards_of).reshape((-1,) + (1,) * (len(dims) - dim - 1))

    gain = one(*shards[0])
    for cut in shards[1:]:
        gain = gain * one(*cut)
    return gain


def gaussian(stream_key, extent, width, most, pieces=(), kind=jnp.bfloat16):
    entries = width * jax.random.normal(stream_key, extent, jnp.float32)
    if pieces:
        entries = entries * levels(stream_key, extent, pieces, -0.22, 0.18)
    return jnp.clip(entries, -most, most).astype(kind)


def setup_inputs(seed: int = 0) -> dict:
    key_list = jax.random.split(jax.random.key(seed), 13)
    return {
        "reduced_basis": gaussian(key_list[0], (F, K, NCELLS), 1.0, 6.0, ((2, 128),)),
        "cell_jacobian": gaussian(key_list[1], (F, F, NCELLS), 0.5, 4.0, ((2, 128),), jnp.float32),
        "face_cells": draw_face_cells(jax.random.fold_in(key_list[12], 71), 0),
        "face_jacobian": gaussian(key_list[3], (2, F, F, FACES), 0.3, 3.0, ((3, 128),), jnp.float32),
        "limiter_flags": touch_ends((jax.random.randint(key_list[4], (FACES,), 0, 4) < 1).astype(jnp.int32), jax.random.fold_in(key_list[4], 1), 0, 1),
        "viscosity": jnp.clip(jnp.exp(jax.random.uniform(key_list[5], (F,), jnp.float32, math.log(0.1), math.log(1.0))), 0.1, 1.0),
        "ghost_cells": touch_ends(jax.random.randint(key_list[6], (SLOTS_ALL,), 0, CELLS_DEV), jax.random.fold_in(key_list[6], 1), 0, CELLS_DEV - 1).astype(jnp.int32),
        "ghost_jacobian": gaussian(key_list[7], (F, F, SLOTS_ALL), 0.3, 3.0, ((2, 128),), jnp.float32),
        "ghost_counts": draw_ghost_counts(jax.random.fold_in(key_list[12], 71), 0),
        "receive_cells": touch_ends(jax.random.randint(key_list[9], (SLOTS_ALL,), 0, CELLS_DEV), jax.random.fold_in(key_list[9], 1), 0, CELLS_DEV - 1).astype(jnp.int32),
        "coordinates": gaussian(key_list[10], (K,), 1.0, 5.0, (), jnp.float32),
        "base_residual": gaussian(key_list[11], (F, NCELLS), 1.0, 6.0, ((1, 128),), jnp.float32),
    }


direction_offsets = ((-1, 0), (1, 0), (0, -1), (0, 1), (-1, -1), (-1, 1), (1, -1), (1, 1))

def block_sizes():
    return [FACE_CAP] * 4 + [EDGE_CAP] * 4

def slot_limits(counts):
    capacity_each = block_sizes()
    slot_owner = np.concatenate([np.full(total_quantity, position, np.int32) for position, total_quantity in enumerate(capacity_each)])
    slot_position = np.concatenate([np.arange(total_quantity, dtype=np.int32) for total_quantity in capacity_each])
    compare = slot_owner[None, :] == np.arange(8, dtype=np.int32)[:, None]
    slot_limit = lax.optimization_barrier(jnp.sum(jnp.where(compare, counts[:, None], 0), axis=0))
    return slot_position < slot_limit

def upper_cholesky(matrix):
    order = matrix.shape[0]
    indices = jnp.arange(order, dtype=jnp.int32)

    def column_step(column, lower):
        row_vector = lax.dynamic_slice_in_dim(lower, column, 1, 0)[0]
        target = lax.dynamic_slice_in_dim(matrix, column, 1, 1)[:, 0]
        remain = target - jnp.dot(lower, row_vector, precision=lax.Precision.HIGHEST)
        pivot = jnp.sqrt(jnp.sum(jnp.where(indices == column, remain, 0.0)))
        new_column = jnp.where(indices > column, remain / pivot, jnp.where(indices == column, pivot, 0.0))
        return lax.dynamic_update_slice_in_dim(lower, new_column[:, None], column, 1)
    lower = lax.fori_loop(0, order, column_step, jnp.zeros_like(matrix))
    return lower.T

def upper_solve(upper, rhs):
    order = upper.shape[0]
    indices = jnp.arange(order, dtype=jnp.int32)

    def row_step(turn, solution):
        place = order - 1 - turn
        upper_row = lax.dynamic_slice_in_dim(upper, place, 1, 0)[0]
        known = jnp.dot(upper_row, solution, precision=lax.Precision.HIGHEST)
        pivot = jnp.sum(jnp.where(indices == place, upper_row, 0.0))
        target = jnp.sum(jnp.where(indices == place, rhs, 0.0))
        return jnp.where(indices == place, (target - known) / pivot, solution)
    return lax.fori_loop(0, order, row_step, jnp.zeros_like(rhs))

def per_device(array, devices):
    split_array = array.reshape(array.shape[:-1] + (devices, array.shape[-1] // devices))
    return jnp.moveaxis(split_array, -2, 0)

def ghost_partials(device_items):
    basis_block, ghost_block, jacobian_block, count_block = device_items
    gathered = jnp.take(basis_block, ghost_block, axis=2).astype(jnp.float32)
    partial_value = jnp.einsum('gfs,fks->gks', jacobian_block, gathered, precision=lax.Precision.HIGHEST)
    slot_kept = slot_limits(count_block)
    return jnp.where(slot_kept[None, None, :], partial_value, 0.0).astype(jnp.bfloat16)

def reference(reduced_basis, cell_jacobian, face_cells, face_jacobian, limiter_flags, viscosity, ghost_cells, ghost_jacobian, ghost_counts, receive_cells, coordinates, base_residual):
    devices = N_ROW * N_COL
    basis_dev = per_device(reduced_basis, devices)
    partials = lax.map(ghost_partials, (basis_dev, per_device(ghost_cells, devices), per_device(ghost_jacobian, devices), per_device(ghost_counts, devices)))
    partial_grid = partials.reshape((N_ROW, N_COL) + partials.shape[1:])
    padded = jnp.pad(partial_grid, ((1, 1), (1, 1), (0, 0), (0, 0), (0, 0)))
    fragment_list = []
    slot_start = 0
    for direction, offset_pair in enumerate(direction_offsets):
        row_offset, col_offset = offset_pair
        block_width = block_sizes()[direction]
        shifted = padded[1 - row_offset:1 - row_offset + N_ROW, 1 - col_offset:1 - col_offset + N_COL]
        fragment_list.append(shifted[..., slot_start:slot_start + block_width])
        slot_start += block_width
    incoming_block = jnp.concatenate(fragment_list, axis=-1).reshape(partials.shape)
    row_scale = (F * NCELLS) ** (-0.5)

    def device_work(device_items):
        basis_block, cell_tile_block, paired_block, face_block, flag_block, receive_block, got_block, base_block = device_items
        broad_basis_matrix = basis_block.astype(jnp.float32)
        jacobian_projection = jnp.einsum('irx,rtx->itx', cell_tile_block, broad_basis_matrix, precision=lax.Precision.HIGHEST)
        left_basis = jnp.take(broad_basis_matrix, paired_block[0], axis=2)
        right_basis = jnp.take(broad_basis_matrix, paired_block[1], axis=2)
        damping = viscosity[:, None, None] * flag_block.astype(jnp.float32)[None, None, :]
        difference = left_basis - right_basis
        to_left = jnp.einsum('gfn,fkn->gkn', face_block[0], right_basis, precision=lax.Precision.HIGHEST) + damping * difference
        to_right = jnp.einsum('gfn,fkn->gkn', face_block[1], left_basis, precision=lax.Precision.HIGHEST) - damping * difference
        jacobian_projection = jacobian_projection.at[:, :, paired_block[0]].add(to_left)
        jacobian_projection = jacobian_projection.at[:, :, paired_block[1]].add(to_right)
        jacobian_projection = jacobian_projection.at[:, :, receive_block].add(got_block.astype(jnp.float32))
        test_block = lax.optimization_barrier(jacobian_projection.astype(jnp.bfloat16))
        test_wide = test_block.astype(jnp.float32)
        residual_vector = base_block + row_scale * jnp.einsum('fkc,k->fc', test_wide, coordinates, precision=lax.Precision.HIGHEST)
        residual_low = lax.optimization_barrier(residual_vector.astype(jnp.bfloat16))
        stacked = jnp.concatenate([test_wide, residual_low.astype(jnp.float32)[:, None, :]], axis=1)
        gram_matrix = jnp.einsum('fkc,fjc->kj', stacked, stacked, precision=lax.Precision.HIGHEST) * (row_scale * row_scale)
        return (test_block, gram_matrix)
    test_blocks, gram_blocks = lax.map(device_work, (basis_dev, per_device(cell_jacobian, devices), per_device(face_cells, devices), per_device(face_jacobian, devices), per_device(limiter_flags, devices), per_device(receive_cells, devices), incoming_block, per_device(base_residual, devices)))
    test_basis = jnp.moveaxis(test_blocks, 0, 2).reshape(F, K, NCELLS)
    gram_sum = lax.optimization_barrier(jnp.sum(gram_blocks, axis=0))
    upper_factor = upper_cholesky(gram_sum)
    solved = upper_solve(upper_factor[:K, :K], upper_factor[:K, K])
    gauss_step = -solved / row_scale
    return (test_basis, upper_factor, gauss_step)
```

```python
import functools

import jax
import jax.numpy as jnp
from jax import lax
from jax.experimental import pallas as pl
from jax.experimental.pallas import tpu as pltpu
from jax.sharding import Mesh
from jax.sharding import PartitionSpec as P

ROW = ("row_0", "row_1")
COL = ("col_0", "col_1")
ROW_COL = ROW + COL
F = 5
K = 96
C = 512
N = 1024
S = 160
FK = F * K
HALF = FK // 2
BF = jnp.bfloat16
F32 = jnp.float32
VMEM_LIMIT = 48 * 1024 * 1024


def vmem(count):
    return [pl.BlockSpec(memory_space=pltpu.VMEM)] * count


def smem(count):
    return [pl.BlockSpec(memory_space=pltpu.SMEM)] * count


def one_hot(row):
    cells = lax.broadcasted_iota(jnp.int32, (C, row.shape[1]), 0)
    return jnp.where(cells == row, 1.0, 0.0).astype(BF)


def dot_nn(a, b):
    return lax.dot_general(a, b, (((1,), (0,)), ((), ())), preferred_element_type=F32)


def dot_nt(a, b):
    return lax.dot_general(a, b, (((1,), (1,)), ((), ())), preferred_element_type=F32)


def send_order(x, fill):
    def pad(width):
        return jnp.full(x.shape[:-1] + (width,), fill, x.dtype)

    return jnp.concatenate(
        [
            x[..., 0:32], x[..., 128:136], x[..., 136:144], pad(16),
            x[..., 32:64], x[..., 152:160], x[..., 144:152], pad(16),
            x[..., 64:96], pad(32),
            x[..., 96:128], pad(32),
        ],
        axis=-1,
    )


def receive_order(x):
    def pad(width):
        return jnp.full(x.shape[:-1] + (width,), -1, x.dtype)

    return jnp.concatenate(
        [
            x[..., 0:32], pad(32),
            x[..., 32:64], pad(32),
            x[..., 64:96], x[..., 128:136], x[..., 144:152], pad(16),
            x[..., 96:128], x[..., 152:160], x[..., 136:144], pad(16),
        ],
        axis=-1,
    )


def ghost_kernel(count_ref, basis_ref, cell_ref, jac_ref, minus_ref, plus_ref, left_ref, right_ref, val):
    lane = lax.broadcasted_iota(jnp.int32, (1, 256), 1)
    spot = lane % 64
    side = lane // 64
    limit = jnp.zeros((1, 256), jnp.int32)
    for place in range(4):
        limit = jnp.where((side == place) & (spot < 32), count_ref[place], limit)
    for place, at, block in ((0, 32, 4), (0, 40, 5), (1, 32, 7), (1, 40, 6)):
        inside = (side == place) & (spot >= at) & (spot < at + 8)
        limit = jnp.where(inside, count_ref[block] + at, limit)
    index = send_order(cell_ref[...], -1)
    index = jnp.where(spot < limit, index, -1)
    hot = one_hot(index)
    taken = dot_nn(basis_ref[...], hot)
    for f in range(F):
        val[f] = taken[f * K : (f + 1) * K]
    low = lax.broadcasted_iota(jnp.int32, (1, 128), 1) < 64
    parts = []
    for g in range(F):
        jac = send_order(jac_ref[g], 0.0)
        total = jac[0:1] * val[0]
        for f in range(1, F):
            total = total + jac[f : f + 1] * val[f]
        parts.append(total)
    full = jnp.concatenate(parts, axis=0)
    for tile, first, second in ((0, minus_ref, plus_ref), (1, left_ref, right_ref)):
        wide = full[:, tile * 128 : (tile + 1) * 128]
        top, bottom = wide[:HALF], wide[HALF:]
        first[...] = jnp.where(low, top, pltpu.roll(bottom, 64, 1)).astype(BF)
        second[...] = jnp.where(low, pltpu.roll(top, 64, 1), bottom).astype(BF)


def ghost_call(counts, basis, cells, jacobian):
    message = jax.ShapeDtypeStruct((HALF, 128), BF)
    return pl.pallas_call(
        ghost_kernel,
        out_shape=(message,) * 4,
        in_specs=smem(1) + vmem(3),
        out_specs=tuple(vmem(4)),
        scratch_shapes=[pltpu.VMEM((F, K, 256), F32)],
        compiler_params=pltpu.CompilerParams(vmem_limit_bytes=VMEM_LIMIT),
        name="ghost",
    )(counts, basis, cells, jacobian)


BLOCK = 256
BLOCKS = N // BLOCK
CHUNK = 32


def face_kernel(nu_ref, basis_ref, diag_ref, pair_ref, jac_ref, flag_ref, out_ref, hot, got, add):
    basis = basis_ref[...]
    for block in range(BLOCKS):
        lanes = slice(block * BLOCK, (block + 1) * BLOCK)
        hot[block, :, :BLOCK] = one_hot(pair_ref[0:1, lanes])
        hot[block, :, BLOCK:] = one_hot(pair_ref[1:2, lanes])
        got[block] = dot_nn(basis, hot[block])
        for tile in range(BLOCK // 128):
            here = slice(block * BLOCK + tile * 128, block * BLOCK + (tile + 1) * 128)
            at_a = slice(tile * 128, (tile + 1) * 128)
            at_b = slice(BLOCK + tile * 128, BLOCK + (tile + 1) * 128)
            flag = flag_ref[0:1, here].astype(F32)
            for start in range(0, K, CHUNK):
                a = [got[block, f * K + start : f * K + start + CHUNK, at_a] for f in range(F)]
                b = [got[block, f * K + start : f * K + start + CHUNK, at_b] for f in range(F)]
                for g in range(F):
                    damp = (nu_ref[g] * flag) * (a[g] - b[g])
                    to_a, to_b = damp, -damp
                    for f in range(F):
                        to_a = to_a + jac_ref[0, g, f : f + 1, here] * b[f]
                        to_b = to_b + jac_ref[1, g, f : f + 1, here] * a[f]
                    rows = slice(g * K + start, g * K + start + CHUNK)
                    add[block, rows, at_a] = to_a.astype(BF)
                    add[block, rows, at_b] = to_b.astype(BF)
    for tile in range(C // 128):
        here = slice(tile * 128, (tile + 1) * 128)
        for start in range(0, K, CHUNK):
            v = [basis_ref[f * K + start : f * K + start + CHUNK, here].astype(F32) for f in range(F)]
            for g in range(F):
                total = diag_ref[g, 0:1, here] * v[0]
                for f in range(1, F):
                    total = total + diag_ref[g, f : f + 1, here] * v[f]
                out_ref[g * K + start : g * K + start + CHUNK, here] = total
    for block in range(BLOCKS):
        out_ref[...] += dot_nt(add[block], hot[block])


def face_call(nu, basis, diag, pair, jacobian, flags):
    return pl.pallas_call(
        face_kernel,
        out_shape=jax.ShapeDtypeStruct((FK, C), F32),
        in_specs=smem(1) + vmem(5),
        out_specs=vmem(1)[0],
        scratch_shapes=[
            pltpu.VMEM((BLOCKS, C, 2 * BLOCK), BF),
            pltpu.VMEM((BLOCKS, FK, 2 * BLOCK), F32),
            pltpu.VMEM((BLOCKS, FK, 2 * BLOCK), BF),
        ],
        compiler_params=pltpu.CompilerParams(vmem_limit_bytes=VMEM_LIMIT),
        cost_estimate=pl.CostEstimate(flops=4_000_000_000, bytes_accessed=2_000_000, transcendentals=0),
        name="faces",
    )(nu, basis, diag, pair, jacobian, flags)


ROWS = 112


def finish_kernel(row_scale, image_ref, above_ref, below_ref, right_ref, left_ref, cell_ref, coord_ref, base_ref,
                  test_ref, gram_ref, arrive, stack):
    low = lax.broadcasted_iota(jnp.int32, (1, 128), 1) < 64
    for tile, first, second in ((0, above_ref, below_ref), (1, right_ref, left_ref)):
        here = slice(tile * 128, (tile + 1) * 128)
        one, two = first[...].astype(F32), second[...].astype(F32)
        arrive[:HALF, here] = jnp.where(low, one, pltpu.roll(two, 64, 1)).astype(BF)
        arrive[HALF:, here] = jnp.where(low, pltpu.roll(one, 64, 1), two).astype(BF)
    hot = one_hot(receive_order(cell_ref[...]))
    image = image_ref[...] + dot_nt(arrive[...], hot)
    test = image.astype(BF)
    coord = coord_ref[...]
    high = coord.astype(BF)
    small = (coord - high.astype(F32)).astype(BF)
    row = lax.broadcasted_iota(jnp.int32, (16, K), 0)
    zero = jnp.zeros((16, K), F32)
    pair = jnp.where(row == 0, high.astype(F32), jnp.where(row == 1, small.astype(F32), zero)).astype(BF)
    first_row = lax.broadcasted_iota(jnp.int32, (16, C), 0) == 0
    for f in range(F):
        part = test[f * K : (f + 1) * K]
        here = slice(f * C, (f + 1) * C)
        test_ref[f] = part
        stack[:K, here] = part
        product = dot_nn(pair, part)
        value = base_ref[f : f + 1] + row_scale * (product[0:1] + product[1:2])
        stack[K:ROWS, here] = jnp.where(first_row, value, 0.0).astype(BF)
    whole = stack[...]
    gram = dot_nt(whole, whole) * (row_scale * row_scale)
    gram_ref[...] = jnp.concatenate([gram[:104], jnp.zeros((104, 128 - ROWS), F32)], axis=1)


def finish_call(row_scale, image, above, below, right, left, cells, coords, base):
    return pl.pallas_call(
        functools.partial(finish_kernel, row_scale),
        out_shape=(jax.ShapeDtypeStruct((F, K, C), BF), jax.ShapeDtypeStruct((104, 128), F32)),
        in_specs=vmem(8),
        out_specs=tuple(vmem(2)),
        scratch_shapes=[pltpu.VMEM((FK, 256), BF), pltpu.VMEM((ROWS, F * C), BF)],
        compiler_params=pltpu.CompilerParams(vmem_limit_bytes=VMEM_LIMIT),
        name="finish",
    )(image, above, below, right, left, cells, coords, base)


TILES = 13


def solve_kernel(row_scale, first_ref, second_ref, factor_ref, step_ref, work):
    work[...] = first_ref[...] + second_ref[...]
    lane = lax.broadcasted_iota(jnp.int32, (8, 128), 1)
    sub = lax.broadcasted_iota(jnp.int32, (8, 128), 0)

    def spread_row(tile, p):
        return jnp.broadcast_to(tile[p : p + 1], (8, 128))

    def spread_lane(tile, j):
        return jnp.broadcast_to(tile[:, j : j + 1], (8, 128))

    tiles = [work[8 * t : 8 * t + 8] for t in range(TILES)]
    for panel in range(12):
        start = 8 * panel
        here = tiles[panel]
        columns = [[spread_lane(tiles[t], start + p) for p in range(8)] for t in range(TILES)]
        rows = [spread_row(here, p) for p in range(8)]
        d = {(p, q): spread_row(columns[panel][q], p) for p in range(8) for q in range(p, 8)}
        m = {}
        inverse = []
        for p in range(8):
            recip = 1.0 / d[p, p]
            inverse.append(recip)
            for q in range(p + 1, 8):
                m[p, q] = d[p, q] * recip
            for q in range(p + 1, 8):
                rows[q] = rows[q] - m[p, q] * rows[p]
                for r in range(q, 8):
                    d[q, r] = d[q, r] - m[p, q] * d[p, r]
        out = jnp.zeros((8, 128), F32)
        for p in range(8):
            out = jnp.where(sub == p, rows[p] * lax.rsqrt(d[p, p]), out)
        out = jnp.where(lane >= start + sub, out, 0.0)
        factor_ref[start : start + 8, :] = out[:, :97]
        for p in range(7, -1, -1):
            rows[p] = rows[p] * inverse[p]
            for q in range(p + 1, 8):
                rows[p] = rows[p] - m[p, q] * rows[q]
        order = [panel + 1] + [t for t in range(TILES) if t not in (panel, panel + 1)]
        for t in order:
            product = [columns[t][p] * rows[p] for p in range(8)]
            while len(product) > 1:
                product = [product[i] + product[i + 1] for i in range(0, len(product), 2)]
            tiles[t] = tiles[t] - product[0]
        new = rows[0]
        for p in range(1, 8):
            new = jnp.where(sub == p, rows[p], new)
        tiles[panel] = new
    last = tiles[12]
    factor_ref[96:97, :] = jnp.where(lane[:1] == 96, jnp.sqrt(last[0:1]), 0.0)[:, :97]
    step = jnp.zeros((1, 128), F32)
    for t in range(12):
        column = spread_lane(tiles[t], 96)
        step = step + jnp.sum(jnp.where(lane == 8 * t + sub, column, 0.0), axis=0, keepdims=True)
    step_ref[...] = step[:, :96] * (-1.0 / row_scale)


def solve_call(row_scale, first, second):
    return pl.pallas_call(
        functools.partial(solve_kernel, row_scale),
        out_shape=(jax.ShapeDtypeStruct((97, 97), F32), jax.ShapeDtypeStruct((1, 96), F32)),
        in_specs=vmem(2),
        out_specs=tuple(vmem(2)),
        scratch_shapes=[pltpu.VMEM((104, 128), F32)],
        compiler_params=pltpu.CompilerParams(vmem_limit_bytes=VMEM_LIMIT),
        name="solve",
    )(first, second)


def shift_up(x, axis):
    count = lax.axis_size(axis)
    return lax.ppermute(x, axis, [(i, i + 1) for i in range(count - 1)])


def shift_down(x, axis):
    count = lax.axis_size(axis)
    return lax.ppermute(x, axis, [(i + 1, i) for i in range(count - 1)])


def swap(x, axis, step):
    count = lax.axis_size(axis)
    return lax.ppermute(x, axis, [(i, i ^ step) for i in range(count)])


def local(
    reduced_basis,
    cell_jacobian,
    face_cells,
    face_jacobian,
    limiter_flags,
    viscosity,
    ghost_cells,
    ghost_jacobian,
    ghost_counts,
    receive_cells,
    coordinates,
    base_residual,
):
    devices = lax.axis_size(ROW) * lax.axis_size(COL)
    row_scale = (F * C * devices) ** (-0.5)
    basis = reduced_basis.reshape(FK, C)
    minus, plus, left, right = ghost_call(
        ghost_counts, basis, ghost_cells.reshape(1, S), ghost_jacobian
    )
    above = shift_down(minus, ROW)
    below = shift_up(plus, ROW)
    spot = lax.broadcasted_iota(jnp.int32, (HALF, 128), 1) % 64
    at_32 = (spot >= 32) & (spot < 40)
    at_40 = (spot >= 40) & (spot < 48)
    to_left = jnp.where(at_32, above, jnp.where(at_40, below, left))
    to_right = jnp.where(at_32, below, jnp.where(at_40, above, right))
    from_right = shift_down(to_left, COL)
    from_left = shift_up(to_right, COL)
    image = face_call(
        viscosity, basis, cell_jacobian, face_cells, face_jacobian, limiter_flags.reshape(1, N)
    )
    test, gram = finish_call(
        row_scale, image, above, below, from_right, from_left,
        receive_cells.reshape(1, S), coordinates.reshape(1, K), base_residual,
    )
    gram = gram + swap(gram, "col_1", 1)
    for axis in ("col_0", "row_1", "row_0"):
        one, two, three = (swap(gram, axis, k) for k in (1, 2, 3))
        first, second = gram + one, two + three
        gram = first + second
    factor, step = solve_call(row_scale, first, second)
    return (test, factor, step.reshape(K))


def solution(mesh):
    torus = Mesh(mesh.devices.reshape(4, 4, 4, 2), ("row_0", "row_1", "col_0", "col_1"))
    in_specs = (
        P(None, None, ROW_COL),
        P(None, None, ROW_COL),
        P(None, ROW_COL),
        P(None, None, None, ROW_COL),
        P(ROW_COL),
        P(),
        P(ROW_COL),
        P(None, None, ROW_COL),
        P(ROW_COL),
        P(ROW_COL),
        P(),
        P(None, ROW_COL),
    )
    out_specs = (P(None, None, ROW_COL), P(), P())
    return jax.shard_map(local, mesh=torus, in_specs=in_specs, out_specs=out_specs, check_vma=False)
```

```python
import functools

import jax
import jax.numpy as jnp
from jax import lax
from jax.experimental import pallas as pl
from jax.experimental.pallas import tpu as pltpu
from jax.sharding import Mesh
from jax.sharding import PartitionSpec as P

ROW = ("row_0", "row_1")
COL = ("col_0", "col_1")
ROW_COL = ROW + COL
F = 5
K = 96
C = 512
N = 1024
S = 160
FK = F * K
HALF = FK // 2
BF = jnp.bfloat16
F32 = jnp.float32
VMEM_LIMIT = 48 * 1024 * 1024


def vmem(count):
    return [pl.BlockSpec(memory_space=pltpu.VMEM)] * count


def smem(count):
    return [pl.BlockSpec(memory_space=pltpu.SMEM)] * count


def one_hot(row):
    cells = lax.broadcasted_iota(jnp.int32, (C, row.shape[1]), 0)
    return jnp.where(cells == row, 1.0, 0.0).astype(BF)


def dot_nn(a, b):
    return lax.dot_general(a, b, (((1,), (0,)), ((), ())), preferred_element_type=F32)


def dot_nt(a, b):
    return lax.dot_general(a, b, (((1,), (1,)), ((), ())), preferred_element_type=F32)


def blocks_of(x):
    ends = [0, 32, 64, 96, 128, 136, 144, 152, 160]
    return [x[..., ends[m] : ends[m + 1]] for m in range(8)]


def pad_like(x, width, fill):
    return jnp.full(x.shape[:-1] + (width,), fill, x.dtype)


def send_order(x, fill, odd_i, odd_j):
    b = blocks_of(x)
    p16, p32 = pad_like(x, 16, fill), pad_like(x, 32, fill)
    corner = jnp.concatenate([b[4], b[5], p16, p16, b[6], b[7], p32, p32], axis=-1)
    lane = lax.broadcasted_iota(jnp.int32, corner.shape, corner.ndim - 1)
    last = corner.ndim - 1
    other = jnp.where((lane // 8) % 2 == 0, pltpu.roll(corner, 120, last), pltpu.roll(corner, 8, last))
    corner = jnp.where(odd_j, corner, other)
    row = jnp.concatenate(
        [b[1], p16, corner[..., 48:64], b[0], corner[..., 0:16], p16], axis=-1
    )
    col = jnp.concatenate([b[3], p32, b[2], p32], axis=-1)
    row = jnp.where(odd_i, pltpu.roll(row, 64, last), row)
    col = jnp.where(odd_j, pltpu.roll(col, 64, last), col)
    return row, col


def receive_order(x, odd_i, odd_j):
    b = blocks_of(x)
    p8, p32 = pad_like(x, 8, -1), pad_like(x, 32, -1)
    row = jnp.concatenate([b[0], p32, b[1], p32], axis=-1)
    row = jnp.where(odd_i, pltpu.roll(row, 64, 1), row)
    even = jnp.concatenate([b[2], b[4], p8, b[6], p8, b[3], p8, b[5], p8, b[7]], axis=-1)
    odd = jnp.concatenate([b[3], b[5], p8, b[7], p8, b[2], p8, b[4], p8, b[6]], axis=-1)
    return row, jnp.where(odd_j, odd, even)


def parities():
    return lax.axis_index("row_1") % 2 == 1, lax.axis_index("col_1") % 2 == 1


def ghost_kernel(count_hbm, basis_hbm, cell_hbm, jac_hbm, row_a, row_b, col_a, col_b,
                 count_ref, basis_ref, cell_ref, jac_ref, val, sems):
    pairs = ((basis_hbm, basis_ref), (cell_hbm, cell_ref), (count_hbm, count_ref), (jac_hbm, jac_ref))
    copies = [pltpu.make_async_copy(src, dst, sems.at[i]) for i, (src, dst) in enumerate(pairs)]
    for copy in copies:
        copy.start()
    odd_i, odd_j = parities()
    copies[1].wait()
    copies[2].wait()
    lane = lax.broadcasted_iota(jnp.int32, (1, S), 1)
    limit = jnp.zeros((1, S), jnp.int32)
    for block, start in enumerate((0, 32, 64, 96, 128, 136, 144, 152)):
        limit = jnp.where(lane >= start, count_ref[0:1, block : block + 1] + start, limit)
    index = jnp.where(lane < limit, cell_ref[...], -1)
    hot = one_hot(jnp.concatenate(send_order(index, -1, odd_i, odd_j), axis=-1))
    copies[3].wait()
    weights = [jnp.concatenate(send_order(jac_ref[g], 0.0, odd_i, odd_j), axis=-1) for g in range(F)]
    copies[0].wait()
    taken = dot_nn(basis_ref[...], hot)
    for f in range(F):
        val[f] = taken[f * K : (f + 1) * K]
    low = lax.broadcasted_iota(jnp.int32, (1, 128), 1) < 64
    parts = []
    for g in range(F):
        total = weights[g][0:1] * val[0]
        for f in range(1, F):
            total = total + weights[g][f : f + 1] * val[f]
        parts.append(total)
    full = jnp.concatenate(parts, axis=0)
    for tile, first, second in ((0, row_a, row_b), (1, col_a, col_b)):
        wide = full[:, tile * 128 : (tile + 1) * 128]
        top, bottom = wide[:HALF], wide[HALF:]
        first[...] = jnp.where(low, top, pltpu.roll(bottom, 64, 1)).astype(BF)
        second[...] = jnp.where(low, pltpu.roll(top, 64, 1), bottom).astype(BF)


def ghost_call(counts, basis, cells, jacobian):
    message = jax.ShapeDtypeStruct((HALF, 128), BF)
    return pl.pallas_call(
        ghost_kernel,
        out_shape=(message,) * 4,
        in_specs=[pl.BlockSpec(memory_space=pltpu.MemorySpace.HBM)] * 4,
        out_specs=tuple(vmem(4)),
        scratch_shapes=[
            pltpu.VMEM((1, 8), jnp.int32),
            pltpu.VMEM((FK, C), BF),
            pltpu.VMEM((1, S), jnp.int32),
            pltpu.VMEM((F, F, S), F32),
            pltpu.VMEM((F, K, 256), F32),
            pltpu.SemaphoreType.DMA((4,)),
        ],
        compiler_params=pltpu.CompilerParams(vmem_limit_bytes=VMEM_LIMIT),
        name="ghost",
    )(counts, basis, cells, jacobian)


BLOCK = 256
HALF_BLOCKS = 2
CHUNK = 32
WIDE = FK + 16


def face_blocks(first_block, nu_ref, basis, pair_ref, jac_ref, flag_ref, hot, got, add, image):
    for block in range(HALF_BLOCKS):
        base = (first_block + block) * BLOCK
        lanes = slice(base, base + BLOCK)
        hot[block, :, :BLOCK] = one_hot(pair_ref[0:1, lanes])
        hot[block, :, BLOCK:] = one_hot(pair_ref[1:2, lanes])
        got[block] = dot_nn(basis, hot[block])
        flags = flag_ref[0:1, lanes].astype(F32)
        add[block, FK:] = jnp.broadcast_to(jnp.concatenate([flags, flags], axis=1), (16, 2 * BLOCK)).astype(BF)
        for tile in range(BLOCK // 128):
            here = slice(base + tile * 128, base + (tile + 1) * 128)
            at_a = slice(tile * 128, (tile + 1) * 128)
            at_b = slice(BLOCK + tile * 128, BLOCK + (tile + 1) * 128)
            flag = flags[:, at_a]
            for start in range(0, K, CHUNK):
                a = [got[block, f * K + start : f * K + start + CHUNK, at_a] for f in range(F)]
                b = [got[block, f * K + start : f * K + start + CHUNK, at_b] for f in range(F)]
                for g in range(F):
                    damp = nu_ref[g] * flag
                    to_a = (jac_ref[g, g, 0:1, here] - damp) * b[g]
                    to_b = (jac_ref[g, g, 1:2, here] - damp) * a[g]
                    for f in range(F):
                        if f != g:
                            to_a = to_a + jac_ref[g, f, 0:1, here] * b[f]
                            to_b = to_b + jac_ref[g, f, 1:2, here] * a[f]
                    rows = slice(g * K + start, g * K + start + CHUNK)
                    add[block, rows, at_a] = to_a.astype(BF)
                    add[block, rows, at_b] = to_b.astype(BF)
    for block in range(HALF_BLOCKS):
        image = dot_nt(add[block], hot[block]) if image is None else image + dot_nt(add[block], hot[block])
    return image


def early_kernel(nu_ref, basis_ref, pair_ref, jac_ref, flag_ref, cell_ref, coord_ref,
                 image_ref, hot_ref, coef_ref, hot, got, add):
    odd_i, odd_j = parities()
    hot_ref[...] = one_hot(jnp.concatenate(receive_order(cell_ref[...], odd_i, odd_j), axis=-1))
    coord = coord_ref[...]
    high = coord.astype(BF).astype(F32)
    row = lax.broadcasted_iota(jnp.int32, (16, K), 0)
    coef_ref[...] = jnp.where(row == 0, high, jnp.where(row == 1, coord - high, 0.0)).astype(BF)
    image_ref[...] = face_blocks(0, nu_ref, basis_ref[...], pair_ref, jac_ref, flag_ref, hot, got, add, None)


def late_kernel(nu_ref, basis_ref, diag_ref, pair_ref, jac_ref, flag_ref, image_ref, out_ref, hot, got, add):
    out_ref[...] = face_blocks(
        HALF_BLOCKS, nu_ref, basis_ref[...], pair_ref, jac_ref, flag_ref, hot, got, add, image_ref[...]
    )
    for tile in range(C // 128):
        here = slice(tile * 128, (tile + 1) * 128)
        flagged = out_ref[FK : FK + 1, here]
        for start in range(0, K, CHUNK):
            v = [basis_ref[f * K + start : f * K + start + CHUNK, here].astype(F32) for f in range(F)]
            for g in range(F):
                rows = slice(g * K + start, g * K + start + CHUNK)
                total = out_ref[rows, here] + (diag_ref[g, g : g + 1, here] + nu_ref[g] * flagged) * v[g]
                for f in range(F):
                    if f != g:
                        total = total + diag_ref[g, f : f + 1, here] * v[f]
                out_ref[rows, here] = total


FACE_SCRATCH = (
    ((HALF_BLOCKS, C, 2 * BLOCK), BF),
    ((HALF_BLOCKS, FK, 2 * BLOCK), F32),
    ((HALF_BLOCKS, WIDE, 2 * BLOCK), BF),
)
FACE_COST = pl.CostEstimate(flops=2_500_000_000, bytes_accessed=2_000_000, transcendentals=0)


def early_call(nu, basis, pair, jacobian, flags, cells, coords):
    return pl.pallas_call(
        early_kernel,
        out_shape=(
            jax.ShapeDtypeStruct((WIDE, C), F32),
            jax.ShapeDtypeStruct((C, 256), BF),
            jax.ShapeDtypeStruct((16, K), BF),
        ),
        in_specs=smem(1) + vmem(6),
        out_specs=tuple(vmem(3)),
        scratch_shapes=[pltpu.VMEM(*scratch) for scratch in FACE_SCRATCH],
        compiler_params=pltpu.CompilerParams(vmem_limit_bytes=VMEM_LIMIT),
        cost_estimate=FACE_COST,
        name="early_faces",
    )(nu, basis, pair, jacobian, flags, cells, coords)


def late_call(nu, basis, diag, pair, jacobian, flags, image):
    return pl.pallas_call(
        late_kernel,
        out_shape=jax.ShapeDtypeStruct((WIDE, C), F32),
        in_specs=smem(1) + vmem(6),
        out_specs=vmem(1)[0],
        scratch_shapes=[pltpu.VMEM(*scratch) for scratch in FACE_SCRATCH],
        compiler_params=pltpu.CompilerParams(vmem_limit_bytes=VMEM_LIMIT),
        cost_estimate=FACE_COST,
        name="late_faces",
    )(nu, basis, diag, pair, jacobian, flags, image)


ROWS = 112


def finish_kernel(row_scale, image_ref, row_a, row_b, col_a, col_b, hot_ref, coef_ref, base_ref,
                  test_ref, gram_ref, arrive, stack):
    low = lax.broadcasted_iota(jnp.int32, (1, 128), 1) < 64
    for tile, first, second in ((0, row_a, row_b), (1, col_a, col_b)):
        here = slice(tile * 128, (tile + 1) * 128)
        one, two = first[...].astype(F32), second[...].astype(F32)
        arrive[:HALF, here] = jnp.where(low, one, pltpu.roll(two, 64, 1)).astype(BF)
        arrive[HALF:, here] = jnp.where(low, pltpu.roll(one, 64, 1), two).astype(BF)
    test = (image_ref[:FK] + dot_nt(arrive[...], hot_ref[...])).astype(BF)
    coef = coef_ref[...]
    first_row = lax.broadcasted_iota(jnp.int32, (16, C), 0) == 0
    for f in range(F):
        part = test[f * K : (f + 1) * K]
        here = slice(f * C, (f + 1) * C)
        test_ref[f] = part
        stack[:K, here] = part
        product = dot_nn(coef, part)
        value = base_ref[f : f + 1] + row_scale * (product[0:1] + product[1:2])
        stack[K:ROWS, here] = jnp.where(first_row, value, 0.0).astype(BF)
    whole = stack[...]
    gram = dot_nt(whole, whole) * (row_scale * row_scale)
    gram_ref[...] = jnp.concatenate([gram[:104], jnp.zeros((104, 128 - ROWS), F32)], axis=1)


def finish_call(row_scale, image, row_a, row_b, col_a, col_b, hot, coef, base):
    return pl.pallas_call(
        functools.partial(finish_kernel, row_scale),
        out_shape=(jax.ShapeDtypeStruct((F, K, C), BF), jax.ShapeDtypeStruct((104, 128), F32)),
        in_specs=vmem(8),
        out_specs=tuple(vmem(2)),
        scratch_shapes=[pltpu.VMEM((FK, 256), BF), pltpu.VMEM((ROWS, F * C), BF)],
        compiler_params=pltpu.CompilerParams(vmem_limit_bytes=VMEM_LIMIT),
        name="finish",
    )(image, row_a, row_b, col_a, col_b, hot, coef, base)


TILES = 13


def solve_kernel(row_scale, first_ref, second_ref, factor_ref, step_ref, work):
    work[...] = first_ref[...] + second_ref[...]
    lane = lax.broadcasted_iota(jnp.int32, (8, 128), 1)
    sub = lax.broadcasted_iota(jnp.int32, (8, 128), 0)

    def spread_row(tile, p):
        return jnp.broadcast_to(tile[p : p + 1], (8, 128))

    def spread_lane(tile, j):
        return jnp.broadcast_to(tile[:, j : j + 1], (8, 128))

    tiles = [work[8 * t : 8 * t + 8] for t in range(TILES)]
    for panel in range(12):
        start = 8 * panel
        here = tiles[panel]
        columns = [[spread_lane(tiles[t], start + p) for p in range(8)] for t in range(TILES)]
        rows = [spread_row(here, p) for p in range(8)]
        d = {(p, q): spread_row(columns[panel][q], p) for p in range(8) for q in range(p, 8)}
        m = {}
        inverse = []
        for p in range(8):
            recip = 1.0 / d[p, p]
            inverse.append(recip)
            for q in range(p + 1, 8):
                m[p, q] = d[p, q] * recip
            for q in range(p + 1, 8):
                rows[q] = rows[q] - m[p, q] * rows[p]
                for r in range(q, 8):
                    d[q, r] = d[q, r] - m[p, q] * d[p, r]
        out = jnp.zeros((8, 128), F32)
        for p in range(8):
            out = jnp.where(sub == p, rows[p] * lax.rsqrt(d[p, p]), out)
        out = jnp.where(lane >= start + sub, out, 0.0)
        factor_ref[start : start + 8, :] = out[:, :97]
        for p in range(7, -1, -1):
            rows[p] = rows[p] * inverse[p]
            for q in range(p + 1, 8):
                rows[p] = rows[p] - m[p, q] * rows[q]
        order = [panel + 1] + [t for t in range(TILES) if t not in (panel, panel + 1)]
        for t in order:
            product = [columns[t][p] * rows[p] for p in range(8)]
            while len(product) > 1:
                product = [product[i] + product[i + 1] for i in range(0, len(product), 2)]
            tiles[t] = tiles[t] - product[0]
        new = rows[0]
        for p in range(1, 8):
            new = jnp.where(sub == p, rows[p], new)
        tiles[panel] = new
    last = tiles[12]
    factor_ref[96:97, :] = jnp.where(lane[:1] == 96, jnp.sqrt(last[0:1]), 0.0)[:, :97]
    step = jnp.zeros((1, 128), F32)
    for t in range(12):
        column = spread_lane(tiles[t], 96)
        step = step + jnp.sum(jnp.where(lane == 8 * t + sub, column, 0.0), axis=0, keepdims=True)
    step_ref[...] = step[:, :96] * (-1.0 / row_scale)


def solve_call(row_scale, first, second):
    return pl.pallas_call(
        functools.partial(solve_kernel, row_scale),
        out_shape=(jax.ShapeDtypeStruct((97, 97), F32), jax.ShapeDtypeStruct((1, 96), F32)),
        in_specs=vmem(2),
        out_specs=tuple(vmem(2)),
        scratch_shapes=[pltpu.VMEM((104, 128), F32)],
        compiler_params=pltpu.CompilerParams(vmem_limit_bytes=VMEM_LIMIT),
        name="solve",
    )(first, second)


def swap(x, axis, step):
    count = lax.axis_size(axis)
    return lax.ppermute(x, axis, [(i, i ^ step) for i in range(count)])


def swap_odd(x, axis):
    pairs = []
    for i in range(1, lax.axis_size(axis) - 1, 2):
        pairs += [(i, i + 1), (i + 1, i)]
    return lax.ppermute(x, axis, pairs)


def local(
    reduced_basis,
    cell_jacobian,
    face_cells,
    face_jacobian,
    limiter_flags,
    viscosity,
    ghost_cells,
    ghost_jacobian,
    ghost_counts,
    receive_cells,
    coordinates,
    base_residual,
):
    devices = lax.axis_size(ROW) * lax.axis_size(COL)
    row_scale = (F * C * devices) ** (-0.5)
    basis = reduced_basis.reshape(FK, C)
    jacobian = face_jacobian.transpose(1, 2, 0, 3)
    flags = limiter_flags.reshape(1, N)
    row_a, row_b, col_a, col_b = ghost_call(
        ghost_counts.reshape(1, 8), basis, ghost_cells.reshape(1, S), ghost_jacobian
    )
    row_a = swap(row_a, ROW, 1)
    row_b = swap_odd(row_b, ROW)
    image, hot, coef = early_call(
        viscosity, basis, face_cells, jacobian, flags, receive_cells.reshape(1, S), coordinates.reshape(1, K)
    )
    group = (lax.broadcasted_iota(jnp.int32, (HALF, 128), 1) % 64) // 8
    corner = row_a + row_b
    col_a = jnp.where((group == 4) | (group == 6), corner, col_a)
    col_b = jnp.where((group == 5) | (group == 7), corner, col_b)
    col_a = swap(col_a, COL, 1)
    col_b = swap_odd(col_b, COL)
    image = late_call(viscosity, basis, cell_jacobian, face_cells, jacobian, flags, image)
    test, gram = finish_call(row_scale, image, row_a, row_b, col_a, col_b, hot, coef, base_residual)
    gram = gram + swap(gram, "col_1", 1)
    for axis in ("col_0", "row_1", "row_0"):
        one, two, three = (swap(gram, axis, k) for k in (1, 2, 3))
        first, second = gram + one, two + three
        gram = first + second
    factor, step = solve_call(row_scale, first, second)
    return (test, factor, step.reshape(K))


def solution(mesh):
    torus = Mesh(mesh.devices.reshape(4, 4, 4, 2), ("row_0", "row_1", "col_0", "col_1"))
    in_specs = (
        P(None, None, ROW_COL),
        P(None, None, ROW_COL),
        P(None, ROW_COL),
        P(None, None, None, ROW_COL),
        P(ROW_COL),
        P(),
        P(ROW_COL),
        P(None, None, ROW_COL),
        P(ROW_COL),
        P(ROW_COL),
        P(),
        P(None, ROW_COL),
    )
    out_specs = (P(None, None, ROW_COL), P(), P())
    return jax.shard_map(local, mesh=torus, in_specs=in_specs, out_specs=out_specs, check_vma=False)
```

```python
import functools

import jax
import jax.numpy as jnp
from jax import lax
from jax.experimental import pallas as pl
from jax.experimental.pallas import tpu as pltpu
from jax.sharding import Mesh
from jax.sharding import PartitionSpec as P

ROW = ("row_0", "row_1")
COL = ("col_0", "col_1")
ROW_COL = ROW + COL
F = 5
K = 96
C = 512
N = 1024
S = 160
FK = F * K
HALF = FK // 2
BF = jnp.bfloat16
F32 = jnp.float32
VMEM_LIMIT = 48 * 1024 * 1024


def vmem(count):
    return [pl.BlockSpec(memory_space=pltpu.VMEM)] * count


def one_hot(row):
    cells = lax.broadcasted_iota(jnp.int32, (C, row.shape[1]), 0)
    return jnp.where(cells == row, 1.0, 0.0).astype(BF)


def dot_nn(a, b):
    return lax.dot_general(a, b, (((1,), (0,)), ((), ())), preferred_element_type=F32)


def dot_nt(a, b):
    return lax.dot_general(a, b, (((1,), (1,)), ((), ())), preferred_element_type=F32)


def blocks_of(x):
    ends = [0, 32, 64, 96, 128, 136, 144, 152, 160]
    return [x[..., ends[m] : ends[m + 1]] for m in range(8)]


def pad_like(x, width, fill):
    return jnp.full(x.shape[:-1] + (width,), fill, x.dtype)


def send_order(x, fill, odd_i, odd_j):
    b = blocks_of(x)
    p16, p32 = pad_like(x, 16, fill), pad_like(x, 32, fill)
    corner = jnp.concatenate([b[4], b[5], p16, p16, b[6], b[7], p32, p32], axis=-1)
    lane = lax.broadcasted_iota(jnp.int32, corner.shape, corner.ndim - 1)
    last = corner.ndim - 1
    other = jnp.where((lane // 8) % 2 == 0, pltpu.roll(corner, 120, last), pltpu.roll(corner, 8, last))
    corner = jnp.where(odd_j, corner, other)
    row = jnp.concatenate(
        [b[1], p16, corner[..., 48:64], b[0], corner[..., 0:16], p16], axis=-1
    )
    col = jnp.concatenate([b[3], p32, b[2], p32], axis=-1)
    row = jnp.where(odd_i, pltpu.roll(row, 64, last), row)
    col = jnp.where(odd_j, pltpu.roll(col, 64, last), col)
    return row, col


def receive_order(x, odd_i, odd_j):
    b = blocks_of(x)
    p8, p32 = pad_like(x, 8, -1), pad_like(x, 32, -1)
    row = jnp.concatenate([b[0], p32, b[1], p32], axis=-1)
    row = jnp.where(odd_i, pltpu.roll(row, 64, 1), row)
    even = jnp.concatenate([b[2], b[4], p8, b[6], p8, b[3], p8, b[5], p8, b[7]], axis=-1)
    odd = jnp.concatenate([b[3], b[5], p8, b[7], p8, b[2], p8, b[4], p8, b[6]], axis=-1)
    return row, jnp.where(odd_j, odd, even)


def parities():
    return lax.axis_index("row_1") % 2 == 1, lax.axis_index("col_1") % 2 == 1


def ghost_kernel(count_hbm, cell_hbm, jac_hbm, basis_hbm, pair_hbm, flag_hbm, face_hbm, diag_hbm, arrive_hbm,
                 coord_hbm, base_hbm, nu_hbm, row_a, row_b, col_a, col_b, basis_ref, pair_ref, flag_ref, face_ref,
                 diag_ref, arrive_ref, coord_ref, base_ref, nu_ref, count_ref, cell_ref, jac_ref, val, sems):
    pairs = (
        (basis_hbm, basis_ref), (cell_hbm, cell_ref), (count_hbm, count_ref), (jac_hbm, jac_ref),
        (face_hbm, face_ref), (pair_hbm, pair_ref), (flag_hbm, flag_ref), (diag_hbm, diag_ref),
        (arrive_hbm, arrive_ref), (coord_hbm, coord_ref), (base_hbm, base_ref),
        (nu_hbm, nu_ref),
    )
    copies = [pltpu.make_async_copy(src, dst, sems.at[i]) for i, (src, dst) in enumerate(pairs)]
    for i in (1, 2, 0, 3, 4, 5, 6, 7, 8, 9, 10, 11):
        copies[i].start()
    odd_i, odd_j = parities()
    copies[1].wait()
    copies[2].wait()
    lane = lax.broadcasted_iota(jnp.int32, (1, S), 1)
    limit = jnp.zeros((1, S), jnp.int32)
    for block, start in enumerate((0, 32, 64, 96, 128, 136, 144, 152)):
        limit = jnp.where(lane >= start, count_ref[0:1, block : block + 1] + start, limit)
    index = jnp.where(lane < limit, cell_ref[...], -1)
    hot = one_hot(jnp.concatenate(send_order(index, -1, odd_i, odd_j), axis=-1))
    copies[3].wait()
    weights = [jnp.concatenate(send_order(jac_ref[g], 0.0, odd_i, odd_j), axis=-1) for g in range(F)]
    copies[0].wait()
    taken = dot_nn(basis_ref[...], hot)
    for f in range(F):
        val[f] = taken[f * K : (f + 1) * K]
    low = lax.broadcasted_iota(jnp.int32, (1, 128), 1) < 64
    parts = []
    for g in range(F):
        total = weights[g][0:1] * val[0]
        for f in range(1, F):
            total = total + weights[g][f : f + 1] * val[f]
        parts.append(total)
    full = jnp.concatenate(parts, axis=0)
    for tile, first, second in ((0, row_a, row_b), (1, col_a, col_b)):
        wide = full[:, tile * 128 : (tile + 1) * 128]
        top, bottom = wide[:HALF], wide[HALF:]
        first[...] = jnp.where(low, top, pltpu.roll(bottom, 64, 1)).astype(BF)
        second[...] = jnp.where(low, pltpu.roll(top, 64, 1), bottom).astype(BF)
    for copy in copies[4:]:
        copy.wait()


def ghost_call(counts, cells, jacobian, *loaded):
    message = jax.ShapeDtypeStruct((HALF, 128), BF)
    operands = [pltpu.with_memory_space_constraint(x, pltpu.MemorySpace.HBM) for x in (counts, cells, jacobian) + loaded]
    return pl.pallas_call(
        ghost_kernel,
        out_shape=(message,) * 4 + tuple(jax.ShapeDtypeStruct(x.shape, x.dtype) for x in loaded),
        in_specs=[pl.BlockSpec(memory_space=pltpu.MemorySpace.HBM)] * len(operands),
        out_specs=tuple(vmem(4 + len(loaded))),
        scratch_shapes=[
            pltpu.VMEM((1, 8), jnp.int32),
            pltpu.VMEM((1, S), jnp.int32),
            pltpu.VMEM((F, F, S), F32),
            pltpu.VMEM((F, K, 256), F32),
            pltpu.SemaphoreType.DMA((12,)),
        ],
        compiler_params=pltpu.CompilerParams(vmem_limit_bytes=VMEM_LIMIT),
        name="ghost",
    )(*operands)


BLOCK = 256
HALF_BLOCKS = 2
CHUNK = 32
WIDE = FK + 16


def face_blocks(first_block, nu_ref, basis, pair_ref, jac_ref, flag_ref, hot, got, add, image):
    for block in range(HALF_BLOCKS):
        base = (first_block + block) * BLOCK
        lanes = slice(base, base + BLOCK)
        hot[block, :, :BLOCK] = one_hot(pair_ref[0:1, lanes])
        hot[block, :, BLOCK:] = one_hot(pair_ref[1:2, lanes])
        got[block] = dot_nn(basis, hot[block])
        flags = flag_ref[0:1, lanes].astype(F32)
        add[block, FK:] = jnp.broadcast_to(jnp.concatenate([flags, flags], axis=1), (16, 2 * BLOCK)).astype(BF)
        for tile in range(BLOCK // 128):
            here = slice(base + tile * 128, base + (tile + 1) * 128)
            at_a = slice(tile * 128, (tile + 1) * 128)
            at_b = slice(BLOCK + tile * 128, BLOCK + (tile + 1) * 128)
            damps = [nu_ref[0:1, g : g + 1] * flags[:, at_a] for g in range(F)]
            for start in range(0, K, CHUNK):
                a = [got[block, f * K + start : f * K + start + CHUNK, at_a] for f in range(F)]
                b = [got[block, f * K + start : f * K + start + CHUNK, at_b] for f in range(F)]
                for g in range(F):
                    damp = damps[g]
                    to_a = (jac_ref[g, g, 0:1, here] - damp) * b[g]
                    to_b = (jac_ref[g, g, 1:2, here] - damp) * a[g]
                    for f in range(F):
                        if f != g:
                            to_a = to_a + jac_ref[g, f, 0:1, here] * b[f]
                            to_b = to_b + jac_ref[g, f, 1:2, here] * a[f]
                    rows = slice(g * K + start, g * K + start + CHUNK)
                    add[block, rows, at_a] = to_a.astype(BF)
                    add[block, rows, at_b] = to_b.astype(BF)
    for block in range(HALF_BLOCKS):
        image = dot_nt(add[block], hot[block]) if image is None else image + dot_nt(add[block], hot[block])
    return image


def early_kernel(nu_ref, basis_ref, pair_ref, jac_ref, flag_ref, cell_ref, coord_ref,
                 image_ref, hot_ref, coef_ref, hot, got, add):
    odd_i, odd_j = parities()
    hot_ref[...] = one_hot(jnp.concatenate(receive_order(cell_ref[...], odd_i, odd_j), axis=-1))
    coord = coord_ref[...]
    high = coord.astype(BF).astype(F32)
    row = lax.broadcasted_iota(jnp.int32, (16, K), 0)
    coef_ref[...] = jnp.where(row == 0, high, jnp.where(row == 1, coord - high, 0.0)).astype(BF)
    image_ref[...] = face_blocks(0, nu_ref, basis_ref[...], pair_ref, jac_ref, flag_ref, hot, got, add, None)


def late_kernel(nu_ref, basis_ref, diag_ref, pair_ref, jac_ref, flag_ref, image_ref, out_ref, hot, got, add):
    out_ref[...] = face_blocks(
        HALF_BLOCKS, nu_ref, basis_ref[...], pair_ref, jac_ref, flag_ref, hot, got, add, image_ref[...]
    )
    for tile in range(C // 128):
        here = slice(tile * 128, (tile + 1) * 128)
        flagged = out_ref[FK : FK + 1, here]
        own = [diag_ref[g, g : g + 1, here] + nu_ref[0:1, g : g + 1] * flagged for g in range(F)]
        for start in range(0, K, CHUNK):
            v = [basis_ref[f * K + start : f * K + start + CHUNK, here].astype(F32) for f in range(F)]
            for g in range(F):
                rows = slice(g * K + start, g * K + start + CHUNK)
                total = out_ref[rows, here] + own[g] * v[g]
                for f in range(F):
                    if f != g:
                        total = total + diag_ref[g, f : f + 1, here] * v[f]
                out_ref[rows, here] = total


FACE_SCRATCH = (
    ((HALF_BLOCKS, C, 2 * BLOCK), BF),
    ((HALF_BLOCKS, FK, 2 * BLOCK), F32),
    ((HALF_BLOCKS, WIDE, 2 * BLOCK), BF),
)
FACE_COST = pl.CostEstimate(flops=2_500_000_000, bytes_accessed=2_000_000, transcendentals=0)


def early_call(nu, basis, pair, jacobian, flags, cells, coords):
    return pl.pallas_call(
        early_kernel,
        out_shape=(
            jax.ShapeDtypeStruct((WIDE, C), F32),
            jax.ShapeDtypeStruct((C, 256), BF),
            jax.ShapeDtypeStruct((16, K), BF),
        ),
        in_specs=vmem(7),
        out_specs=tuple(vmem(3)),
        scratch_shapes=[pltpu.VMEM(*scratch) for scratch in FACE_SCRATCH],
        compiler_params=pltpu.CompilerParams(vmem_limit_bytes=VMEM_LIMIT),
        cost_estimate=FACE_COST,
        name="early_faces",
    )(nu, basis, pair, jacobian, flags, cells, coords)


def late_call(nu, basis, diag, pair, jacobian, flags, image):
    return pl.pallas_call(
        late_kernel,
        out_shape=jax.ShapeDtypeStruct((WIDE, C), F32),
        in_specs=vmem(7),
        out_specs=vmem(1)[0],
        scratch_shapes=[pltpu.VMEM(*scratch) for scratch in FACE_SCRATCH],
        compiler_params=pltpu.CompilerParams(vmem_limit_bytes=VMEM_LIMIT),
        cost_estimate=FACE_COST,
        name="late_faces",
    )(nu, basis, diag, pair, jacobian, flags, image)


ROWS = 112


def finish_kernel(row_scale, image_ref, row_a, row_b, col_a, col_b, hot_ref, coef_ref, base_ref,
                  test_ref, gram_ref, arrive, stack):
    low = lax.broadcasted_iota(jnp.int32, (1, 128), 1) < 64
    for tile, first, second in ((0, row_a, row_b), (1, col_a, col_b)):
        here = slice(tile * 128, (tile + 1) * 128)
        one, two = first[...].astype(F32), second[...].astype(F32)
        arrive[:HALF, here] = jnp.where(low, one, pltpu.roll(two, 64, 1)).astype(BF)
        arrive[HALF:, here] = jnp.where(low, pltpu.roll(one, 64, 1), two).astype(BF)
    test = (image_ref[:FK] + dot_nt(arrive[...], hot_ref[...])).astype(BF)
    coef = coef_ref[...]
    first_row = lax.broadcasted_iota(jnp.int32, (16, C), 0) == 0
    for f in range(F):
        part = test[f * K : (f + 1) * K]
        here = slice(f * C, (f + 1) * C)
        test_ref[f] = part
        stack[:K, here] = part
        product = dot_nn(coef, part)
        value = base_ref[f : f + 1] + row_scale * (product[0:1] + product[1:2])
        stack[K:ROWS, here] = jnp.where(first_row, value, 0.0).astype(BF)
    whole = stack[...]
    gram = dot_nt(whole, whole) * (row_scale * row_scale)
    gram_ref[...] = jnp.concatenate([gram[:104], jnp.zeros((104, 128 - ROWS), F32)], axis=1)


def finish_call(row_scale, image, row_a, row_b, col_a, col_b, hot, coef, base):
    return pl.pallas_call(
        functools.partial(finish_kernel, row_scale),
        out_shape=(jax.ShapeDtypeStruct((F, K, C), BF), jax.ShapeDtypeStruct((104, 128), F32)),
        in_specs=vmem(8),
        out_specs=tuple(vmem(2)),
        scratch_shapes=[pltpu.VMEM((FK, 256), BF), pltpu.VMEM((ROWS, F * C), BF)],
        compiler_params=pltpu.CompilerParams(vmem_limit_bytes=VMEM_LIMIT),
        name="finish",
    )(image, row_a, row_b, col_a, col_b, hot, coef, base)


TILES = 13


def solve_kernel(row_scale, first_ref, second_ref, factor_ref, step_ref, work):
    work[...] = first_ref[...] + second_ref[...]
    lane = lax.broadcasted_iota(jnp.int32, (8, 128), 1)
    sub = lax.broadcasted_iota(jnp.int32, (8, 128), 0)

    def spread_row(tile, p):
        return jnp.broadcast_to(tile[p : p + 1], (8, 128))

    def spread_lane(tile, j):
        return jnp.broadcast_to(tile[:, j : j + 1], (8, 128))

    tiles = [work[8 * t : 8 * t + 8] for t in range(TILES)]
    for panel in range(12):
        start = 8 * panel
        here = tiles[panel]
        columns = [[spread_lane(tiles[t], start + p) for p in range(8)] for t in range(TILES)]
        rows = [spread_row(here, p) for p in range(8)]
        d = {(p, q): spread_row(columns[panel][q], p) for p in range(8) for q in range(p, 8)}
        m = {}
        inverse = []
        for p in range(8):
            recip = 1.0 / d[p, p]
            inverse.append(recip)
            for q in range(p + 1, 8):
                m[p, q] = d[p, q] * recip
            for q in range(p + 1, 8):
                rows[q] = rows[q] - m[p, q] * rows[p]
                for r in range(q, 8):
                    d[q, r] = d[q, r] - m[p, q] * d[p, r]
        out = jnp.zeros((8, 128), F32)
        for p in range(8):
            out = jnp.where(sub == p, rows[p] * lax.rsqrt(d[p, p]), out)
        out = jnp.where(lane >= start + sub, out, 0.0)
        factor_ref[start : start + 8, :] = out[:, :97]
        for p in range(7, -1, -1):
            rows[p] = rows[p] * inverse[p]
            for q in range(p + 1, 8):
                rows[p] = rows[p] - m[p, q] * rows[q]
        order = [panel + 1] + [t for t in range(TILES) if t not in (panel, panel + 1)]
        for t in order:
            product = [columns[t][p] * rows[p] for p in range(8)]
            while len(product) > 1:
                product = [product[i] + product[i + 1] for i in range(0, len(product), 2)]
            tiles[t] = tiles[t] - product[0]
        new = rows[0]
        for p in range(1, 8):
            new = jnp.where(sub == p, rows[p], new)
        tiles[panel] = new
    last = tiles[12]
    factor_ref[96:97, :] = jnp.where(lane[:1] == 96, jnp.sqrt(last[0:1]), 0.0)[:, :97]
    step = jnp.zeros((1, 128), F32)
    for t in range(12):
        column = spread_lane(tiles[t], 96)
        step = step + jnp.sum(jnp.where(lane == 8 * t + sub, column, 0.0), axis=0, keepdims=True)
    step_ref[...] = step[:, :96] * (-1.0 / row_scale)


def solve_call(row_scale, first, second):
    return pl.pallas_call(
        functools.partial(solve_kernel, row_scale),
        out_shape=(jax.ShapeDtypeStruct((97, 97), F32), jax.ShapeDtypeStruct((1, 96), F32)),
        in_specs=vmem(2),
        out_specs=tuple(vmem(2)),
        scratch_shapes=[pltpu.VMEM((104, 128), F32)],
        compiler_params=pltpu.CompilerParams(vmem_limit_bytes=VMEM_LIMIT),
        name="solve",
    )(first, second)


def swap(x, axis, step):
    count = lax.axis_size(axis)
    return lax.ppermute(x, axis, [(i, i ^ step) for i in range(count)])


def swap_odd(x, axis):
    pairs = []
    for i in range(1, lax.axis_size(axis) - 1, 2):
        pairs += [(i, i + 1), (i + 1, i)]
    return lax.ppermute(x, axis, pairs)


def local(
    reduced_basis,
    cell_jacobian,
    face_cells,
    face_jacobian,
    limiter_flags,
    viscosity,
    ghost_cells,
    ghost_jacobian,
    ghost_counts,
    receive_cells,
    coordinates,
    base_residual,
):
    devices = lax.axis_size(ROW) * lax.axis_size(COL)
    row_scale = (F * C * devices) ** (-0.5)
    basis = reduced_basis.reshape(FK, C)
    jacobian = face_jacobian.transpose(1, 2, 0, 3)
    flags = limiter_flags.reshape(1, N)
    row_a, row_b, col_a, col_b, basis, pair, flags, jacobian, diag, arrive, coords, base, nu = ghost_call(
        ghost_counts.reshape(1, 8), ghost_cells.reshape(1, S), ghost_jacobian,
        basis, face_cells, flags, jacobian, cell_jacobian, receive_cells.reshape(1, S),
        coordinates.reshape(1, K), base_residual, viscosity.reshape(1, F),
    )
    row_a = swap(row_a, ROW, 1)
    row_b = swap_odd(row_b, ROW)
    image, hot, coef = early_call(
        nu, basis, pair, jacobian, flags, arrive, coords
    )
    group = (lax.broadcasted_iota(jnp.int32, (HALF, 128), 1) % 64) // 8
    corner = row_a + row_b
    col_a = jnp.where((group == 4) | (group == 6), corner, col_a)
    col_b = jnp.where((group == 5) | (group == 7), corner, col_b)
    col_a = swap(col_a, COL, 1)
    col_b = swap_odd(col_b, COL)
    image = late_call(nu, basis, diag, pair, jacobian, flags, image)
    test, gram = finish_call(row_scale, image, row_a, row_b, col_a, col_b, hot, coef, base)
    gram = gram + swap(gram, "col_1", 1)
    for axis in ("col_0", "row_1", "row_0"):
        one, two, three = (swap(gram, axis, k) for k in (1, 2, 3))
        first, second = gram + one, two + three
        gram = first + second
    factor, step = solve_call(row_scale, first, second)
    return (test, factor, step.reshape(K))


def solution(mesh):
    torus = Mesh(mesh.devices.reshape(4, 4, 4, 2), ("row_0", "row_1", "col_0", "col_1"))
    in_specs = (
        P(None, None, ROW_COL),
        P(None, None, ROW_COL),
        P(None, ROW_COL),
        P(None, None, None, ROW_COL),
        P(ROW_COL),
        P(),
        P(ROW_COL),
        P(None, None, ROW_COL),
        P(ROW_COL),
        P(ROW_COL),
        P(),
        P(None, ROW_COL),
    )
    out_specs = (P(None, None, ROW_COL), P(), P())
    return jax.shard_map(local, mesh=torus, in_specs=in_specs, out_specs=out_specs, check_vma=False)
```

```python
import functools

import jax
import jax.numpy as jnp
from jax import lax
from jax.experimental import pallas as pl
from jax.experimental.pallas import tpu as pltpu
from jax.sharding import Mesh
from jax.sharding import PartitionSpec as P

ROW = ("row_0", "row_1")
COL = ("col_0", "col_1")
ROW_COL = ROW + COL
F = 5
K = 96
C = 512
N = 1024
S = 160
FK = F * K
HALF = FK // 2
BF = jnp.bfloat16
F32 = jnp.float32
VMEM_LIMIT = 48 * 1024 * 1024


def vmem(count):
    return [pl.BlockSpec(memory_space=pltpu.VMEM)] * count


def one_hot(row):
    cells = lax.broadcasted_iota(jnp.int32, (C, row.shape[1]), 0)
    return jnp.where(cells == row, 1.0, 0.0).astype(BF)


def dot_nn(a, b):
    return lax.dot_general(a, b, (((1,), (0,)), ((), ())), preferred_element_type=F32)


def dot_nt(a, b):
    return lax.dot_general(a, b, (((1,), (1,)), ((), ())), preferred_element_type=F32)


def blocks_of(x):
    ends = [0, 32, 64, 96, 128, 136, 144, 152, 160]
    return [x[..., ends[m] : ends[m + 1]] for m in range(8)]


def pad_like(x, width, fill):
    return jnp.full(x.shape[:-1] + (width,), fill, x.dtype)


def send_order(x, fill, odd_i, odd_j):
    b = blocks_of(x)
    p16, p32 = pad_like(x, 16, fill), pad_like(x, 32, fill)
    corner = jnp.concatenate([b[4], b[5], p16, p16, b[6], b[7], p32, p32], axis=-1)
    lane = lax.broadcasted_iota(jnp.int32, corner.shape, corner.ndim - 1)
    last = corner.ndim - 1
    other = jnp.where((lane // 8) % 2 == 0, pltpu.roll(corner, 120, last), pltpu.roll(corner, 8, last))
    corner = jnp.where(odd_j, corner, other)
    row = jnp.concatenate(
        [b[1], p16, corner[..., 48:64], b[0], corner[..., 0:16], p16], axis=-1
    )
    col = jnp.concatenate([b[3], p32, b[2], p32], axis=-1)
    row = jnp.where(odd_i, pltpu.roll(row, 64, last), row)
    col = jnp.where(odd_j, pltpu.roll(col, 64, last), col)
    return row, col


def receive_order(x, odd_i, odd_j):
    b = blocks_of(x)
    p8, p32 = pad_like(x, 8, -1), pad_like(x, 32, -1)
    row = jnp.concatenate([b[0], p32, b[1], p32], axis=-1)
    row = jnp.where(odd_i, pltpu.roll(row, 64, 1), row)
    even = jnp.concatenate([b[2], b[4], p8, b[6], p8, b[3], p8, b[5], p8, b[7]], axis=-1)
    odd = jnp.concatenate([b[3], b[5], p8, b[7], p8, b[2], p8, b[4], p8, b[6]], axis=-1)
    return row, jnp.where(odd_j, odd, even)


def parities():
    return lax.axis_index("row_1") % 2 == 1, lax.axis_index("col_1") % 2 == 1


def ghost_kernel(count_hbm, cell_hbm, jac_hbm, basis_hbm, pair_hbm, flag_hbm, face_hbm, diag_hbm, arrive_hbm,
                 coord_hbm, base_hbm, nu_hbm, row_a, row_b, col_a, col_b, basis_ref, pair_ref, flag_ref, face_ref,
                 diag_ref, arrive_ref, coord_ref, base_ref, nu_ref, count_ref, cell_ref, jac_ref, val, sems):
    pairs = (
        (basis_hbm, basis_ref), (cell_hbm, cell_ref), (count_hbm, count_ref), (jac_hbm, jac_ref),
        (face_hbm, face_ref), (pair_hbm, pair_ref), (flag_hbm, flag_ref), (diag_hbm, diag_ref),
        (arrive_hbm, arrive_ref), (coord_hbm, coord_ref), (base_hbm, base_ref),
        (nu_hbm, nu_ref),
    )
    copies = [pltpu.make_async_copy(src, dst, sems.at[i]) for i, (src, dst) in enumerate(pairs)]
    for i in (1, 2, 0, 3, 4, 5, 6, 7, 8, 9, 10, 11):
        copies[i].start()
    odd_i, odd_j = parities()
    copies[1].wait()
    copies[2].wait()
    lane = lax.broadcasted_iota(jnp.int32, (1, S), 1)
    limit = jnp.zeros((1, S), jnp.int32)
    for block, start in enumerate((0, 32, 64, 96, 128, 136, 144, 152)):
        limit = jnp.where(lane >= start, count_ref[0:1, block : block + 1] + start, limit)
    index = jnp.where(lane < limit, cell_ref[...], -1)
    hot = one_hot(jnp.concatenate(send_order(index, -1, odd_i, odd_j), axis=-1))
    copies[3].wait()
    weights = [jnp.concatenate(send_order(jac_ref[g], 0.0, odd_i, odd_j), axis=-1) for g in range(F)]
    copies[0].wait()
    taken = dot_nn(basis_ref[...], hot)
    for f in range(F):
        val[f] = taken[f * K : (f + 1) * K]
    low = lax.broadcasted_iota(jnp.int32, (1, 128), 1) < 64
    parts = []
    for g in range(F):
        total = weights[g][0:1] * val[0]
        for f in range(1, F):
            total = total + weights[g][f : f + 1] * val[f]
        parts.append(total)
    full = jnp.concatenate(parts, axis=0)
    for tile, first, second in ((0, row_a, row_b), (1, col_a, col_b)):
        wide = full[:, tile * 128 : (tile + 1) * 128]
        top, bottom = wide[:HALF], wide[HALF:]
        first[...] = jnp.where(low, top, pltpu.roll(bottom, 64, 1)).astype(BF)
        second[...] = jnp.where(low, pltpu.roll(top, 64, 1), bottom).astype(BF)
    for copy in copies[4:]:
        copy.wait()


def ghost_call(counts, cells, jacobian, *loaded):
    message = jax.ShapeDtypeStruct((HALF, 128), BF)
    operands = [pltpu.with_memory_space_constraint(x, pltpu.MemorySpace.HBM) for x in (counts, cells, jacobian) + loaded]
    return pl.pallas_call(
        ghost_kernel,
        out_shape=(message,) * 4 + tuple(jax.ShapeDtypeStruct(x.shape, x.dtype) for x in loaded),
        in_specs=[pl.BlockSpec(memory_space=pltpu.MemorySpace.HBM)] * len(operands),
        out_specs=tuple(vmem(4 + len(loaded))),
        scratch_shapes=[
            pltpu.VMEM((1, 8), jnp.int32),
            pltpu.VMEM((1, S), jnp.int32),
            pltpu.VMEM((F, F, S), F32),
            pltpu.VMEM((F, K, 256), F32),
            pltpu.SemaphoreType.DMA((12,)),
        ],
        compiler_params=pltpu.CompilerParams(vmem_limit_bytes=VMEM_LIMIT),
        name="ghost",
    )(*operands)


BLOCK = 256
HALF_BLOCKS = 2
CHUNK = 32
WIDE = FK + 16


def face_blocks(first_block, nu_ref, basis, pair_ref, jac_ref, flag_ref, hot, got, add, image):
    for block in range(HALF_BLOCKS):
        base = (first_block + block) * BLOCK
        lanes = slice(base, base + BLOCK)
        hot[block, :, :BLOCK] = one_hot(pair_ref[0:1, lanes])
        hot[block, :, BLOCK:] = one_hot(pair_ref[1:2, lanes])
        got[block] = dot_nn(basis, hot[block])
        flags = flag_ref[0:1, lanes].astype(F32)
        add[block, FK:] = jnp.broadcast_to(jnp.concatenate([flags, flags], axis=1), (16, 2 * BLOCK)).astype(BF)
        for tile in range(BLOCK // 128):
            here = slice(base + tile * 128, base + (tile + 1) * 128)
            at_a = slice(tile * 128, (tile + 1) * 128)
            at_b = slice(BLOCK + tile * 128, BLOCK + (tile + 1) * 128)
            damps = [nu_ref[0:1, g : g + 1] * flags[:, at_a] for g in range(F)]
            for start in range(0, K, CHUNK):
                a = [got[block, f * K + start : f * K + start + CHUNK, at_a] for f in range(F)]
                b = [got[block, f * K + start : f * K + start + CHUNK, at_b] for f in range(F)]
                for g in range(F):
                    damp = damps[g]
                    to_a = (jac_ref[g, g, 0:1, here] - damp) * b[g]
                    to_b = (jac_ref[g, g, 1:2, here] - damp) * a[g]
                    for f in range(F):
                        if f != g:
                            to_a = to_a + jac_ref[g, f, 0:1, here] * b[f]
                            to_b = to_b + jac_ref[g, f, 1:2, here] * a[f]
                    rows = slice(g * K + start, g * K + start + CHUNK)
                    add[block, rows, at_a] = to_a.astype(BF)
                    add[block, rows, at_b] = to_b.astype(BF)
    for block in range(HALF_BLOCKS):
        image = dot_nt(add[block], hot[block]) if image is None else image + dot_nt(add[block], hot[block])
    return image


def early_kernel(nu_ref, basis_ref, pair_ref, jac_ref, flag_ref, cell_ref, coord_ref,
                 image_ref, hot_ref, coef_ref, hot, got, add):
    odd_i, odd_j = parities()
    hot_ref[...] = one_hot(jnp.concatenate(receive_order(cell_ref[...], odd_i, odd_j), axis=-1))
    coord = coord_ref[...]
    high = coord.astype(BF).astype(F32)
    row = lax.broadcasted_iota(jnp.int32, (16, K), 0)
    coef_ref[...] = jnp.where(row == 0, high, jnp.where(row == 1, coord - high, 0.0)).astype(BF)
    image_ref[...] = face_blocks(0, nu_ref, basis_ref[...], pair_ref, jac_ref, flag_ref, hot, got, add, None)


def late_kernel(nu_ref, basis_ref, diag_ref, pair_ref, jac_ref, flag_ref, image_ref, out_ref, hot, got, add):
    out_ref[...] = face_blocks(
        HALF_BLOCKS, nu_ref, basis_ref[...], pair_ref, jac_ref, flag_ref, hot, got, add, image_ref[...]
    )
    for tile in range(C // 128):
        here = slice(tile * 128, (tile + 1) * 128)
        flagged = out_ref[FK : FK + 1, here]
        own = [diag_ref[g, g : g + 1, here] + nu_ref[0:1, g : g + 1] * flagged for g in range(F)]
        for start in range(0, K, CHUNK):
            v = [basis_ref[f * K + start : f * K + start + CHUNK, here].astype(F32) for f in range(F)]
            for g in range(F):
                rows = slice(g * K + start, g * K + start + CHUNK)
                total = out_ref[rows, here] + own[g] * v[g]
                for f in range(F):
                    if f != g:
                        total = total + diag_ref[g, f : f + 1, here] * v[f]
                out_ref[rows, here] = total


FACE_SCRATCH = (
    ((HALF_BLOCKS, C, 2 * BLOCK), BF),
    ((HALF_BLOCKS, FK, 2 * BLOCK), F32),
    ((HALF_BLOCKS, WIDE, 2 * BLOCK), BF),
)
FACE_COST = pl.CostEstimate(flops=2_500_000_000, bytes_accessed=2_000_000, transcendentals=0)


def early_call(nu, basis, pair, jacobian, flags, cells, coords):
    return pl.pallas_call(
        early_kernel,
        out_shape=(
            jax.ShapeDtypeStruct((WIDE, C), F32),
            jax.ShapeDtypeStruct((C, 256), BF),
            jax.ShapeDtypeStruct((16, K), BF),
        ),
        in_specs=vmem(7),
        out_specs=tuple(vmem(3)),
        scratch_shapes=[pltpu.VMEM(*scratch) for scratch in FACE_SCRATCH],
        compiler_params=pltpu.CompilerParams(vmem_limit_bytes=VMEM_LIMIT),
        cost_estimate=FACE_COST,
        name="early_faces",
    )(nu, basis, pair, jacobian, flags, cells, coords)


def late_call(nu, basis, diag, pair, jacobian, flags, image):
    return pl.pallas_call(
        late_kernel,
        out_shape=jax.ShapeDtypeStruct((WIDE, C), F32),
        in_specs=vmem(7),
        out_specs=vmem(1)[0],
        scratch_shapes=[pltpu.VMEM(*scratch) for scratch in FACE_SCRATCH],
        compiler_params=pltpu.CompilerParams(vmem_limit_bytes=VMEM_LIMIT),
        cost_estimate=FACE_COST,
        name="late_faces",
    )(nu, basis, diag, pair, jacobian, flags, image)


ROWS = 112


def finish_kernel(row_scale, image_ref, row_a, row_b, col_a, col_b, hot_ref, coef_ref, base_ref,
                  test_ref, gram_ref, arrive, stack):
    low = lax.broadcasted_iota(jnp.int32, (1, 128), 1) < 64
    for tile, first, second in ((0, row_a, row_b), (1, col_a, col_b)):
        here = slice(tile * 128, (tile + 1) * 128)
        one, two = first[...].astype(F32), second[...].astype(F32)
        arrive[:HALF, here] = jnp.where(low, one, pltpu.roll(two, 64, 1)).astype(BF)
        arrive[HALF:, here] = jnp.where(low, pltpu.roll(one, 64, 1), two).astype(BF)
    test = (image_ref[:FK] + dot_nt(arrive[...], hot_ref[...])).astype(BF)
    coef = coef_ref[...]
    first_row = lax.broadcasted_iota(jnp.int32, (16, C), 0) == 0
    for f in range(F):
        part = test[f * K : (f + 1) * K]
        here = slice(f * C, (f + 1) * C)
        test_ref[f] = part
        stack[:K, here] = part
        product = dot_nn(coef, part)
        value = base_ref[f : f + 1] + row_scale * (product[0:1] + product[1:2])
        stack[K:ROWS, here] = jnp.where(first_row, value, 0.0).astype(BF)
    whole = stack[...]
    gram = dot_nt(whole, whole) * (row_scale * row_scale)
    gram_ref[...] = jnp.concatenate([gram[:104], jnp.zeros((104, 128 - ROWS), F32)], axis=1)


def finish_call(row_scale, image, row_a, row_b, col_a, col_b, hot, coef, base):
    return pl.pallas_call(
        functools.partial(finish_kernel, row_scale),
        out_shape=(jax.ShapeDtypeStruct((F, K, C), BF), jax.ShapeDtypeStruct((104, 128), F32)),
        in_specs=vmem(8),
        out_specs=tuple(vmem(2)),
        scratch_shapes=[pltpu.VMEM((FK, 256), BF), pltpu.VMEM((ROWS, F * C), BF)],
        compiler_params=pltpu.CompilerParams(vmem_limit_bytes=VMEM_LIMIT),
        name="finish",
    )(image, row_a, row_b, col_a, col_b, hot, coef, base)


TILES = 13


def solve_kernel(row_scale, one_ref, three_ref, two_ref, own_ref, factor_ref, step_ref, work):
    work[...] = (one_ref[...] + three_ref[...]) + (two_ref[...] + own_ref[...])
    lane = lax.broadcasted_iota(jnp.int32, (8, 128), 1)
    sub = lax.broadcasted_iota(jnp.int32, (8, 128), 0)

    def spread_row(tile, p):
        return jnp.broadcast_to(tile[p : p + 1], (8, 128))

    def spread_lane(tile, j):
        place = jnp.full((8, 128), j, jnp.int32)
        return jnp.take_along_axis(tile, place, axis=1, mode="promise_in_bounds")

    tiles = [work[8 * t : 8 * t + 8] for t in range(TILES)]
    for panel in range(12):
        start = 8 * panel
        here = tiles[panel]
        columns = [[spread_lane(tiles[t], start + p) for p in range(8)] for t in range(TILES)]
        rows = [spread_row(here, p) for p in range(8)]
        d = {(p, q): spread_row(columns[panel][q], p) for p in range(8) for q in range(p, 8)}
        m = {}
        inverse = []
        for p in range(8):
            recip = 1.0 / d[p, p]
            inverse.append(recip)
            for q in range(p + 1, 8):
                m[p, q] = d[p, q] * recip
            for q in range(p + 1, 8):
                rows[q] = rows[q] - m[p, q] * rows[p]
                for r in range(q, 8):
                    d[q, r] = d[q, r] - m[p, q] * d[p, r]
        out = jnp.zeros((8, 128), F32)
        for p in range(8):
            out = jnp.where(sub == p, rows[p] * lax.rsqrt(d[p, p]), out)
        out = jnp.where(lane >= start + sub, out, 0.0)
        factor_ref[start : start + 8, :] = out[:, :97]
        for p in range(7, -1, -1):
            rows[p] = rows[p] * inverse[p]
            for q in range(p + 1, 8):
                rows[p] = rows[p] - m[p, q] * rows[q]
        order = [panel + 1] + [t for t in range(TILES) if t not in (panel, panel + 1)]
        for t in order:
            product = [columns[t][p] * rows[p] for p in range(8)]
            while len(product) > 1:
                product = [product[i] + product[i + 1] for i in range(0, len(product), 2)]
            tiles[t] = tiles[t] - product[0]
        new = rows[0]
        for p in range(1, 8):
            new = jnp.where(sub == p, rows[p], new)
        tiles[panel] = new
    last = tiles[12]
    factor_ref[96:97, :] = jnp.where(lane[:1] == 96, jnp.sqrt(last[0:1]), 0.0)[:, :97]
    step = jnp.zeros((1, 128), F32)
    for t in range(12):
        column = spread_lane(tiles[t], 96)
        step = step + jnp.sum(jnp.where(lane == 8 * t + sub, column, 0.0), axis=0, keepdims=True)
    step_ref[...] = step[:, :96] * (-1.0 / row_scale)


def solve_call(row_scale, *terms):
    return pl.pallas_call(
        functools.partial(solve_kernel, row_scale),
        out_shape=(jax.ShapeDtypeStruct((97, 97), F32), jax.ShapeDtypeStruct((1, 96), F32)),
        in_specs=vmem(4),
        out_specs=tuple(vmem(2)),
        scratch_shapes=[pltpu.VMEM((104, 128), F32)],
        compiler_params=pltpu.CompilerParams(vmem_limit_bytes=VMEM_LIMIT),
        name="solve",
    )(*terms)


def swap(x, axis, step):
    count = lax.axis_size(axis)
    return lax.ppermute(x, axis, [(i, i ^ step) for i in range(count)])


def cross(x, axis, step):
    pairs = [(2 * i + c, 2 * (i ^ step) + 1 - c) for i in range(lax.axis_size(axis)) for c in range(2)]
    return lax.ppermute(x, (axis, "col_1"), pairs)


def swap_odd(x, axis):
    pairs = []
    for i in range(1, lax.axis_size(axis) - 1, 2):
        pairs += [(i, i + 1), (i + 1, i)]
    return lax.ppermute(x, axis, pairs)


def local(
    reduced_basis,
    cell_jacobian,
    face_cells,
    face_jacobian,
    limiter_flags,
    viscosity,
    ghost_cells,
    ghost_jacobian,
    ghost_counts,
    receive_cells,
    coordinates,
    base_residual,
):
    devices = lax.axis_size(ROW) * lax.axis_size(COL)
    row_scale = (F * C * devices) ** (-0.5)
    basis = reduced_basis.reshape(FK, C)
    jacobian = face_jacobian.transpose(1, 2, 0, 3)
    flags = limiter_flags.reshape(1, N)
    row_a, row_b, col_a, col_b, basis, pair, flags, jacobian, diag, arrive, coords, base, nu = ghost_call(
        ghost_counts.reshape(1, 8), ghost_cells.reshape(1, S), ghost_jacobian,
        basis, face_cells, flags, jacobian, cell_jacobian, receive_cells.reshape(1, S),
        coordinates.reshape(1, K), base_residual, viscosity.reshape(1, F),
    )
    row_a = swap(row_a, ROW, 1)
    row_b = swap_odd(row_b, ROW)
    image, hot, coef = early_call(
        nu, basis, pair, jacobian, flags, arrive, coords
    )
    group = (lax.broadcasted_iota(jnp.int32, (HALF, 128), 1) % 64) // 8
    corner = row_a + row_b
    col_a = jnp.where((group == 4) | (group == 6), corner, col_a)
    col_b = jnp.where((group == 5) | (group == 7), corner, col_b)
    col_a = swap(col_a, COL, 1)
    col_b = swap_odd(col_b, COL)
    image = late_call(nu, basis, diag, pair, jacobian, flags, image)
    test, gram = finish_call(row_scale, image, row_a, row_b, col_a, col_b, hot, coef, base)
    gram = gram + swap(gram, "col_1", 1)
    for axis in ("col_0", "row_1", "row_0"):
        one, three, two = (cross(gram, axis, k) for k in (1, 3, 2))
        terms = (one, three, two, gram)
        gram = (one + three) + (two + gram)
    factor, step = solve_call(row_scale, *terms)
    return (test, factor, step.reshape(K))


def solution(mesh):
    torus = Mesh(mesh.devices.reshape(4, 4, 4, 2), ("row_0", "row_1", "col_0", "col_1"))
    in_specs = (
        P(None, None, ROW_COL),
        P(None, None, ROW_COL),
        P(None, ROW_COL),
        P(None, None, None, ROW_COL),
        P(ROW_COL),
        P(),
        P(ROW_COL),
        P(None, None, ROW_COL),
        P(ROW_COL),
        P(ROW_COL),
        P(),
        P(None, ROW_COL),
    )
    out_specs = (P(None, None, ROW_COL), P(), P())
    return jax.shard_map(local, mesh=torus, in_specs=in_specs, out_specs=out_specs, check_vma=False)
```

```python
import functools

import jax
import jax.numpy as jnp
from jax import lax
from jax.experimental import pallas as pl
from jax.experimental.pallas import tpu as pltpu
from jax.sharding import Mesh
from jax.sharding import PartitionSpec as P

ROW = ("row_0", "row_1")
COL = ("col_0", "col_1")
ROW_COL = ROW + COL
F = 5
K = 96
C = 512
N = 1024
S = 160
FK = F * K
HALF = FK // 2
BF = jnp.bfloat16
F32 = jnp.float32
VMEM_LIMIT = 48 * 1024 * 1024


def vmem(count):
    return [pl.BlockSpec(memory_space=pltpu.VMEM)] * count


def one_hot(row):
    cells = lax.broadcasted_iota(jnp.int32, (C, row.shape[1]), 0)
    return jnp.where(cells == row, 1.0, 0.0).astype(BF)


def dot_nn(a, b):
    return lax.dot_general(a, b, (((1,), (0,)), ((), ())), preferred_element_type=F32)


def dot_nt(a, b):
    return lax.dot_general(a, b, (((1,), (1,)), ((), ())), preferred_element_type=F32)


def blocks_of(x):
    ends = [0, 32, 64, 96, 128, 136, 144, 152, 160]
    return [x[..., ends[m] : ends[m + 1]] for m in range(8)]


def pad_like(x, width, fill):
    return jnp.full(x.shape[:-1] + (width,), fill, x.dtype)


def send_order(x, fill, odd_i, odd_j):
    b = blocks_of(x)
    p16, p32 = pad_like(x, 16, fill), pad_like(x, 32, fill)
    corner = jnp.concatenate([b[4], b[5], p16, p16, b[6], b[7], p32, p32], axis=-1)
    lane = lax.broadcasted_iota(jnp.int32, corner.shape, corner.ndim - 1)
    last = corner.ndim - 1
    other = jnp.where((lane // 8) % 2 == 0, pltpu.roll(corner, 120, last), pltpu.roll(corner, 8, last))
    corner = jnp.where(odd_j, corner, other)
    row = jnp.concatenate(
        [b[1], p16, corner[..., 48:64], b[0], corner[..., 0:16], p16], axis=-1
    )
    col = jnp.concatenate([b[3], p32, b[2], p32], axis=-1)
    row = jnp.where(odd_i, pltpu.roll(row, 64, last), row)
    col = jnp.where(odd_j, pltpu.roll(col, 64, last), col)
    return row, col


def receive_order(x, odd_i, odd_j):
    b = blocks_of(x)
    p8, p32 = pad_like(x, 8, -1), pad_like(x, 32, -1)
    row = jnp.concatenate([b[0], p32, b[1], p32], axis=-1)
    row = jnp.where(odd_i, pltpu.roll(row, 64, 1), row)
    even = jnp.concatenate([b[2], b[4], p8, b[6], p8, b[3], p8, b[5], p8, b[7]], axis=-1)
    odd = jnp.concatenate([b[3], b[5], p8, b[7], p8, b[2], p8, b[4], p8, b[6]], axis=-1)
    return row, jnp.where(odd_j, odd, even)


BLOCK_AIMS = (
    (0, -1, 0), (32, 1, 0), (64, 0, -1), (96, 0, 1),
    (128, -1, -1), (136, -1, 1), (144, 1, -1), (152, 1, 1),
)


def parities():
    return lax.axis_index("row_1") % 2 == 1, lax.axis_index("col_1") % 2 == 1


def ghost_kernel(count_hbm, cell_hbm, jac_hbm, basis_hbm, pair_hbm, flag_hbm, face_hbm, diag_hbm, arrive_hbm,
                 coord_hbm, base_hbm, nu_hbm, row_a, row_b, col_a, col_b, basis_ref, pair_ref, flag_ref, face_ref,
                 diag_ref, arrive_ref, coord_ref, base_ref, nu_ref, count_ref, cell_ref, jac_ref, val, sems):
    pairs = (
        (basis_hbm, basis_ref), (cell_hbm, cell_ref), (count_hbm, count_ref), (jac_hbm, jac_ref),
        (face_hbm, face_ref), (pair_hbm, pair_ref), (flag_hbm, flag_ref), (diag_hbm, diag_ref),
        (arrive_hbm, arrive_ref), (coord_hbm, coord_ref), (base_hbm, base_ref),
        (nu_hbm, nu_ref),
    )
    copies = [pltpu.make_async_copy(src, dst, sems.at[i]) for i, (src, dst) in enumerate(pairs)]
    for i in (1, 2, 0, 3, 4, 5, 6, 7, 8, 9, 10, 11):
        copies[i].start()
    odd_i, odd_j = parities()
    copies[1].wait()
    copies[2].wait()
    lane = lax.broadcasted_iota(jnp.int32, (1, S), 1)
    at_i = lax.axis_index("row_0") * lax.axis_size("row_1") + lax.axis_index("row_1")
    at_j = lax.axis_index("col_0") * lax.axis_size("col_1") + lax.axis_index("col_1")
    end_i = lax.axis_size("row_0") * lax.axis_size("row_1") - 1
    end_j = lax.axis_size("col_0") * lax.axis_size("col_1") - 1
    limit = jnp.zeros((1, S), jnp.int32)
    for block, (start, dr, dc) in enumerate(BLOCK_AIMS):
        count = count_ref[0:1, block : block + 1]
        if dr:
            count = jnp.where(at_i == (0 if dr < 0 else end_i), 0, count)
        if dc:
            count = jnp.where(at_j == (0 if dc < 0 else end_j), 0, count)
        limit = jnp.where(lane >= start, count + start, limit)
    index = jnp.where(lane < limit, cell_ref[...], -1)
    hot = one_hot(jnp.concatenate(send_order(index, -1, odd_i, odd_j), axis=-1))
    copies[3].wait()
    weights = [jnp.concatenate(send_order(jac_ref[g], 0.0, odd_i, odd_j), axis=-1) for g in range(F)]
    copies[0].wait()
    taken = dot_nn(basis_ref[...], hot)
    for f in range(F):
        val[f] = taken[f * K : (f + 1) * K]
    low = lax.broadcasted_iota(jnp.int32, (1, 128), 1) < 64
    parts = []
    for g in range(F):
        total = weights[g][0:1] * val[0]
        for f in range(1, F):
            total = total + weights[g][f : f + 1] * val[f]
        parts.append(total)
    full = jnp.concatenate(parts, axis=0)
    for tile, first, second in ((0, row_a, row_b), (1, col_a, col_b)):
        wide = full[:, tile * 128 : (tile + 1) * 128]
        top, bottom = wide[:HALF], wide[HALF:]
        first[...] = jnp.where(low, top, pltpu.roll(bottom, 64, 1)).astype(BF)
        second[...] = jnp.where(low, pltpu.roll(top, 64, 1), bottom).astype(BF)
    for copy in copies[4:]:
        copy.wait()


def ghost_call(counts, cells, jacobian, *loaded):
    message = jax.ShapeDtypeStruct((HALF, 128), BF)
    operands = [pltpu.with_memory_space_constraint(x, pltpu.MemorySpace.HBM) for x in (counts, cells, jacobian) + loaded]
    return pl.pallas_call(
        ghost_kernel,
        out_shape=(message,) * 4 + tuple(jax.ShapeDtypeStruct(x.shape, x.dtype) for x in loaded),
        in_specs=[pl.BlockSpec(memory_space=pltpu.MemorySpace.HBM)] * len(operands),
        out_specs=tuple(vmem(4 + len(loaded))),
        scratch_shapes=[
            pltpu.VMEM((1, 8), jnp.int32),
            pltpu.VMEM((1, S), jnp.int32),
            pltpu.VMEM((F, F, S), F32),
            pltpu.VMEM((F, K, 256), F32),
            pltpu.SemaphoreType.DMA((12,)),
        ],
        compiler_params=pltpu.CompilerParams(vmem_limit_bytes=VMEM_LIMIT),
        name="ghost",
    )(*operands)


BLOCK = 256
HALF_BLOCKS = 2
CHUNK = 32
WIDE = FK + 16


def face_blocks(first_block, nu_ref, basis, pair_ref, jac_ref, flag_ref, hot, got, add, image):
    for block in range(HALF_BLOCKS):
        base = (first_block + block) * BLOCK
        lanes = slice(base, base + BLOCK)
        hot[block, :, :BLOCK] = one_hot(pair_ref[0:1, lanes])
        hot[block, :, BLOCK:] = one_hot(pair_ref[1:2, lanes])
        got[block] = dot_nn(basis, hot[block])
        flags = flag_ref[0:1, lanes].astype(F32)
        add[block, FK:] = jnp.broadcast_to(jnp.concatenate([flags, flags], axis=1), (16, 2 * BLOCK)).astype(BF)
        for tile in range(BLOCK // 128):
            here = slice(base + tile * 128, base + (tile + 1) * 128)
            at_a = slice(tile * 128, (tile + 1) * 128)
            at_b = slice(BLOCK + tile * 128, BLOCK + (tile + 1) * 128)
            damps = [nu_ref[0:1, g : g + 1] * flags[:, at_a] for g in range(F)]
            for start in range(0, K, CHUNK):
                a = [got[block, f * K + start : f * K + start + CHUNK, at_a] for f in range(F)]
                b = [got[block, f * K + start : f * K + start + CHUNK, at_b] for f in range(F)]
                for g in range(F):
                    damp = damps[g]
                    to_a = (jac_ref[g, g, 0:1, here] - damp) * b[g]
                    to_b = (jac_ref[g, g, 1:2, here] - damp) * a[g]
                    for f in range(F):
                        if f != g:
                            to_a = to_a + jac_ref[g, f, 0:1, here] * b[f]
                            to_b = to_b + jac_ref[g, f, 1:2, here] * a[f]
                    rows = slice(g * K + start, g * K + start + CHUNK)
                    add[block, rows, at_a] = to_a.astype(BF)
                    add[block, rows, at_b] = to_b.astype(BF)
    for block in range(HALF_BLOCKS):
        image = dot_nt(add[block], hot[block]) if image is None else image + dot_nt(add[block], hot[block])
    return image


def early_kernel(nu_ref, basis_ref, pair_ref, jac_ref, flag_ref, cell_ref, coord_ref,
                 image_ref, hot_ref, coef_ref, hot, got, add):
    odd_i, odd_j = parities()
    hot_ref[...] = one_hot(jnp.concatenate(receive_order(cell_ref[...], odd_i, odd_j), axis=-1))
    coord = coord_ref[...]
    high = coord.astype(BF).astype(F32)
    row = lax.broadcasted_iota(jnp.int32, (16, K), 0)
    coef_ref[...] = jnp.where(row == 0, high, jnp.where(row == 1, coord - high, 0.0)).astype(BF)
    image_ref[...] = face_blocks(0, nu_ref, basis_ref[...], pair_ref, jac_ref, flag_ref, hot, got, add, None)


def late_kernel(nu_ref, basis_ref, diag_ref, pair_ref, jac_ref, flag_ref, image_ref, out_ref, hot, got, add):
    out_ref[...] = face_blocks(
        HALF_BLOCKS, nu_ref, basis_ref[...], pair_ref, jac_ref, flag_ref, hot, got, add, image_ref[...]
    )
    for tile in range(C // 128):
        here = slice(tile * 128, (tile + 1) * 128)
        flagged = out_ref[FK : FK + 1, here]
        own = [diag_ref[g, g : g + 1, here] + nu_ref[0:1, g : g + 1] * flagged for g in range(F)]
        for start in range(0, K, CHUNK):
            v = [basis_ref[f * K + start : f * K + start + CHUNK, here].astype(F32) for f in range(F)]
            for g in range(F):
                rows = slice(g * K + start, g * K + start + CHUNK)
                total = out_ref[rows, here] + own[g] * v[g]
                for f in range(F):
                    if f != g:
                        total = total + diag_ref[g, f : f + 1, here] * v[f]
                out_ref[rows, here] = total


FACE_SCRATCH = (
    ((HALF_BLOCKS, C, 2 * BLOCK), BF),
    ((HALF_BLOCKS, FK, 2 * BLOCK), F32),
    ((HALF_BLOCKS, WIDE, 2 * BLOCK), BF),
)
FACE_COST = pl.CostEstimate(flops=2_500_000_000, bytes_accessed=2_000_000, transcendentals=0)


def early_call(nu, basis, pair, jacobian, flags, cells, coords):
    return pl.pallas_call(
        early_kernel,
        out_shape=(
            jax.ShapeDtypeStruct((WIDE, C), F32),
            jax.ShapeDtypeStruct((C, 256), BF),
            jax.ShapeDtypeStruct((16, K), BF),
        ),
        in_specs=vmem(7),
        out_specs=tuple(vmem(3)),
        scratch_shapes=[pltpu.VMEM(*scratch) for scratch in FACE_SCRATCH],
        compiler_params=pltpu.CompilerParams(vmem_limit_bytes=VMEM_LIMIT),
        cost_estimate=FACE_COST,
        name="early_faces",
    )(nu, basis, pair, jacobian, flags, cells, coords)


def late_call(nu, basis, diag, pair, jacobian, flags, image):
    return pl.pallas_call(
        late_kernel,
        out_shape=jax.ShapeDtypeStruct((WIDE, C), F32),
        in_specs=vmem(7),
        out_specs=vmem(1)[0],
        scratch_shapes=[pltpu.VMEM(*scratch) for scratch in FACE_SCRATCH],
        compiler_params=pltpu.CompilerParams(vmem_limit_bytes=VMEM_LIMIT),
        cost_estimate=FACE_COST,
        name="late_faces",
    )(nu, basis, diag, pair, jacobian, flags, image)


ROWS = 112


def finish_kernel(row_scale, image_ref, row_a, row_b, col_a, col_b, hot_ref, coef_ref, base_ref,
                  test_ref, gram_ref, arrive, stack):
    low = lax.broadcasted_iota(jnp.int32, (1, 128), 1) < 64
    for tile, first, second in ((0, row_a, row_b), (1, col_a, col_b)):
        here = slice(tile * 128, (tile + 1) * 128)
        one, two = first[...].astype(F32), second[...].astype(F32)
        arrive[:HALF, here] = jnp.where(low, one, pltpu.roll(two, 64, 1)).astype(BF)
        arrive[HALF:, here] = jnp.where(low, pltpu.roll(one, 64, 1), two).astype(BF)
    test = (image_ref[:FK] + dot_nt(arrive[...], hot_ref[...])).astype(BF)
    coef = coef_ref[...]
    first_row = lax.broadcasted_iota(jnp.int32, (16, C), 0) == 0
    for f in range(F):
        part = test[f * K : (f + 1) * K]
        here = slice(f * C, (f + 1) * C)
        test_ref[f] = part
        stack[:K, here] = part
        product = dot_nn(coef, part)
        value = base_ref[f : f + 1] + row_scale * (product[0:1] + product[1:2])
        stack[K:ROWS, here] = jnp.where(first_row, value, 0.0).astype(BF)
    whole = stack[...]
    gram = dot_nt(whole, whole) * (row_scale * row_scale)
    gram_ref[...] = jnp.concatenate([gram[:104], jnp.zeros((104, 128 - ROWS), F32)], axis=1)


def finish_call(row_scale, image, row_a, row_b, col_a, col_b, hot, coef, base):
    return pl.pallas_call(
        functools.partial(finish_kernel, row_scale),
        out_shape=(jax.ShapeDtypeStruct((F, K, C), BF), jax.ShapeDtypeStruct((104, 128), F32)),
        in_specs=vmem(8),
        out_specs=tuple(vmem(2)),
        scratch_shapes=[pltpu.VMEM((FK, 256), BF), pltpu.VMEM((ROWS, F * C), BF)],
        compiler_params=pltpu.CompilerParams(vmem_limit_bytes=VMEM_LIMIT),
        name="finish",
    )(image, row_a, row_b, col_a, col_b, hot, coef, base)


TILES = 13


def solve_kernel(row_scale, one_ref, three_ref, two_ref, own_ref, factor_ref, step_ref, work):
    work[...] = (one_ref[...] + three_ref[...]) + (two_ref[...] + own_ref[...])
    lane = lax.broadcasted_iota(jnp.int32, (8, 128), 1)
    sub = lax.broadcasted_iota(jnp.int32, (8, 128), 0)

    def spread_row(tile, p):
        return jnp.broadcast_to(tile[p : p + 1], (8, 128))

    def spread_lane(tile, j):
        place = jnp.full((8, 128), j, jnp.int32)
        return jnp.take_along_axis(tile, place, axis=1, mode="promise_in_bounds")

    tiles = [work[8 * t : 8 * t + 8] for t in range(TILES)]
    for panel in range(12):
        start = 8 * panel
        here = tiles[panel]
        columns = [[spread_lane(tiles[t], start + p) for p in range(8)] for t in range(TILES)]
        rows = [spread_row(here, p) for p in range(8)]
        d = {(p, q): spread_row(columns[panel][q], p) for p in range(8) for q in range(p, 8)}
        m = {}
        inverse = []
        for p in range(8):
            recip = 1.0 / d[p, p]
            inverse.append(recip)
            for q in range(p + 1, 8):
                m[p, q] = d[p, q] * recip
            for q in range(p + 1, 8):
                rows[q] = rows[q] - m[p, q] * rows[p]
                for r in range(q, 8):
                    d[q, r] = d[q, r] - m[p, q] * d[p, r]
        out = jnp.zeros((8, 128), F32)
        for p in range(8):
            out = jnp.where(sub == p, rows[p] * lax.rsqrt(d[p, p]), out)
        out = jnp.where(lane >= start + sub, out, 0.0)
        factor_ref[start : start + 8, :] = out[:, :97]
        for p in range(7, -1, -1):
            rows[p] = rows[p] * inverse[p]
            for q in range(p + 1, 8):
                rows[p] = rows[p] - m[p, q] * rows[q]
        order = [panel + 1] + [t for t in range(TILES) if t not in (panel, panel + 1)]
        for t in order:
            product = [columns[t][p] * rows[p] for p in range(8)]
            while len(product) > 1:
                product = [product[i] + product[i + 1] for i in range(0, len(product), 2)]
            tiles[t] = tiles[t] - product[0]
        new = rows[0]
        for p in range(1, 8):
            new = jnp.where(sub == p, rows[p], new)
        tiles[panel] = new
    last = tiles[12]
    factor_ref[96:97, :] = jnp.where(lane[:1] == 96, jnp.sqrt(last[0:1]), 0.0)[:, :97]
    step = jnp.zeros((1, 128), F32)
    for t in range(12):
        column = spread_lane(tiles[t], 96)
        step = step + jnp.sum(jnp.where(lane == 8 * t + sub, column, 0.0), axis=0, keepdims=True)
    step_ref[...] = step[:, :96] * (-1.0 / row_scale)


def solve_call(row_scale, *terms):
    return pl.pallas_call(
        functools.partial(solve_kernel, row_scale),
        out_shape=(jax.ShapeDtypeStruct((97, 97), F32), jax.ShapeDtypeStruct((1, 96), F32)),
        in_specs=vmem(4),
        out_specs=tuple(vmem(2)),
        scratch_shapes=[pltpu.VMEM((104, 128), F32)],
        compiler_params=pltpu.CompilerParams(vmem_limit_bytes=VMEM_LIMIT),
        name="solve",
    )(*terms)


def swap(x, axis, step):
    count = lax.axis_size(axis)
    return lax.ppermute(x, axis, [(i, i ^ step) for i in range(count)])


def cross(x, axis, step):
    pairs = [(2 * i + c, 2 * (i ^ step) + 1 - c) for i in range(lax.axis_size(axis)) for c in range(2)]
    return lax.ppermute(x, (axis, "col_1"), pairs)


def swap_odd(x, axis):
    count = lax.axis_size(axis)
    return lax.ppermute(x, axis, [(i, (i + 1) % count if i % 2 else (i - 1) % count) for i in range(count)])


def local(
    reduced_basis,
    cell_jacobian,
    face_cells,
    face_jacobian,
    limiter_flags,
    viscosity,
    ghost_cells,
    ghost_jacobian,
    ghost_counts,
    receive_cells,
    coordinates,
    base_residual,
):
    devices = lax.axis_size(ROW) * lax.axis_size(COL)
    row_scale = (F * C * devices) ** (-0.5)
    basis = reduced_basis.reshape(FK, C)
    jacobian = face_jacobian.transpose(1, 2, 0, 3)
    flags = limiter_flags.reshape(1, N)
    row_a, row_b, col_a, col_b, basis, pair, flags, jacobian, diag, arrive, coords, base, nu = ghost_call(
        ghost_counts.reshape(1, 8), ghost_cells.reshape(1, S), ghost_jacobian,
        basis, face_cells, flags, jacobian, cell_jacobian, receive_cells.reshape(1, S),
        coordinates.reshape(1, K), base_residual, viscosity.reshape(1, F),
    )
    row_a = swap(row_a, ROW, 1)
    row_b = swap_odd(row_b, ROW)
    image, hot, coef = early_call(
        nu, basis, pair, jacobian, flags, arrive, coords
    )
    group = (lax.broadcasted_iota(jnp.int32, (HALF, 128), 1) % 64) // 8
    corner = row_a + row_b
    col_a = jnp.where((group == 4) | (group == 6), corner, col_a)
    col_b = jnp.where((group == 5) | (group == 7), corner, col_b)
    col_a = swap(col_a, COL, 1)
    col_b = swap_odd(col_b, COL)
    image = late_call(nu, basis, diag, pair, jacobian, flags, image)
    test, gram = finish_call(row_scale, image, row_a, row_b, col_a, col_b, hot, coef, base)
    gram = gram + swap(gram, "col_1", 1)
    for axis in ("col_0", "row_1", "row_0"):
        one, three, two = (cross(gram, axis, k) for k in (1, 3, 2))
        terms = (one, three, two, gram)
        gram = (one + three) + (two + gram)
    factor, step = solve_call(row_scale, *terms)
    return (test, factor, step.reshape(K))


def solution(mesh):
    torus = Mesh(mesh.devices.reshape(4, 4, 4, 2), ("row_0", "row_1", "col_0", "col_1"))
    in_specs = (
        P(None, None, ROW_COL),
        P(None, None, ROW_COL),
        P(None, ROW_COL),
        P(None, None, None, ROW_COL),
        P(ROW_COL),
        P(),
        P(ROW_COL),
        P(None, None, ROW_COL),
        P(ROW_COL),
        P(ROW_COL),
        P(),
        P(None, ROW_COL),
    )
    out_specs = (P(None, None, ROW_COL), P(), P())
    return jax.shard_map(local, mesh=torus, in_specs=in_specs, out_specs=out_specs, check_vma=False)
```

```python
import functools

import jax
import jax.numpy as jnp
from jax import lax
from jax.experimental import pallas as pl
from jax.experimental.pallas import tpu as pltpu
from jax.sharding import Mesh
from jax.sharding import PartitionSpec as P

ROW = ("row_0", "row_1")
COL = ("col_0", "col_1")
ROW_COL = ROW + COL
F = 5
K = 96
C = 512
N = 1024
S = 160
FK = F * K
HALF = FK // 2
BF = jnp.bfloat16
F32 = jnp.float32
VMEM_LIMIT = 48 * 1024 * 1024


def vmem(count):
    return [pl.BlockSpec(memory_space=pltpu.VMEM)] * count


def one_hot(row):
    cells = lax.broadcasted_iota(jnp.int32, (C, row.shape[1]), 0)
    return jnp.where(cells == row, 1.0, 0.0).astype(BF)


def dot_nn(a, b):
    return lax.dot_general(a, b, (((1,), (0,)), ((), ())), preferred_element_type=F32)


def dot_nt(a, b):
    return lax.dot_general(a, b, (((1,), (1,)), ((), ())), preferred_element_type=F32)


def blocks_of(x):
    ends = [0, 32, 64, 96, 128, 136, 144, 152, 160]
    return [x[..., ends[m] : ends[m + 1]] for m in range(8)]


def pad_like(x, width, fill):
    return jnp.full(x.shape[:-1] + (width,), fill, x.dtype)


def send_order(x, fill, odd_i, odd_j):
    b = blocks_of(x)
    p16, p32 = pad_like(x, 16, fill), pad_like(x, 32, fill)
    corner = jnp.concatenate([b[4], b[5], p16, p16, b[6], b[7], p32, p32], axis=-1)
    lane = lax.broadcasted_iota(jnp.int32, corner.shape, corner.ndim - 1)
    last = corner.ndim - 1
    other = jnp.where((lane // 8) % 2 == 0, pltpu.roll(corner, 120, last), pltpu.roll(corner, 8, last))
    corner = jnp.where(odd_j, corner, other)
    row = jnp.concatenate(
        [b[1], p16, corner[..., 48:64], b[0], corner[..., 0:16], p16], axis=-1
    )
    col = jnp.concatenate([b[3], p32, b[2], p32], axis=-1)
    row = jnp.where(odd_i, pltpu.roll(row, 64, last), row)
    col = jnp.where(odd_j, pltpu.roll(col, 64, last), col)
    return row, col


def receive_order(x, odd_i, odd_j):
    b = blocks_of(x)
    p8, p32 = pad_like(x, 8, -1), pad_like(x, 32, -1)
    row = jnp.concatenate([b[0], p32, b[1], p32], axis=-1)
    row = jnp.where(odd_i, pltpu.roll(row, 64, 1), row)
    even = jnp.concatenate([b[2], b[4], p8, b[6], p8, b[3], p8, b[5], p8, b[7]], axis=-1)
    odd = jnp.concatenate([b[3], b[5], p8, b[7], p8, b[2], p8, b[4], p8, b[6]], axis=-1)
    return row, jnp.where(odd_j, odd, even)


BLOCK_AIMS = (
    (0, -1, 0), (32, 1, 0), (64, 0, -1), (96, 0, 1),
    (128, -1, -1), (136, -1, 1), (144, 1, -1), (152, 1, 1),
)


def parities():
    return lax.axis_index("row_1") % 2 == 1, lax.axis_index("col_1") % 2 == 1


def ghost_kernel(count_hbm, cell_hbm, jac_hbm, basis_hbm, pair_hbm, flag_hbm, face_hbm, diag_hbm, arrive_hbm,
                 coord_hbm, base_hbm, nu_hbm, row_a, row_b, col_a, col_b, basis_ref, pair_ref, flag_ref, face_ref,
                 diag_ref, arrive_ref, coord_ref, base_ref, nu_ref, count_ref, cell_ref, jac_ref, val, sems):
    pairs = (
        (basis_hbm, basis_ref), (cell_hbm, cell_ref), (count_hbm, count_ref), (jac_hbm, jac_ref),
        (face_hbm, face_ref), (pair_hbm, pair_ref), (flag_hbm, flag_ref), (diag_hbm, diag_ref),
        (arrive_hbm, arrive_ref), (coord_hbm, coord_ref), (base_hbm, base_ref),
        (nu_hbm, nu_ref),
    )
    copies = [pltpu.make_async_copy(src, dst, sems.at[i]) for i, (src, dst) in enumerate(pairs)]
    for i in (1, 2, 0, 3, 4, 5, 6, 7, 8, 9, 10, 11):
        copies[i].start()
    odd_i, odd_j = parities()
    copies[1].wait()
    copies[2].wait()
    lane = lax.broadcasted_iota(jnp.int32, (1, S), 1)
    at_i = lax.axis_index("row_0") * lax.axis_size("row_1") + lax.axis_index("row_1")
    at_j = lax.axis_index("col_0") * lax.axis_size("col_1") + lax.axis_index("col_1")
    end_i = lax.axis_size("row_0") * lax.axis_size("row_1") - 1
    end_j = lax.axis_size("col_0") * lax.axis_size("col_1") - 1
    limit = jnp.zeros((1, S), jnp.int32)
    for block, (start, dr, dc) in enumerate(BLOCK_AIMS):
        count = count_ref[0:1, block : block + 1]
        if dr:
            count = jnp.where(at_i == (0 if dr < 0 else end_i), 0, count)
        if dc:
            count = jnp.where(at_j == (0 if dc < 0 else end_j), 0, count)
        limit = jnp.where(lane >= start, count + start, limit)
    index = jnp.where(lane < limit, cell_ref[...], -1)
    hot = one_hot(jnp.concatenate(send_order(index, -1, odd_i, odd_j), axis=-1))
    copies[3].wait()
    weights = [jnp.concatenate(send_order(jac_ref[g], 0.0, odd_i, odd_j), axis=-1) for g in range(F)]
    copies[0].wait()
    taken = dot_nn(basis_ref[...], hot)
    for f in range(F):
        val[f] = taken[f * K : (f + 1) * K]
    low = lax.broadcasted_iota(jnp.int32, (1, 128), 1) < 64
    parts = []
    for g in range(F):
        total = weights[g][0:1] * val[0]
        for f in range(1, F):
            total = total + weights[g][f : f + 1] * val[f]
        parts.append(total)
    full = jnp.concatenate(parts, axis=0)
    for tile, first, second in ((0, row_a, row_b), (1, col_a, col_b)):
        wide = full[:, tile * 128 : (tile + 1) * 128]
        top, bottom = wide[:HALF], wide[HALF:]
        first[...] = jnp.where(low, top, pltpu.roll(bottom, 64, 1)).astype(BF)
        second[...] = jnp.where(low, pltpu.roll(top, 64, 1), bottom).astype(BF)
    for copy in copies[4:]:
        copy.wait()


def ghost_call(counts, cells, jacobian, *loaded):
    message = jax.ShapeDtypeStruct((HALF, 128), BF)
    operands = [pltpu.with_memory_space_constraint(x, pltpu.MemorySpace.HBM) for x in (counts, cells, jacobian) + loaded]
    return pl.pallas_call(
        ghost_kernel,
        out_shape=(message,) * 4 + tuple(jax.ShapeDtypeStruct(x.shape, x.dtype) for x in loaded),
        in_specs=[pl.BlockSpec(memory_space=pltpu.MemorySpace.HBM)] * len(operands),
        out_specs=tuple(vmem(4 + len(loaded))),
        scratch_shapes=[
            pltpu.VMEM((1, 8), jnp.int32),
            pltpu.VMEM((1, S), jnp.int32),
            pltpu.VMEM((F, F, S), F32),
            pltpu.VMEM((F, K, 256), F32),
            pltpu.SemaphoreType.DMA((12,)),
        ],
        compiler_params=pltpu.CompilerParams(vmem_limit_bytes=VMEM_LIMIT),
        name="ghost",
    )(*operands)


BLOCK = 256
HALF_BLOCKS = 2
CHUNK = 32
WIDE = FK + 16


def face_blocks(first_block, nu_ref, basis, pair_ref, jac_ref, flag_ref, hot, got, add, image):
    for block in range(HALF_BLOCKS):
        base = (first_block + block) * BLOCK
        lanes = slice(base, base + BLOCK)
        hot[block, :, :BLOCK] = one_hot(pair_ref[0:1, lanes])
        hot[block, :, BLOCK:] = one_hot(pair_ref[1:2, lanes])
        got[block] = dot_nn(basis, hot[block])
        flags = flag_ref[0:1, lanes].astype(F32)
        add[block, FK:] = jnp.broadcast_to(jnp.concatenate([flags, flags], axis=1), (16, 2 * BLOCK)).astype(BF)
        for tile in range(BLOCK // 128):
            here = slice(base + tile * 128, base + (tile + 1) * 128)
            at_a = slice(tile * 128, (tile + 1) * 128)
            at_b = slice(BLOCK + tile * 128, BLOCK + (tile + 1) * 128)
            damps = [nu_ref[0:1, g : g + 1] * flags[:, at_a] for g in range(F)]
            for start in range(0, K, CHUNK):
                a = [got[block, f * K + start : f * K + start + CHUNK, at_a] for f in range(F)]
                b = [got[block, f * K + start : f * K + start + CHUNK, at_b] for f in range(F)]
                for g in range(F):
                    damp = damps[g]
                    to_a = (jac_ref[g, g, 0:1, here] - damp) * b[g]
                    to_b = (jac_ref[g, g, 1:2, here] - damp) * a[g]
                    for f in range(F):
                        if f != g:
                            to_a = to_a + jac_ref[g, f, 0:1, here] * b[f]
                            to_b = to_b + jac_ref[g, f, 1:2, here] * a[f]
                    rows = slice(g * K + start, g * K + start + CHUNK)
                    add[block, rows, at_a] = to_a.astype(BF)
                    add[block, rows, at_b] = to_b.astype(BF)
    for block in range(HALF_BLOCKS):
        image = dot_nt(add[block], hot[block]) if image is None else image + dot_nt(add[block], hot[block])
    return image


def early_kernel(nu_ref, basis_ref, pair_ref, jac_ref, flag_ref, cell_ref, coord_ref,
                 image_ref, hot_ref, coef_ref, hot, got, add):
    odd_i, odd_j = parities()
    hot_ref[...] = one_hot(jnp.concatenate(receive_order(cell_ref[...], odd_i, odd_j), axis=-1))
    coord = coord_ref[...]
    high = coord.astype(BF).astype(F32)
    row = lax.broadcasted_iota(jnp.int32, (16, K), 0)
    coef_ref[...] = jnp.where(row == 0, high, jnp.where(row == 1, coord - high, 0.0)).astype(BF)
    image_ref[...] = face_blocks(0, nu_ref, basis_ref[...], pair_ref, jac_ref, flag_ref, hot, got, add, None)


def late_kernel(nu_ref, basis_ref, diag_ref, pair_ref, jac_ref, flag_ref, image_ref, out_ref, hot, got, add):
    out_ref[...] = face_blocks(
        HALF_BLOCKS, nu_ref, basis_ref[...], pair_ref, jac_ref, flag_ref, hot, got, add, image_ref[...]
    )
    for tile in range(C // 128):
        here = slice(tile * 128, (tile + 1) * 128)
        flagged = out_ref[FK : FK + 1, here]
        own = [diag_ref[g, g : g + 1, here] + nu_ref[0:1, g : g + 1] * flagged for g in range(F)]
        for start in range(0, K, CHUNK):
            v = [basis_ref[f * K + start : f * K + start + CHUNK, here].astype(F32) for f in range(F)]
            for g in range(F):
                rows = slice(g * K + start, g * K + start + CHUNK)
                total = out_ref[rows, here] + own[g] * v[g]
                for f in range(F):
                    if f != g:
                        total = total + diag_ref[g, f : f + 1, here] * v[f]
                out_ref[rows, here] = total


FACE_SCRATCH = (
    ((HALF_BLOCKS, C, 2 * BLOCK), BF),
    ((HALF_BLOCKS, FK, 2 * BLOCK), F32),
    ((HALF_BLOCKS, WIDE, 2 * BLOCK), BF),
)
FACE_COST = pl.CostEstimate(flops=2_500_000_000, bytes_accessed=2_000_000, transcendentals=0)


def early_call(nu, basis, pair, jacobian, flags, cells, coords):
    return pl.pallas_call(
        early_kernel,
        out_shape=(
            jax.ShapeDtypeStruct((WIDE, C), F32),
            jax.ShapeDtypeStruct((C, 256), BF),
            jax.ShapeDtypeStruct((16, K), BF),
        ),
        in_specs=vmem(7),
        out_specs=tuple(vmem(3)),
        scratch_shapes=[pltpu.VMEM(*scratch) for scratch in FACE_SCRATCH],
        compiler_params=pltpu.CompilerParams(vmem_limit_bytes=VMEM_LIMIT),
        cost_estimate=FACE_COST,
        name="early_faces",
    )(nu, basis, pair, jacobian, flags, cells, coords)


def late_call(nu, basis, diag, pair, jacobian, flags, image):
    return pl.pallas_call(
        late_kernel,
        out_shape=jax.ShapeDtypeStruct((WIDE, C), F32),
        in_specs=vmem(7),
        out_specs=vmem(1)[0],
        scratch_shapes=[pltpu.VMEM(*scratch) for scratch in FACE_SCRATCH],
        compiler_params=pltpu.CompilerParams(vmem_limit_bytes=VMEM_LIMIT),
        cost_estimate=FACE_COST,
        name="late_faces",
    )(nu, basis, diag, pair, jacobian, flags, image)


ROWS = 128
PACK = 56
MID = K // 2


def grids(rows, first=0):
    row = lax.broadcasted_iota(jnp.int32, (rows, 128), 0) + first
    return row, lax.broadcasted_iota(jnp.int32, (rows, 128), 1)


def pack_gram(gram):
    row, lane = grids(MID)
    lower = pltpu.roll(gram[MID:K], 128 - MID, 1)
    upper = jnp.where((lane < MID) & (lane < row), lower, gram[:MID])
    row, lane = grids(MID, MID)
    diagonal = jnp.sum(jnp.where(row == lane, gram[MID:K], 0.0), axis=0, keepdims=True)
    row, lane = grids(8)
    tail = jnp.where(row == 0, gram[K : K + 1], jnp.where(row == 1, diagonal, 0.0))
    return jnp.concatenate([upper, tail], axis=0)


def unpack_gram(packed, work):
    flipped = packed.T
    row, lane = grids(MID)
    first = packed[:MID]
    turned = jnp.concatenate([flipped, jnp.zeros((128, 128 - PACK), F32)], axis=1)
    work[:MID] = jnp.where((lane < MID) & (lane < row), turned[:MID], first)
    half = jnp.where(lane < row, first, turned[:MID])
    half = pltpu.roll(jnp.where(lane < MID, half, turned[MID:K]), MID, 1)
    half = jnp.where(lane < MID, turned[MID:K], half)
    work[MID:K] = jnp.where(lane == row + MID, packed[MID + 1 : MID + 2], half)
    row, lane = grids(8)
    work[K : K + 8] = jnp.where(row == 0, packed[MID : MID + 1], 0.0)


def finish_kernel(row_scale, image_ref, row_a, row_b, col_a, col_b, hot_ref, coef_ref, base_ref,
                  test_ref, gram_ref, arrive, stack):
    low = lax.broadcasted_iota(jnp.int32, (1, 128), 1) < 64
    for tile, first, second in ((0, row_a, row_b), (1, col_a, col_b)):
        here = slice(tile * 128, (tile + 1) * 128)
        one, two = first[...].astype(F32), second[...].astype(F32)
        arrive[:HALF, here] = jnp.where(low, one, pltpu.roll(two, 64, 1)).astype(BF)
        arrive[HALF:, here] = jnp.where(low, pltpu.roll(one, 64, 1), two).astype(BF)
    test = (image_ref[:FK] + dot_nt(arrive[...], hot_ref[...])).astype(BF)
    coef = coef_ref[...]
    first_row = lax.broadcasted_iota(jnp.int32, (ROWS - K, C), 0) == 0
    for f in range(F):
        part = test[f * K : (f + 1) * K]
        here = slice(f * C, (f + 1) * C)
        test_ref[f] = part
        stack[:K, here] = part
        product = dot_nn(coef, part)
        value = base_ref[f : f + 1] + row_scale * (product[0:1] + product[1:2])
        stack[K:ROWS, here] = jnp.where(first_row, value, 0.0).astype(BF)
    whole = stack[...]
    gram = dot_nt(whole, whole) * (row_scale * row_scale)
    gram_ref[...] = pack_gram(gram)


def finish_call(row_scale, image, row_a, row_b, col_a, col_b, hot, coef, base):
    return pl.pallas_call(
        functools.partial(finish_kernel, row_scale),
        out_shape=(jax.ShapeDtypeStruct((F, K, C), BF), jax.ShapeDtypeStruct((PACK, 128), F32)),
        in_specs=vmem(8),
        out_specs=tuple(vmem(2)),
        scratch_shapes=[pltpu.VMEM((FK, 256), BF), pltpu.VMEM((ROWS, F * C), BF)],
        compiler_params=pltpu.CompilerParams(vmem_limit_bytes=VMEM_LIMIT),
        name="finish",
    )(image, row_a, row_b, col_a, col_b, hot, coef, base)


TILES = 13


def solve_kernel(row_scale, one_ref, three_ref, two_ref, own_ref, factor_ref, step_ref, work):
    unpack_gram((one_ref[...] + three_ref[...]) + (two_ref[...] + own_ref[...]), work)
    lane = lax.broadcasted_iota(jnp.int32, (8, 128), 1)
    sub = lax.broadcasted_iota(jnp.int32, (8, 128), 0)

    def spread_row(tile, p):
        return jnp.broadcast_to(tile[p : p + 1], (8, 128))

    def spread_lane(tile, j):
        place = jnp.full((8, 128), j, jnp.int32)
        return jnp.take_along_axis(tile, place, axis=1, mode="promise_in_bounds")

    tiles = [work[8 * t : 8 * t + 8] for t in range(TILES)]
    for panel in range(12):
        start = 8 * panel
        here = tiles[panel]
        columns = [[spread_lane(tiles[t], start + p) for p in range(8)] for t in range(TILES)]
        rows = [spread_row(here, p) for p in range(8)]
        d = {(p, q): spread_row(columns[panel][q], p) for p in range(8) for q in range(p, 8)}
        m = {}
        inverse = []
        for p in range(8):
            recip = 1.0 / d[p, p]
            inverse.append(recip)
            for q in range(p + 1, 8):
                m[p, q] = d[p, q] * recip
            for q in range(p + 1, 8):
                rows[q] = rows[q] - m[p, q] * rows[p]
                for r in range(q, 8):
                    d[q, r] = d[q, r] - m[p, q] * d[p, r]
        out = jnp.zeros((8, 128), F32)
        for p in range(8):
            out = jnp.where(sub == p, rows[p] * lax.rsqrt(d[p, p]), out)
        out = jnp.where(lane >= start + sub, out, 0.0)
        factor_ref[start : start + 8, :] = out[:, :97]
        for p in range(7, -1, -1):
            rows[p] = rows[p] * inverse[p]
            for q in range(p + 1, 8):
                rows[p] = rows[p] - m[p, q] * rows[q]
        order = [panel + 1] + [t for t in range(TILES) if t not in (panel, panel + 1)]
        for t in order:
            product = [columns[t][p] * rows[p] for p in range(8)]
            while len(product) > 1:
                product = [product[i] + product[i + 1] for i in range(0, len(product), 2)]
            tiles[t] = tiles[t] - product[0]
        new = rows[0]
        for p in range(1, 8):
            new = jnp.where(sub == p, rows[p], new)
        tiles[panel] = new
    last = tiles[12]
    factor_ref[96:97, :] = jnp.where(lane[:1] == 96, jnp.sqrt(last[0:1]), 0.0)[:, :97]
    step = jnp.zeros((1, 128), F32)
    for t in range(12):
        column = spread_lane(tiles[t], 96)
        step = step + jnp.sum(jnp.where(lane == 8 * t + sub, column, 0.0), axis=0, keepdims=True)
    step_ref[...] = step[:, :96] * (-1.0 / row_scale)


def solve_call(row_scale, *terms):
    return pl.pallas_call(
        functools.partial(solve_kernel, row_scale),
        out_shape=(jax.ShapeDtypeStruct((97, 97), F32), jax.ShapeDtypeStruct((1, 96), F32)),
        in_specs=vmem(4),
        out_specs=tuple(vmem(2)),
        scratch_shapes=[pltpu.VMEM((104, 128), F32)],
        compiler_params=pltpu.CompilerParams(vmem_limit_bytes=VMEM_LIMIT),
        name="solve",
    )(*terms)


def swap(x, axis, step):
    count = lax.axis_size(axis)
    return lax.ppermute(x, axis, [(i, i ^ step) for i in range(count)])


def cross(x, axis, step):
    pairs = [(2 * i + c, 2 * (i ^ step) + 1 - c) for i in range(lax.axis_size(axis)) for c in range(2)]
    return lax.ppermute(x, (axis, "col_1"), pairs)


def swap_odd(x, axis):
    count = lax.axis_size(axis)
    return lax.ppermute(x, axis, [(i, (i + 1) % count if i % 2 else (i - 1) % count) for i in range(count)])


def local(
    reduced_basis,
    cell_jacobian,
    face_cells,
    face_jacobian,
    limiter_flags,
    viscosity,
    ghost_cells,
    ghost_jacobian,
    ghost_counts,
    receive_cells,
    coordinates,
    base_residual,
):
    devices = lax.axis_size(ROW) * lax.axis_size(COL)
    row_scale = (F * C * devices) ** (-0.5)
    basis = reduced_basis.reshape(FK, C)
    jacobian = face_jacobian.transpose(1, 2, 0, 3)
    flags = limiter_flags.reshape(1, N)
    row_a, row_b, col_a, col_b, basis, pair, flags, jacobian, diag, arrive, coords, base, nu = ghost_call(
        ghost_counts.reshape(1, 8), ghost_cells.reshape(1, S), ghost_jacobian,
        basis, face_cells, flags, jacobian, cell_jacobian, receive_cells.reshape(1, S),
        coordinates.reshape(1, K), base_residual, viscosity.reshape(1, F),
    )
    row_a = swap(row_a, ROW, 1)
    row_b = swap_odd(row_b, ROW)
    image, hot, coef = early_call(
        nu, basis, pair, jacobian, flags, arrive, coords
    )
    group = (lax.broadcasted_iota(jnp.int32, (HALF, 128), 1) % 64) // 8
    corner = row_a + row_b
    col_a = jnp.where((group == 4) | (group == 6), corner, col_a)
    col_b = jnp.where((group == 5) | (group == 7), corner, col_b)
    col_a = swap(col_a, COL, 1)
    col_b = swap_odd(col_b, COL)
    image = late_call(nu, basis, diag, pair, jacobian, flags, image)
    test, gram = finish_call(row_scale, image, row_a, row_b, col_a, col_b, hot, coef, base)
    gram = gram + swap(gram, "col_1", 1)
    for axis in ("col_0", "row_1", "row_0"):
        one, three, two = (cross(gram, axis, k) for k in (1, 3, 2))
        terms = (one, three, two, gram)
        gram = (one + three) + (two + gram)
    factor, step = solve_call(row_scale, *terms)
    return (test, factor, step.reshape(K))


def solution(mesh):
    torus = Mesh(mesh.devices.reshape(4, 4, 4, 2), ("row_0", "row_1", "col_0", "col_1"))
    in_specs = (
        P(None, None, ROW_COL),
        P(None, None, ROW_COL),
        P(None, ROW_COL),
        P(None, None, None, ROW_COL),
        P(ROW_COL),
        P(),
        P(ROW_COL),
        P(None, None, ROW_COL),
        P(ROW_COL),
        P(ROW_COL),
        P(),
        P(None, ROW_COL),
    )
    out_specs = (P(None, None, ROW_COL), P(), P())
    return jax.shard_map(local, mesh=torus, in_specs=in_specs, out_specs=out_specs, check_vma=False)
```

```python
import functools

import jax
import jax.numpy as jnp
from jax import lax
from jax.experimental import pallas as pl
from jax.experimental.pallas import tpu as pltpu
from jax.sharding import Mesh
from jax.sharding import PartitionSpec as P

ROW = ("row_0", "row_1")
COL = ("col_0", "col_1")
ROW_COL = ROW + COL
F = 5
K = 96
C = 512
N = 1024
S = 160
FK = F * K
HALF = FK // 2
BF = jnp.bfloat16
F32 = jnp.float32
VMEM_LIMIT = 48 * 1024 * 1024


def vmem(count):
    return [pl.BlockSpec(memory_space=pltpu.VMEM)] * count


def one_hot(row):
    cells = lax.broadcasted_iota(jnp.int32, (C, row.shape[1]), 0)
    return jnp.where(cells == row, 1.0, 0.0).astype(BF)


def dot_nn(a, b):
    return lax.dot_general(a, b, (((1,), (0,)), ((), ())), preferred_element_type=F32)


def dot_nt(a, b):
    return lax.dot_general(a, b, (((1,), (1,)), ((), ())), preferred_element_type=F32)


def blocks_of(x):
    ends = [0, 32, 64, 96, 128, 136, 144, 152, 160]
    return [x[..., ends[m] : ends[m + 1]] for m in range(8)]


def pad_like(x, width, fill):
    return jnp.full(x.shape[:-1] + (width,), fill, x.dtype)


def send_order(x, fill, odd_i, odd_j):
    b = blocks_of(x)
    p16, p32 = pad_like(x, 16, fill), pad_like(x, 32, fill)
    corner = jnp.concatenate([b[4], b[5], p16, p16, b[6], b[7], p32, p32], axis=-1)
    lane = lax.broadcasted_iota(jnp.int32, corner.shape, corner.ndim - 1)
    last = corner.ndim - 1
    other = jnp.where((lane // 8) % 2 == 0, pltpu.roll(corner, 120, last), pltpu.roll(corner, 8, last))
    corner = jnp.where(odd_j, corner, other)
    row = jnp.concatenate(
        [b[1], p16, corner[..., 48:64], b[0], corner[..., 0:16], p16], axis=-1
    )
    col = jnp.concatenate([b[3], p32, b[2], p32], axis=-1)
    row = jnp.where(odd_i, pltpu.roll(row, 64, last), row)
    col = jnp.where(odd_j, pltpu.roll(col, 64, last), col)
    return row, col


def receive_order(x, odd_i, odd_j):
    b = blocks_of(x)
    p8, p32 = pad_like(x, 8, -1), pad_like(x, 32, -1)
    row = jnp.concatenate([b[0], p32, b[1], p32], axis=-1)
    row = jnp.where(odd_i, pltpu.roll(row, 64, 1), row)
    even = jnp.concatenate([b[2], b[4], p8, b[6], p8, b[3], p8, b[5], p8, b[7]], axis=-1)
    odd = jnp.concatenate([b[3], b[5], p8, b[7], p8, b[2], p8, b[4], p8, b[6]], axis=-1)
    return row, jnp.where(odd_j, odd, even)


BLOCK_AIMS = (
    (0, -1, 0), (32, 1, 0), (64, 0, -1), (96, 0, 1),
    (128, -1, -1), (136, -1, 1), (144, 1, -1), (152, 1, 1),
)


def parities():
    return lax.axis_index("row_1") % 2 == 1, lax.axis_index("col_1") % 2 == 1


def ghost_kernel(count_hbm, cell_hbm, jac_hbm, basis_hbm, pair_hbm, flag_hbm, face_hbm, diag_hbm, arrive_hbm,
                 coord_hbm, base_hbm, nu_hbm, row_a, row_b, col_a, col_b, basis_ref, pair_ref, flag_ref, face_ref,
                 diag_ref, arrive_ref, coord_ref, base_ref, nu_ref, count_ref, cell_ref, jac_ref, val, sems):
    pairs = (
        (basis_hbm, basis_ref), (cell_hbm, cell_ref), (count_hbm, count_ref), (jac_hbm, jac_ref),
        (face_hbm, face_ref), (pair_hbm, pair_ref), (flag_hbm, flag_ref), (diag_hbm, diag_ref),
        (arrive_hbm, arrive_ref), (coord_hbm, coord_ref), (base_hbm, base_ref),
        (nu_hbm, nu_ref),
    )
    copies = [pltpu.make_async_copy(src, dst, sems.at[i]) for i, (src, dst) in enumerate(pairs)]
    for i in (1, 2, 0, 3, 4, 5, 6, 7, 8, 9, 10, 11):
        copies[i].start()
    odd_i, odd_j = parities()
    copies[1].wait()
    copies[2].wait()
    lane = lax.broadcasted_iota(jnp.int32, (1, S), 1)
    at_i = lax.axis_index("row_0") * lax.axis_size("row_1") + lax.axis_index("row_1")
    at_j = lax.axis_index("col_0") * lax.axis_size("col_1") + lax.axis_index("col_1")
    end_i = lax.axis_size("row_0") * lax.axis_size("row_1") - 1
    end_j = lax.axis_size("col_0") * lax.axis_size("col_1") - 1
    limit = jnp.zeros((1, S), jnp.int32)
    for block, (start, dr, dc) in enumerate(BLOCK_AIMS):
        count = count_ref[0:1, block : block + 1]
        if dr:
            count = jnp.where(at_i == (0 if dr < 0 else end_i), 0, count)
        if dc:
            count = jnp.where(at_j == (0 if dc < 0 else end_j), 0, count)
        limit = jnp.where(lane >= start, count + start, limit)
    index = jnp.where(lane < limit, cell_ref[...], -1)
    hot = one_hot(jnp.concatenate(send_order(index, -1, odd_i, odd_j), axis=-1))
    copies[3].wait()
    weights = [jnp.concatenate(send_order(jac_ref[g], 0.0, odd_i, odd_j), axis=-1) for g in range(F)]
    copies[0].wait()
    taken = dot_nn(basis_ref[...], hot)
    for f in range(F):
        val[f] = taken[f * K : (f + 1) * K]
    low = lax.broadcasted_iota(jnp.int32, (1, 128), 1) < 64
    parts = []
    for g in range(F):
        total = weights[g][0:1] * val[0]
        for f in range(1, F):
            total = total + weights[g][f : f + 1] * val[f]
        parts.append(total)
    full = jnp.concatenate(parts, axis=0)
    for tile, first, second in ((0, row_a, row_b), (1, col_a, col_b)):
        wide = full[:, tile * 128 : (tile + 1) * 128]
        top, bottom = wide[:HALF], wide[HALF:]
        first[...] = jnp.where(low, top, pltpu.roll(bottom, 64, 1)).astype(BF)
        second[...] = jnp.where(low, pltpu.roll(top, 64, 1), bottom).astype(BF)
    for copy in copies[4:]:
        copy.wait()


def ghost_call(counts, cells, jacobian, *loaded):
    message = jax.ShapeDtypeStruct((HALF, 128), BF)
    operands = [pltpu.with_memory_space_constraint(x, pltpu.MemorySpace.HBM) for x in (counts, cells, jacobian) + loaded]
    return pl.pallas_call(
        ghost_kernel,
        out_shape=(message,) * 4 + tuple(jax.ShapeDtypeStruct(x.shape, x.dtype) for x in loaded),
        in_specs=[pl.BlockSpec(memory_space=pltpu.MemorySpace.HBM)] * len(operands),
        out_specs=tuple(vmem(4 + len(loaded))),
        scratch_shapes=[
            pltpu.VMEM((1, 8), jnp.int32),
            pltpu.VMEM((1, S), jnp.int32),
            pltpu.VMEM((F, F, S), F32),
            pltpu.VMEM((F, K, 256), F32),
            pltpu.SemaphoreType.DMA((12,)),
        ],
        compiler_params=pltpu.CompilerParams(vmem_limit_bytes=VMEM_LIMIT),
        name="ghost",
    )(*operands)


BLOCK = 256
EARLY = 3
LATE = 1
CHUNK = 32
WIDE = FK + 16


def face_blocks(first_block, count, nu_ref, basis, pair_ref, jac_ref, flag_ref, hot, got, add, image):
    for block in range(count):
        base = (first_block + block) * BLOCK
        lanes = slice(base, base + BLOCK)
        hot[block, :, :BLOCK] = one_hot(pair_ref[0:1, lanes])
        hot[block, :, BLOCK:] = one_hot(pair_ref[1:2, lanes])
        got[block] = dot_nn(basis, hot[block])
        flags = flag_ref[0:1, lanes].astype(F32)
        add[block, FK:] = jnp.broadcast_to(jnp.concatenate([flags, flags], axis=1), (16, 2 * BLOCK)).astype(BF)
        for tile in range(BLOCK // 128):
            here = slice(base + tile * 128, base + (tile + 1) * 128)
            at_a = slice(tile * 128, (tile + 1) * 128)
            at_b = slice(BLOCK + tile * 128, BLOCK + (tile + 1) * 128)
            damps = [nu_ref[0:1, g : g + 1] * flags[:, at_a] for g in range(F)]
            for start in range(0, K, CHUNK):
                a = [got[block, f * K + start : f * K + start + CHUNK, at_a] for f in range(F)]
                b = [got[block, f * K + start : f * K + start + CHUNK, at_b] for f in range(F)]
                for g in range(F):
                    damp = damps[g]
                    to_a = (jac_ref[g, g, 0:1, here] - damp) * b[g]
                    to_b = (jac_ref[g, g, 1:2, here] - damp) * a[g]
                    for f in range(F):
                        if f != g:
                            to_a = to_a + jac_ref[g, f, 0:1, here] * b[f]
                            to_b = to_b + jac_ref[g, f, 1:2, here] * a[f]
                    rows = slice(g * K + start, g * K + start + CHUNK)
                    add[block, rows, at_a] = to_a.astype(BF)
                    add[block, rows, at_b] = to_b.astype(BF)
    for block in range(count):
        image = dot_nt(add[block], hot[block]) if image is None else image + dot_nt(add[block], hot[block])
    return image


def add_diagonal(image_ref, basis_ref, nu_ref, diag_ref):
    for tile in range(C // 128):
        here = slice(tile * 128, (tile + 1) * 128)
        flagged = image_ref[FK : FK + 1, here]
        own = [diag_ref[g, g : g + 1, here] + nu_ref[0:1, g : g + 1] * flagged for g in range(F)]
        for start in range(0, K, CHUNK):
            v = [basis_ref[f * K + start : f * K + start + CHUNK, here].astype(F32) for f in range(F)]
            for g in range(F):
                rows = slice(g * K + start, g * K + start + CHUNK)
                total = image_ref[rows, here] + own[g] * v[g]
                for f in range(F):
                    if f != g:
                        total = total + diag_ref[g, f : f + 1, here] * v[f]
                image_ref[rows, here] = total


def early_kernel(nu_ref, basis_ref, diag_ref, pair_ref, jac_ref, flag_ref, cell_ref, coord_ref,
                 image_ref, hot_ref, coef_ref, hot, got, add):
    odd_i, odd_j = parities()
    hot_ref[...] = one_hot(jnp.concatenate(receive_order(cell_ref[...], odd_i, odd_j), axis=-1))
    coord = coord_ref[...]
    high = coord.astype(BF).astype(F32)
    row = lax.broadcasted_iota(jnp.int32, (16, K), 0)
    coef_ref[...] = jnp.where(row == 0, high, jnp.where(row == 1, coord - high, 0.0)).astype(BF)
    image_ref[...] = face_blocks(0, EARLY, nu_ref, basis_ref[...], pair_ref, jac_ref, flag_ref, hot, got, add, None)
    add_diagonal(image_ref, basis_ref, nu_ref, diag_ref)


def late_kernel(nu_ref, basis_ref, pair_ref, jac_ref, flag_ref, image_ref, out_ref, hot, got, add):
    image = face_blocks(EARLY, LATE, nu_ref, basis_ref[...], pair_ref, jac_ref, flag_ref, hot, got, add, None)
    flagged = image[FK : FK + 1]
    for g in range(F):
        rows = slice(g * K, (g + 1) * K)
        damp = (nu_ref[0:1, g : g + 1] * flagged) * basis_ref[rows].astype(F32)
        out_ref[rows] = (image_ref[rows] + image[rows]) + damp


def face_scratch(count):
    return [
        pltpu.VMEM((count, C, 2 * BLOCK), BF),
        pltpu.VMEM((count, FK, 2 * BLOCK), F32),
        pltpu.VMEM((count, WIDE, 2 * BLOCK), BF),
    ]


def face_cost(count):
    return pl.CostEstimate(flops=count * 1_250_000_000, bytes_accessed=2_000_000, transcendentals=0)


def early_call(nu, basis, diag, pair, jacobian, flags, cells, coords):
    return pl.pallas_call(
        early_kernel,
        out_shape=(
            jax.ShapeDtypeStruct((WIDE, C), F32),
            jax.ShapeDtypeStruct((C, 256), BF),
            jax.ShapeDtypeStruct((16, K), BF),
        ),
        in_specs=vmem(8),
        out_specs=tuple(vmem(3)),
        scratch_shapes=face_scratch(EARLY),
        compiler_params=pltpu.CompilerParams(vmem_limit_bytes=VMEM_LIMIT),
        cost_estimate=face_cost(EARLY),
        name="early_faces",
    )(nu, basis, diag, pair, jacobian, flags, cells, coords)


def late_call(nu, basis, pair, jacobian, flags, image):
    return pl.pallas_call(
        late_kernel,
        out_shape=jax.ShapeDtypeStruct((FK, C), F32),
        in_specs=vmem(6),
        out_specs=vmem(1)[0],
        scratch_shapes=face_scratch(LATE),
        compiler_params=pltpu.CompilerParams(vmem_limit_bytes=VMEM_LIMIT),
        cost_estimate=face_cost(LATE),
        name="late_faces",
    )(nu, basis, pair, jacobian, flags, image)


ROWS = 128
PACK = 56
MID = K // 2


def grids(rows, first=0):
    row = lax.broadcasted_iota(jnp.int32, (rows, 128), 0) + first
    return row, lax.broadcasted_iota(jnp.int32, (rows, 128), 1)


def pack_gram(gram):
    row, lane = grids(MID)
    lower = pltpu.roll(gram[MID:K], 128 - MID, 1)
    upper = jnp.where((lane < MID) & (lane < row), lower, gram[:MID])
    row, lane = grids(MID, MID)
    diagonal = jnp.sum(jnp.where(row == lane, gram[MID:K], 0.0), axis=0, keepdims=True)
    row, lane = grids(8)
    tail = jnp.where(row == 0, gram[K : K + 1], jnp.where(row == 1, diagonal, 0.0))
    return jnp.concatenate([upper, tail], axis=0)


def unpack_gram(packed, work):
    flipped = packed.T
    row, lane = grids(MID)
    first = packed[:MID]
    turned = jnp.concatenate([flipped, jnp.zeros((128, 128 - PACK), F32)], axis=1)
    work[:MID] = jnp.where((lane < MID) & (lane < row), turned[:MID], first)
    half = jnp.where(lane < row, first, turned[:MID])
    half = pltpu.roll(jnp.where(lane < MID, half, turned[MID:K]), MID, 1)
    half = jnp.where(lane < MID, turned[MID:K], half)
    work[MID:K] = jnp.where(lane == row + MID, packed[MID + 1 : MID + 2], half)
    row, lane = grids(8)
    work[K : K + 8] = jnp.where(row == 0, packed[MID : MID + 1], 0.0)


def finish_kernel(row_scale, image_ref, row_a, row_b, col_a, col_b, hot_ref, coef_ref, base_ref,
                  test_ref, gram_ref, arrive, stack):
    low = lax.broadcasted_iota(jnp.int32, (1, 128), 1) < 64
    for tile, first, second in ((0, row_a, row_b), (1, col_a, col_b)):
        here = slice(tile * 128, (tile + 1) * 128)
        one, two = first[...].astype(F32), second[...].astype(F32)
        arrive[:HALF, here] = jnp.where(low, one, pltpu.roll(two, 64, 1)).astype(BF)
        arrive[HALF:, here] = jnp.where(low, pltpu.roll(one, 64, 1), two).astype(BF)
    test = (image_ref[...] + dot_nt(arrive[...], hot_ref[...])).astype(BF)
    coef = coef_ref[...]
    first_row = lax.broadcasted_iota(jnp.int32, (ROWS - K, C), 0) == 0
    for f in range(F):
        part = test[f * K : (f + 1) * K]
        here = slice(f * C, (f + 1) * C)
        test_ref[f] = part
        stack[:K, here] = part
        product = dot_nn(coef, part)
        value = base_ref[f : f + 1] + row_scale * (product[0:1] + product[1:2])
        stack[K:ROWS, here] = jnp.where(first_row, value, 0.0).astype(BF)
    whole = stack[...]
    gram = dot_nt(whole, whole) * (row_scale * row_scale)
    gram_ref[...] = pack_gram(gram)


def finish_call(row_scale, image, row_a, row_b, col_a, col_b, hot, coef, base):
    return pl.pallas_call(
        functools.partial(finish_kernel, row_scale),
        out_shape=(jax.ShapeDtypeStruct((F, K, C), BF), jax.ShapeDtypeStruct((PACK, 128), F32)),
        in_specs=vmem(8),
        out_specs=tuple(vmem(2)),
        scratch_shapes=[pltpu.VMEM((FK, 256), BF), pltpu.VMEM((ROWS, F * C), BF)],
        compiler_params=pltpu.CompilerParams(vmem_limit_bytes=VMEM_LIMIT),
        name="finish",
    )(image, row_a, row_b, col_a, col_b, hot, coef, base)


TILES = 13


def solve_kernel(row_scale, one_ref, three_ref, two_ref, own_ref, test_ref, factor_ref, step_ref, out_hbm, work, sem):
    copy = pltpu.make_async_copy(test_ref, out_hbm, sem.at[0])
    copy.start()
    unpack_gram((one_ref[...] + three_ref[...]) + (two_ref[...] + own_ref[...]), work)
    lane = lax.broadcasted_iota(jnp.int32, (8, 128), 1)
    sub = lax.broadcasted_iota(jnp.int32, (8, 128), 0)

    def spread_row(tile, p):
        return jnp.broadcast_to(tile[p : p + 1], (8, 128))

    def spread_lane(tile, j):
        place = jnp.full((8, 128), j, jnp.int32)
        return jnp.take_along_axis(tile, place, axis=1, mode="promise_in_bounds")

    tiles = [work[8 * t : 8 * t + 8] for t in range(TILES)]
    for panel in range(12):
        start = 8 * panel
        here = tiles[panel]
        columns = [[spread_lane(tiles[t], start + p) for p in range(8)] for t in range(TILES)]
        rows = [spread_row(here, p) for p in range(8)]
        d = {(p, q): spread_row(columns[panel][q], p) for p in range(8) for q in range(p, 8)}
        m = {}
        inverse = []
        for p in range(8):
            recip = 1.0 / d[p, p]
            inverse.append(recip)
            for q in range(p + 1, 8):
                m[p, q] = d[p, q] * recip
            for q in range(p + 1, 8):
                rows[q] = rows[q] - m[p, q] * rows[p]
                for r in range(q, 8):
                    d[q, r] = d[q, r] - m[p, q] * d[p, r]
        out = jnp.zeros((8, 128), F32)
        for p in range(8):
            out = jnp.where(sub == p, rows[p] * lax.rsqrt(d[p, p]), out)
        out = jnp.where(lane >= start + sub, out, 0.0)
        factor_ref[start : start + 8, :] = out[:, :97]
        for p in range(7, -1, -1):
            rows[p] = rows[p] * inverse[p]
            for q in range(p + 1, 8):
                rows[p] = rows[p] - m[p, q] * rows[q]
        order = [panel + 1] + [t for t in range(TILES) if t not in (panel, panel + 1)]
        for t in order:
            product = [columns[t][p] * rows[p] for p in range(8)]
            while len(product) > 1:
                product = [product[i] + product[i + 1] for i in range(0, len(product), 2)]
            tiles[t] = tiles[t] - product[0]
        new = rows[0]
        for p in range(1, 8):
            new = jnp.where(sub == p, rows[p], new)
        tiles[panel] = new
    last = tiles[12]
    factor_ref[96:97, :] = jnp.where(lane[:1] == 96, jnp.sqrt(last[0:1]), 0.0)[:, :97]
    step = jnp.zeros((1, 128), F32)
    for t in range(12):
        column = spread_lane(tiles[t], 96)
        step = step + jnp.sum(jnp.where(lane == 8 * t + sub, column, 0.0), axis=0, keepdims=True)
    step_ref[...] = step[:, :96] * (-1.0 / row_scale)
    copy.wait()


def solve_call(row_scale, *terms):
    return pl.pallas_call(
        functools.partial(solve_kernel, row_scale),
        out_shape=(
            jax.ShapeDtypeStruct((97, 97), F32),
            jax.ShapeDtypeStruct((1, 96), F32),
            jax.ShapeDtypeStruct((F, K, C), BF),
        ),
        in_specs=vmem(5),
        out_specs=tuple(vmem(2)) + (pl.BlockSpec(memory_space=pltpu.MemorySpace.HBM),),
        scratch_shapes=[pltpu.VMEM((104, 128), F32), pltpu.SemaphoreType.DMA((1,))],
        compiler_params=pltpu.CompilerParams(vmem_limit_bytes=VMEM_LIMIT),
        name="solve",
    )(*terms)


def swap(x, axis, step):
    count = lax.axis_size(axis)
    return lax.ppermute(x, axis, [(i, i ^ step) for i in range(count)])


def cross(x, axis, step):
    pairs = [(2 * i + c, 2 * (i ^ step) + 1 - c) for i in range(lax.axis_size(axis)) for c in range(2)]
    return lax.ppermute(x, (axis, "col_1"), pairs)


def swap_odd(x, axis):
    count = lax.axis_size(axis)
    return lax.ppermute(x, axis, [(i, (i + 1) % count if i % 2 else (i - 1) % count) for i in range(count)])


def local(
    reduced_basis,
    cell_jacobian,
    face_cells,
    face_jacobian,
    limiter_flags,
    viscosity,
    ghost_cells,
    ghost_jacobian,
    ghost_counts,
    receive_cells,
    coordinates,
    base_residual,
):
    devices = lax.axis_size(ROW) * lax.axis_size(COL)
    row_scale = (F * C * devices) ** (-0.5)
    basis = reduced_basis.reshape(FK, C)
    jacobian = face_jacobian.transpose(1, 2, 0, 3)
    flags = limiter_flags.reshape(1, N)
    row_a, row_b, col_a, col_b, basis, pair, flags, jacobian, diag, arrive, coords, base, nu = ghost_call(
        ghost_counts.reshape(1, 8), ghost_cells.reshape(1, S), ghost_jacobian,
        basis, face_cells, flags, jacobian, cell_jacobian, receive_cells.reshape(1, S),
        coordinates.reshape(1, K), base_residual, viscosity.reshape(1, F),
    )
    row_a = swap(row_a, ROW, 1)
    row_b = swap_odd(row_b, ROW)
    image, hot, coef = early_call(
        nu, basis, diag, pair, jacobian, flags, arrive, coords
    )
    group = (lax.broadcasted_iota(jnp.int32, (HALF, 128), 1) % 64) // 8
    corner = row_a + row_b
    col_a = jnp.where((group == 4) | (group == 6), corner, col_a)
    col_b = jnp.where((group == 5) | (group == 7), corner, col_b)
    col_a = swap(col_a, COL, 1)
    col_b = swap_odd(col_b, COL)
    image = late_call(nu, basis, pair, jacobian, flags, image)
    test, gram = finish_call(row_scale, image, row_a, row_b, col_a, col_b, hot, coef, base)
    gram = gram + swap(gram, "col_1", 1)
    for axis in ("col_0", "row_1", "row_0"):
        one, three, two = (cross(gram, axis, k) for k in (1, 3, 2))
        terms = (one, three, two, gram)
        gram = (one + three) + (two + gram)
    factor, step, test = solve_call(row_scale, *terms, test)
    return (test, factor, step.reshape(K))


def solution(mesh):
    torus = Mesh(mesh.devices.reshape(4, 4, 4, 2), ("row_0", "row_1", "col_0", "col_1"))
    in_specs = (
        P(None, None, ROW_COL),
        P(None, None, ROW_COL),
        P(None, ROW_COL),
        P(None, None, None, ROW_COL),
        P(ROW_COL),
        P(),
        P(ROW_COL),
        P(None, None, ROW_COL),
        P(ROW_COL),
        P(ROW_COL),
        P(),
        P(None, ROW_COL),
    )
    out_specs = (P(None, None, ROW_COL), P(), P())
    return jax.shard_map(local, mesh=torus, in_specs=in_specs, out_specs=out_specs, check_vma=False)
```

```python
import functools

import jax
import jax.numpy as jnp
from jax import lax
from jax.experimental import pallas as pl
from jax.experimental.pallas import tpu as pltpu
from jax.sharding import Mesh
from jax.sharding import PartitionSpec as P

ROW = ("row_0", "row_1")
COL = ("col_0", "col_1")
ROW_COL = ROW + COL
F = 5
K = 96
C = 512
N = 1024
S = 160
FK = F * K
HALF = FK // 2
BF = jnp.bfloat16
F32 = jnp.float32
VMEM_LIMIT = 48 * 1024 * 1024


def vmem(count):
    return [pl.BlockSpec(memory_space=pltpu.VMEM)] * count


def one_hot(row):
    cells = lax.broadcasted_iota(jnp.int16, (C, row.shape[1]), 0)
    return jnp.where(cells == row.astype(jnp.int16), jnp.ones((), BF), jnp.zeros((), BF))


def dot_nn(a, b):
    return lax.dot_general(a, b, (((1,), (0,)), ((), ())), preferred_element_type=F32)


def dot_nt(a, b):
    return lax.dot_general(a, b, (((1,), (1,)), ((), ())), preferred_element_type=F32)


def blocks_of(x):
    ends = [0, 32, 64, 96, 128, 136, 144, 152, 160]
    return [x[..., ends[m] : ends[m + 1]] for m in range(8)]


def pad_like(x, width, fill):
    return jnp.full(x.shape[:-1] + (width,), fill, x.dtype)


def send_order(x, fill, odd_i, odd_j):
    b = blocks_of(x)
    p16, p32 = pad_like(x, 16, fill), pad_like(x, 32, fill)
    corner = jnp.concatenate([b[4], b[5], p16, p16, b[6], b[7], p32, p32], axis=-1)
    lane = lax.broadcasted_iota(jnp.int32, corner.shape, corner.ndim - 1)
    last = corner.ndim - 1
    other = jnp.where((lane // 8) % 2 == 0, pltpu.roll(corner, 120, last), pltpu.roll(corner, 8, last))
    corner = jnp.where(odd_j, corner, other)
    row = jnp.concatenate(
        [b[1], p16, corner[..., 48:64], b[0], corner[..., 0:16], p16], axis=-1
    )
    col = jnp.concatenate([b[3], p32, b[2], p32], axis=-1)
    row = jnp.where(odd_i, pltpu.roll(row, 64, last), row)
    col = jnp.where(odd_j, pltpu.roll(col, 64, last), col)
    return row, col


def receive_order(x, odd_i, odd_j):
    b = blocks_of(x)
    p8, p32 = pad_like(x, 8, -1), pad_like(x, 32, -1)
    row = jnp.concatenate([b[0], p32, b[1], p32], axis=-1)
    row = jnp.where(odd_i, pltpu.roll(row, 64, 1), row)
    even = jnp.concatenate([b[2], b[4], p8, b[6], p8, b[3], p8, b[5], p8, b[7]], axis=-1)
    odd = jnp.concatenate([b[3], b[5], p8, b[7], p8, b[2], p8, b[4], p8, b[6]], axis=-1)
    return row, jnp.where(odd_j, odd, even)


BLOCK_AIMS = (
    (0, -1, 0), (32, 1, 0), (64, 0, -1), (96, 0, 1),
    (128, -1, -1), (136, -1, 1), (144, 1, -1), (152, 1, 1),
)


def parities():
    return lax.axis_index("row_1") % 2 == 1, lax.axis_index("col_1") % 2 == 1


def ghost_kernel(count_hbm, cell_hbm, jac_hbm, basis_hbm, pair_hbm, flag_hbm, face_hbm, diag_hbm, arrive_hbm,
                 coord_hbm, base_hbm, nu_hbm, row_a, row_b, col_a, col_b, basis_ref, pair_ref, flag_ref, face_ref,
                 diag_ref, arrive_ref, coord_ref, base_ref, nu_ref, count_ref, cell_ref, jac_ref, val, sems):
    pairs = (
        (basis_hbm, basis_ref), (cell_hbm, cell_ref), (count_hbm, count_ref), (jac_hbm, jac_ref),
        (face_hbm, face_ref), (pair_hbm, pair_ref), (flag_hbm, flag_ref), (diag_hbm, diag_ref),
        (arrive_hbm, arrive_ref), (coord_hbm, coord_ref), (base_hbm, base_ref),
        (nu_hbm, nu_ref),
    )
    copies = [pltpu.make_async_copy(src, dst, sems.at[i]) for i, (src, dst) in enumerate(pairs)]
    for i in (1, 2, 0, 3, 4, 5, 6, 7, 8, 9, 10, 11):
        copies[i].start()
    odd_i, odd_j = parities()
    copies[1].wait()
    copies[2].wait()
    lane = lax.broadcasted_iota(jnp.int32, (1, S), 1)
    at_i = lax.axis_index("row_0") * lax.axis_size("row_1") + lax.axis_index("row_1")
    at_j = lax.axis_index("col_0") * lax.axis_size("col_1") + lax.axis_index("col_1")
    end_i = lax.axis_size("row_0") * lax.axis_size("row_1") - 1
    end_j = lax.axis_size("col_0") * lax.axis_size("col_1") - 1
    limit = jnp.zeros((1, S), jnp.int32)
    for block, (start, dr, dc) in enumerate(BLOCK_AIMS):
        count = count_ref[0:1, block : block + 1]
        if dr:
            count = jnp.where(at_i == (0 if dr < 0 else end_i), 0, count)
        if dc:
            count = jnp.where(at_j == (0 if dc < 0 else end_j), 0, count)
        limit = jnp.where(lane >= start, count + start, limit)
    index = jnp.where(lane < limit, cell_ref[...], -1)
    hot = one_hot(jnp.concatenate(send_order(index, -1, odd_i, odd_j), axis=-1))
    copies[3].wait()
    weights = [jnp.concatenate(send_order(jac_ref[g], 0.0, odd_i, odd_j), axis=-1) for g in range(F)]
    copies[0].wait()
    taken = dot_nn(basis_ref[...], hot)
    for f in range(F):
        val[f] = taken[f * K : (f + 1) * K]
    low = lax.broadcasted_iota(jnp.int32, (1, 128), 1) < 64
    parts = []
    for g in range(F):
        total = weights[g][0:1] * val[0]
        for f in range(1, F):
            total = total + weights[g][f : f + 1] * val[f]
        parts.append(total)
    full = jnp.concatenate(parts, axis=0)
    for tile, first, second in ((0, row_a, row_b), (1, col_a, col_b)):
        wide = full[:, tile * 128 : (tile + 1) * 128]
        top, bottom = wide[:HALF], wide[HALF:]
        first[...] = jnp.where(low, top, pltpu.roll(bottom, 64, 1)).astype(BF)
        second[...] = jnp.where(low, pltpu.roll(top, 64, 1), bottom).astype(BF)
    for copy in copies[4:]:
        copy.wait()


def ghost_call(counts, cells, jacobian, *loaded):
    message = jax.ShapeDtypeStruct((HALF, 128), BF)
    operands = [pltpu.with_memory_space_constraint(x, pltpu.MemorySpace.HBM) for x in (counts, cells, jacobian) + loaded]
    return pl.pallas_call(
        ghost_kernel,
        out_shape=(message,) * 4 + tuple(jax.ShapeDtypeStruct(x.shape, x.dtype) for x in loaded),
        in_specs=[pl.BlockSpec(memory_space=pltpu.MemorySpace.HBM)] * len(operands),
        out_specs=tuple(vmem(4 + len(loaded))),
        scratch_shapes=[
            pltpu.VMEM((1, 8), jnp.int32),
            pltpu.VMEM((1, S), jnp.int32),
            pltpu.VMEM((F, F, S), F32),
            pltpu.VMEM((F, K, 256), F32),
            pltpu.SemaphoreType.DMA((12,)),
        ],
        compiler_params=pltpu.CompilerParams(vmem_limit_bytes=VMEM_LIMIT),
        name="ghost",
    )(*operands)


BLOCK = 256
EARLY = 3
LATE = 1
CHUNK = 32
WIDE = FK + 16


def face_blocks(first_block, count, nu_ref, basis, pair_ref, jac_ref, flag_ref, hot, got, add):
    for block in range(count):
        base = (first_block + block) * BLOCK
        lanes = slice(base, base + BLOCK)
        left = 2 * block * BLOCK
        both = slice(left, left + 2 * BLOCK)
        hot[:, left : left + BLOCK] = one_hot(pair_ref[0:1, lanes])
        hot[:, left + BLOCK : left + 2 * BLOCK] = one_hot(pair_ref[1:2, lanes])
        got[:, both] = dot_nn(basis, hot[:, both]).astype(BF)
        flags = flag_ref[0:1, lanes].astype(F32)
        add[FK:, both] = jnp.broadcast_to(jnp.concatenate([flags, flags], axis=1), (16, 2 * BLOCK)).astype(BF)
        for tile in range(BLOCK // 128):
            here = slice(base + tile * 128, base + (tile + 1) * 128)
            at_a = slice(left + tile * 128, left + (tile + 1) * 128)
            at_b = slice(left + BLOCK + tile * 128, left + BLOCK + (tile + 1) * 128)
            damps = [nu_ref[0:1, g : g + 1] * flags[:, tile * 128 : (tile + 1) * 128] for g in range(F)]
            for start in range(0, K, CHUNK):
                a = [got[f * K + start : f * K + start + CHUNK, at_a].astype(F32) for f in range(F)]
                b = [got[f * K + start : f * K + start + CHUNK, at_b].astype(F32) for f in range(F)]
                for g in range(F):
                    to_a = (jac_ref[g, g, 0:1, here] - damps[g]) * b[g]
                    to_b = (jac_ref[g, g, 1:2, here] - damps[g]) * a[g]
                    for f in range(F):
                        if f != g:
                            to_a = to_a + jac_ref[g, f, 0:1, here] * b[f]
                            to_b = to_b + jac_ref[g, f, 1:2, here] * a[f]
                    rows = slice(g * K + start, g * K + start + CHUNK)
                    add[rows, at_a] = to_a.astype(BF)
                    add[rows, at_b] = to_b.astype(BF)
    return dot_nt(add[...], hot[...])


def add_diagonal(image_ref, basis_ref, nu_ref, diag_ref):
    for tile in range(C // 128):
        here = slice(tile * 128, (tile + 1) * 128)
        flagged = image_ref[FK : FK + 1, here]
        own = [diag_ref[g, g : g + 1, here] + nu_ref[0:1, g : g + 1] * flagged for g in range(F)]
        for start in range(0, K, CHUNK):
            v = [basis_ref[f * K + start : f * K + start + CHUNK, here].astype(F32) for f in range(F)]
            for g in range(F):
                rows = slice(g * K + start, g * K + start + CHUNK)
                total = image_ref[rows, here] + own[g] * v[g]
                for f in range(F):
                    if f != g:
                        total = total + diag_ref[g, f : f + 1, here] * v[f]
                image_ref[rows, here] = total


def early_kernel(nu_ref, basis_ref, diag_ref, pair_ref, jac_ref, flag_ref, cell_ref, coord_ref,
                 image_ref, hot_ref, coef_ref, hot, got, add):
    odd_i, odd_j = parities()
    hot_ref[...] = one_hot(jnp.concatenate(receive_order(cell_ref[...], odd_i, odd_j), axis=-1))
    coord = coord_ref[...]
    high = coord.astype(BF).astype(F32)
    row = lax.broadcasted_iota(jnp.int32, (16, K), 0)
    coef_ref[...] = jnp.where(row == 0, high, jnp.where(row == 1, coord - high, 0.0)).astype(BF)
    image_ref[...] = face_blocks(0, EARLY, nu_ref, basis_ref[...], pair_ref, jac_ref, flag_ref, hot, got, add)
    add_diagonal(image_ref, basis_ref, nu_ref, diag_ref)


def late_kernel(nu_ref, basis_ref, pair_ref, jac_ref, flag_ref, image_ref, out_ref, hot, got, add):
    image = face_blocks(EARLY, LATE, nu_ref, basis_ref[...], pair_ref, jac_ref, flag_ref, hot, got, add)
    flagged = image[FK : FK + 1]
    for g in range(F):
        rows = slice(g * K, (g + 1) * K)
        damp = (nu_ref[0:1, g : g + 1] * flagged) * basis_ref[rows].astype(F32)
        out_ref[rows] = (image_ref[rows] + image[rows]) + damp


def face_scratch(count):
    return [pltpu.VMEM((rows, 2 * count * BLOCK), BF) for rows in (C, FK, WIDE)]


def face_cost(count):
    return pl.CostEstimate(flops=count * 1_250_000_000, bytes_accessed=2_000_000, transcendentals=0)


def early_call(nu, basis, diag, pair, jacobian, flags, cells, coords):
    return pl.pallas_call(
        early_kernel,
        out_shape=(
            jax.ShapeDtypeStruct((WIDE, C), F32),
            jax.ShapeDtypeStruct((C, 256), BF),
            jax.ShapeDtypeStruct((16, K), BF),
        ),
        in_specs=vmem(8),
        out_specs=tuple(vmem(3)),
        scratch_shapes=face_scratch(EARLY),
        compiler_params=pltpu.CompilerParams(vmem_limit_bytes=VMEM_LIMIT),
        cost_estimate=face_cost(EARLY),
        name="early_faces",
    )(nu, basis, diag, pair, jacobian, flags, cells, coords)


def late_call(nu, basis, pair, jacobian, flags, image):
    return pl.pallas_call(
        late_kernel,
        out_shape=jax.ShapeDtypeStruct((FK, C), F32),
        in_specs=vmem(6),
        out_specs=vmem(1)[0],
        scratch_shapes=face_scratch(LATE),
        compiler_params=pltpu.CompilerParams(vmem_limit_bytes=VMEM_LIMIT),
        cost_estimate=face_cost(LATE),
        name="late_faces",
    )(nu, basis, pair, jacobian, flags, image)


ROWS = 128
PACK = 56
MID = K // 2


def grids(rows, first=0):
    row = lax.broadcasted_iota(jnp.int32, (rows, 128), 0) + first
    return row, lax.broadcasted_iota(jnp.int32, (rows, 128), 1)


def pack_gram(gram):
    row, lane = grids(MID)
    lower = pltpu.roll(gram[MID:K], 128 - MID, 1)
    upper = jnp.where((lane < MID) & (lane < row), lower, gram[:MID])
    row, lane = grids(MID, MID)
    diagonal = jnp.sum(jnp.where(row == lane, gram[MID:K], 0.0), axis=0, keepdims=True)
    row, lane = grids(8)
    tail = jnp.where(row == 0, gram[K : K + 1], jnp.where(row == 1, diagonal, 0.0))
    return jnp.concatenate([upper, tail], axis=0)


def unpack_gram(packed, work):
    flipped = packed.T
    row, lane = grids(MID)
    first = packed[:MID]
    turned = jnp.concatenate([flipped, jnp.zeros((128, 128 - PACK), F32)], axis=1)
    work[:MID] = jnp.where((lane < MID) & (lane < row), turned[:MID], first)
    half = jnp.where(lane < row, first, turned[:MID])
    half = pltpu.roll(jnp.where(lane < MID, half, turned[MID:K]), MID, 1)
    half = jnp.where(lane < MID, turned[MID:K], half)
    work[MID:K] = jnp.where(lane == row + MID, packed[MID + 1 : MID + 2], half)
    row, lane = grids(8)
    work[K : K + 8] = jnp.where(row == 0, packed[MID : MID + 1], 0.0)


def finish_kernel(row_scale, image_ref, row_a, row_b, col_a, col_b, hot_ref, coef_ref, base_ref,
                  test_ref, gram_ref, arrive, stack):
    low = lax.broadcasted_iota(jnp.int32, (1, 128), 1) < 64
    for tile, first, second in ((0, row_a, row_b), (1, col_a, col_b)):
        here = slice(tile * 128, (tile + 1) * 128)
        one, two = first[...].astype(F32), second[...].astype(F32)
        arrive[:HALF, here] = jnp.where(low, one, pltpu.roll(two, 64, 1)).astype(BF)
        arrive[HALF:, here] = jnp.where(low, pltpu.roll(one, 64, 1), two).astype(BF)
    test = (image_ref[...] + dot_nt(arrive[...], hot_ref[...])).astype(BF)
    coef = coef_ref[...]
    first_row = lax.broadcasted_iota(jnp.int32, (ROWS - K, C), 0) == 0
    for f in range(F):
        part = test[f * K : (f + 1) * K]
        here = slice(f * C, (f + 1) * C)
        test_ref[f] = part
        stack[:K, here] = part
        product = dot_nn(coef, part)
        value = base_ref[f : f + 1] + row_scale * (product[0:1] + product[1:2])
        stack[K:ROWS, here] = jnp.where(first_row, value, 0.0).astype(BF)
    whole = stack[...]
    gram = dot_nt(whole, whole) * (row_scale * row_scale)
    gram_ref[...] = pack_gram(gram)


def finish_call(row_scale, image, row_a, row_b, col_a, col_b, hot, coef, base):
    return pl.pallas_call(
        functools.partial(finish_kernel, row_scale),
        out_shape=(jax.ShapeDtypeStruct((F, K, C), BF), jax.ShapeDtypeStruct((PACK, 128), F32)),
        in_specs=vmem(8),
        out_specs=tuple(vmem(2)),
        scratch_shapes=[pltpu.VMEM((FK, 256), BF), pltpu.VMEM((ROWS, F * C), BF)],
        compiler_params=pltpu.CompilerParams(vmem_limit_bytes=VMEM_LIMIT),
        name="finish",
    )(image, row_a, row_b, col_a, col_b, hot, coef, base)


TILES = 13


def solve_kernel(row_scale, one_ref, three_ref, two_ref, own_ref, test_ref, factor_ref, step_ref, out_hbm, work, sem):
    copy = pltpu.make_async_copy(test_ref, out_hbm, sem.at[0])
    copy.start()
    unpack_gram((one_ref[...] + three_ref[...]) + (two_ref[...] + own_ref[...]), work)
    lane = lax.broadcasted_iota(jnp.int32, (8, 128), 1)
    sub = lax.broadcasted_iota(jnp.int32, (8, 128), 0)

    def spread_row(tile, p):
        return jnp.broadcast_to(tile[p : p + 1], (8, 128))

    def spread_lane(tile, j):
        place = jnp.full((8, 128), j, jnp.int32)
        return jnp.take_along_axis(tile, place, axis=1, mode="promise_in_bounds")

    tiles = [work[8 * t : 8 * t + 8] for t in range(TILES)]
    for panel in range(12):
        start = 8 * panel
        here = tiles[panel]
        columns = [[spread_lane(tiles[t], start + p) for p in range(8)] for t in range(TILES)]
        rows = [spread_row(here, p) for p in range(8)]
        d = {(p, q): spread_row(columns[panel][q], p) for p in range(8) for q in range(p, 8)}
        m = {}
        inverse = []
        for p in range(8):
            recip = 1.0 / d[p, p]
            inverse.append(recip)
            for q in range(p + 1, 8):
                m[p, q] = d[p, q] * recip
            for q in range(p + 1, 8):
                rows[q] = rows[q] - m[p, q] * rows[p]
                for r in range(q, 8):
                    d[q, r] = d[q, r] - m[p, q] * d[p, r]
        out = jnp.zeros((8, 128), F32)
        for p in range(8):
            out = jnp.where(sub == p, rows[p] * lax.rsqrt(d[p, p]), out)
        out = jnp.where(lane >= start + sub, out, 0.0)
        factor_ref[start : start + 8, :] = out[:, :97]
        for p in range(7, -1, -1):
            rows[p] = rows[p] * inverse[p]
            for q in range(p + 1, 8):
                rows[p] = rows[p] - m[p, q] * rows[q]
        order = [panel + 1] + [t for t in range(TILES) if t not in (panel, panel + 1)]
        for t in order:
            product = [columns[t][p] * rows[p] for p in range(8)]
            while len(product) > 1:
                product = [product[i] + product[i + 1] for i in range(0, len(product), 2)]
            tiles[t] = tiles[t] - product[0]
        new = rows[0]
        for p in range(1, 8):
            new = jnp.where(sub == p, rows[p], new)
        tiles[panel] = new
    last = tiles[12]
    factor_ref[96:97, :] = jnp.where(lane[:1] == 96, jnp.sqrt(last[0:1]), 0.0)[:, :97]
    step = jnp.zeros((1, 128), F32)
    for t in range(12):
        column = spread_lane(tiles[t], 96)
        step = step + jnp.sum(jnp.where(lane == 8 * t + sub, column, 0.0), axis=0, keepdims=True)
    step_ref[...] = step[:, :96] * (-1.0 / row_scale)
    copy.wait()


def solve_call(row_scale, *terms):
    return pl.pallas_call(
        functools.partial(solve_kernel, row_scale),
        out_shape=(
            jax.ShapeDtypeStruct((97, 97), F32),
            jax.ShapeDtypeStruct((1, 96), F32),
            jax.ShapeDtypeStruct((F, K, C), BF),
        ),
        in_specs=vmem(5),
        out_specs=tuple(vmem(2)) + (pl.BlockSpec(memory_space=pltpu.MemorySpace.HBM),),
        scratch_shapes=[pltpu.VMEM((104, 128), F32), pltpu.SemaphoreType.DMA((1,))],
        compiler_params=pltpu.CompilerParams(vmem_limit_bytes=VMEM_LIMIT),
        name="solve",
    )(*terms)


def swap(x, axis, step):
    count = lax.axis_size(axis)
    return lax.ppermute(x, axis, [(i, i ^ step) for i in range(count)])


def cross(x, axis, step):
    pairs = [(2 * i + c, 2 * (i ^ step) + 1 - c) for i in range(lax.axis_size(axis)) for c in range(2)]
    return lax.ppermute(x, (axis, "col_1"), pairs)


def swap_odd(x, axis):
    count = lax.axis_size(axis)
    return lax.ppermute(x, axis, [(i, (i + 1) % count if i % 2 else (i - 1) % count) for i in range(count)])


def local(
    reduced_basis,
    cell_jacobian,
    face_cells,
    face_jacobian,
    limiter_flags,
    viscosity,
    ghost_cells,
    ghost_jacobian,
    ghost_counts,
    receive_cells,
    coordinates,
    base_residual,
):
    devices = lax.axis_size(ROW) * lax.axis_size(COL)
    row_scale = (F * C * devices) ** (-0.5)
    basis = reduced_basis.reshape(FK, C)
    jacobian = face_jacobian.transpose(1, 2, 0, 3)
    flags = limiter_flags.reshape(1, N)
    row_a, row_b, col_a, col_b, basis, pair, flags, jacobian, diag, arrive, coords, base, nu = ghost_call(
        ghost_counts.reshape(1, 8), ghost_cells.reshape(1, S), ghost_jacobian,
        basis, face_cells, flags, jacobian, cell_jacobian, receive_cells.reshape(1, S),
        coordinates.reshape(1, K), base_residual, viscosity.reshape(1, F),
    )
    row_a = swap(row_a, ROW, 1)
    row_b = swap_odd(row_b, ROW)
    image, hot, coef = early_call(
        nu, basis, diag, pair, jacobian, flags, arrive, coords
    )
    group = (lax.broadcasted_iota(jnp.int32, (HALF, 128), 1) % 64) // 8
    corner = row_a + row_b
    col_a = jnp.where((group == 4) | (group == 6), corner, col_a)
    col_b = jnp.where((group == 5) | (group == 7), corner, col_b)
    col_a = swap(col_a, COL, 1)
    col_b = swap_odd(col_b, COL)
    image = late_call(nu, basis, pair, jacobian, flags, image)
    test, gram = finish_call(row_scale, image, row_a, row_b, col_a, col_b, hot, coef, base)
    gram = gram + swap(gram, "col_1", 1)
    for axis in ("col_0", "row_1", "row_0"):
        one, three, two = (cross(gram, axis, k) for k in (1, 3, 2))
        terms = (one, three, two, gram)
        gram = (one + three) + (two + gram)
    factor, step, test = solve_call(row_scale, *terms, test)
    return (test, factor, step.reshape(K))


def solution(mesh):
    torus = Mesh(mesh.devices.reshape(4, 4, 4, 2), ("row_0", "row_1", "col_0", "col_1"))
    in_specs = (
        P(None, None, ROW_COL),
        P(None, None, ROW_COL),
        P(None, ROW_COL),
        P(None, None, None, ROW_COL),
        P(ROW_COL),
        P(),
        P(ROW_COL),
        P(None, None, ROW_COL),
        P(ROW_COL),
        P(ROW_COL),
        P(),
        P(None, ROW_COL),
    )
    out_specs = (P(None, None, ROW_COL), P(), P())
    return jax.shard_map(local, mesh=torus, in_specs=in_specs, out_specs=out_specs, check_vma=False)
```

```python
import functools

import jax
import jax.numpy as jnp
from jax import lax
from jax.experimental import pallas as pl
from jax.experimental.pallas import tpu as pltpu
from jax.sharding import Mesh
from jax.sharding import PartitionSpec as P

ROW = ("row_0", "row_1")
COL = ("col_0", "col_1")
ROW_COL = ROW + COL
F = 5
K = 96
C = 512
N = 1024
S = 160
FK = F * K
HALF = FK // 2
BF = jnp.bfloat16
F32 = jnp.float32
VMEM_LIMIT = 48 * 1024 * 1024


def vmem(count):
    return [pl.BlockSpec(memory_space=pltpu.VMEM)] * count


def one_hot(row):
    cells = lax.broadcasted_iota(jnp.int16, (C, row.shape[1]), 0)
    return jnp.where(cells == row.astype(jnp.int16), jnp.ones((), BF), jnp.zeros((), BF))


def dot_nn(a, b):
    return lax.dot_general(a, b, (((1,), (0,)), ((), ())), preferred_element_type=F32)


def dot_nt(a, b):
    return lax.dot_general(a, b, (((1,), (1,)), ((), ())), preferred_element_type=F32)


def blocks_of(x):
    ends = [0, 32, 64, 96, 128, 136, 144, 152, 160]
    return [x[..., ends[m] : ends[m + 1]] for m in range(8)]


def pad_like(x, width, fill):
    return jnp.full(x.shape[:-1] + (width,), fill, x.dtype)


def send_order(x, fill, odd_i, odd_j):
    b = blocks_of(x)
    p16, p32 = pad_like(x, 16, fill), pad_like(x, 32, fill)
    corner = jnp.concatenate([b[4], b[5], p16, p16, b[6], b[7], p32, p32], axis=-1)
    lane = lax.broadcasted_iota(jnp.int32, corner.shape, corner.ndim - 1)
    last = corner.ndim - 1
    other = jnp.where((lane // 8) % 2 == 0, pltpu.roll(corner, 120, last), pltpu.roll(corner, 8, last))
    corner = jnp.where(odd_j, corner, other)
    row = jnp.concatenate(
        [b[1], p16, corner[..., 48:64], b[0], corner[..., 0:16], p16], axis=-1
    )
    col = jnp.concatenate([b[3], p32, b[2], p32], axis=-1)
    row = jnp.where(odd_i, pltpu.roll(row, 64, last), row)
    col = jnp.where(odd_j, pltpu.roll(col, 64, last), col)
    return row, col


def receive_order(x, odd_i, odd_j):
    b = blocks_of(x)
    p8, p32 = pad_like(x, 8, -1), pad_like(x, 32, -1)
    row = jnp.concatenate([b[0], p32, b[1], p32], axis=-1)
    row = jnp.where(odd_i, pltpu.roll(row, 64, 1), row)
    even = jnp.concatenate([b[2], b[4], p8, b[6], p8, b[3], p8, b[5], p8, b[7]], axis=-1)
    odd = jnp.concatenate([b[3], b[5], p8, b[7], p8, b[2], p8, b[4], p8, b[6]], axis=-1)
    return row, jnp.where(odd_j, odd, even)


BLOCK_AIMS = (
    (0, -1, 0), (32, 1, 0), (64, 0, -1), (96, 0, 1),
    (128, -1, -1), (136, -1, 1), (144, 1, -1), (152, 1, 1),
)


def parities():
    return lax.axis_index("row_1") % 2 == 1, lax.axis_index("col_1") % 2 == 1


def ghost_kernel(count_hbm, cell_hbm, jac_hbm, basis_hbm, pair_hbm, flag_hbm, face_hbm, diag_hbm, arrive_hbm,
                 coord_hbm, base_hbm, nu_hbm, row_a, row_b, col_a, col_b, basis_ref, pair_ref, flag_ref, face_ref,
                 diag_ref, arrive_ref, coord_ref, base_ref, nu_ref, count_ref, cell_ref, jac_ref, val, sems):
    pairs = (
        (basis_hbm, basis_ref), (cell_hbm, cell_ref), (count_hbm, count_ref), (jac_hbm, jac_ref),
        (face_hbm, face_ref), (pair_hbm, pair_ref), (flag_hbm, flag_ref), (diag_hbm, diag_ref),
        (arrive_hbm, arrive_ref), (coord_hbm, coord_ref), (base_hbm, base_ref),
        (nu_hbm, nu_ref),
    )
    copies = [pltpu.make_async_copy(src, dst, sems.at[i]) for i, (src, dst) in enumerate(pairs)]
    fields = [
        pltpu.make_async_copy(basis_hbm.at[f * K : (f + 1) * K], basis_ref.at[f * K : (f + 1) * K], sems.at[12 + f])
        for f in range(F)
    ]
    for copy in copies[1:3] + fields + copies[3:]:
        copy.start()
    odd_i, odd_j = parities()
    copies[1].wait()
    copies[2].wait()
    lane = lax.broadcasted_iota(jnp.int32, (1, S), 1)
    at_i = lax.axis_index("row_0") * lax.axis_size("row_1") + lax.axis_index("row_1")
    at_j = lax.axis_index("col_0") * lax.axis_size("col_1") + lax.axis_index("col_1")
    end_i = lax.axis_size("row_0") * lax.axis_size("row_1") - 1
    end_j = lax.axis_size("col_0") * lax.axis_size("col_1") - 1
    limit = jnp.zeros((1, S), jnp.int32)
    for block, (start, dr, dc) in enumerate(BLOCK_AIMS):
        count = count_ref[0:1, block : block + 1]
        if dr:
            count = jnp.where(at_i == (0 if dr < 0 else end_i), 0, count)
        if dc:
            count = jnp.where(at_j == (0 if dc < 0 else end_j), 0, count)
        limit = jnp.where(lane >= start, count + start, limit)
    index = jnp.where(lane < limit, cell_ref[...], -1)
    hot = one_hot(jnp.concatenate(send_order(index, -1, odd_i, odd_j), axis=-1))
    copies[3].wait()
    weights = [jnp.concatenate(send_order(jac_ref[g], 0.0, odd_i, odd_j), axis=-1) for g in range(F)]
    for f in range(F):
        fields[f].wait()
        val[f] = dot_nn(basis_ref[f * K : (f + 1) * K], hot)
    low = lax.broadcasted_iota(jnp.int32, (1, 128), 1) < 64
    parts = []
    for g in range(F):
        total = weights[g][0:1] * val[0]
        for f in range(1, F):
            total = total + weights[g][f : f + 1] * val[f]
        parts.append(total)
    full = jnp.concatenate(parts, axis=0)
    for tile, first, second in ((0, row_a, row_b), (1, col_a, col_b)):
        wide = full[:, tile * 128 : (tile + 1) * 128]
        top, bottom = wide[:HALF], wide[HALF:]
        first[...] = jnp.where(low, top, pltpu.roll(bottom, 64, 1)).astype(BF)
        second[...] = jnp.where(low, pltpu.roll(top, 64, 1), bottom).astype(BF)
    for copy in copies[4:]:
        copy.wait()


def ghost_call(counts, cells, jacobian, *loaded):
    message = jax.ShapeDtypeStruct((HALF, 128), BF)
    operands = [pltpu.with_memory_space_constraint(x, pltpu.MemorySpace.HBM) for x in (counts, cells, jacobian) + loaded]
    return pl.pallas_call(
        ghost_kernel,
        out_shape=(message,) * 4 + tuple(jax.ShapeDtypeStruct(x.shape, x.dtype) for x in loaded),
        in_specs=[pl.BlockSpec(memory_space=pltpu.MemorySpace.HBM)] * len(operands),
        out_specs=tuple(vmem(4 + len(loaded))),
        scratch_shapes=[
            pltpu.VMEM((1, 8), jnp.int32),
            pltpu.VMEM((1, S), jnp.int32),
            pltpu.VMEM((F, F, S), F32),
            pltpu.VMEM((F, K, 256), F32),
            pltpu.SemaphoreType.DMA((17,)),
        ],
        compiler_params=pltpu.CompilerParams(vmem_limit_bytes=VMEM_LIMIT),
        name="ghost",
    )(*operands)


BLOCK = 256
EARLY = 3
LATE = 1
CHUNK = 32
WIDE = FK + 16


def face_blocks(first_block, count, nu_ref, basis, pair_ref, jac_ref, flag_ref, hot, got, add):
    for block in range(count):
        base = (first_block + block) * BLOCK
        lanes = slice(base, base + BLOCK)
        left = 2 * block * BLOCK
        both = slice(left, left + 2 * BLOCK)
        hot[:, left : left + BLOCK] = one_hot(pair_ref[0:1, lanes])
        hot[:, left + BLOCK : left + 2 * BLOCK] = one_hot(pair_ref[1:2, lanes])
        got[:, both] = dot_nn(basis, hot[:, both]).astype(BF)
        flags = flag_ref[0:1, lanes].astype(F32)
        add[FK:, both] = jnp.broadcast_to(jnp.concatenate([flags, flags], axis=1), (16, 2 * BLOCK)).astype(BF)
        for tile in range(BLOCK // 128):
            here = slice(base + tile * 128, base + (tile + 1) * 128)
            at_a = slice(left + tile * 128, left + (tile + 1) * 128)
            at_b = slice(left + BLOCK + tile * 128, left + BLOCK + (tile + 1) * 128)
            damps = [nu_ref[0:1, g : g + 1] * flags[:, tile * 128 : (tile + 1) * 128] for g in range(F)]
            for start in range(0, K, CHUNK):
                a = [got[f * K + start : f * K + start + CHUNK, at_a].astype(F32) for f in range(F)]
                b = [got[f * K + start : f * K + start + CHUNK, at_b].astype(F32) for f in range(F)]
                for g in range(F):
                    to_a = (jac_ref[g, g, 0:1, here] - damps[g]) * b[g]
                    to_b = (jac_ref[g, g, 1:2, here] - damps[g]) * a[g]
                    for f in range(F):
                        if f != g:
                            to_a = to_a + jac_ref[g, f, 0:1, here] * b[f]
                            to_b = to_b + jac_ref[g, f, 1:2, here] * a[f]
                    rows = slice(g * K + start, g * K + start + CHUNK)
                    add[rows, at_a] = to_a.astype(BF)
                    add[rows, at_b] = to_b.astype(BF)
    return dot_nt(add[...], hot[...])


def add_diagonal(image_ref, basis_ref, nu_ref, diag_ref):
    for tile in range(C // 128):
        here = slice(tile * 128, (tile + 1) * 128)
        flagged = image_ref[FK : FK + 1, here]
        own = [diag_ref[g, g : g + 1, here] + nu_ref[0:1, g : g + 1] * flagged for g in range(F)]
        for start in range(0, K, CHUNK):
            v = [basis_ref[f * K + start : f * K + start + CHUNK, here].astype(F32) for f in range(F)]
            for g in range(F):
                rows = slice(g * K + start, g * K + start + CHUNK)
                total = image_ref[rows, here] + own[g] * v[g]
                for f in range(F):
                    if f != g:
                        total = total + diag_ref[g, f : f + 1, here] * v[f]
                image_ref[rows, here] = total


def early_kernel(nu_ref, basis_ref, diag_ref, pair_ref, jac_ref, flag_ref, cell_ref, coord_ref,
                 image_ref, hot_ref, coef_ref, hot, got, add):
    odd_i, odd_j = parities()
    hot_ref[...] = one_hot(jnp.concatenate(receive_order(cell_ref[...], odd_i, odd_j), axis=-1))
    coord = coord_ref[...]
    high = coord.astype(BF).astype(F32)
    row = lax.broadcasted_iota(jnp.int32, (16, K), 0)
    coef_ref[...] = jnp.where(row == 0, high, jnp.where(row == 1, coord - high, 0.0)).astype(BF)
    image_ref[...] = face_blocks(0, EARLY, nu_ref, basis_ref[...], pair_ref, jac_ref, flag_ref, hot, got, add)
    add_diagonal(image_ref, basis_ref, nu_ref, diag_ref)


def late_kernel(nu_ref, basis_ref, pair_ref, jac_ref, flag_ref, image_ref, out_ref, hot, got, add):
    image = face_blocks(EARLY, LATE, nu_ref, basis_ref[...], pair_ref, jac_ref, flag_ref, hot, got, add)
    flagged = image[FK : FK + 1]
    for g in range(F):
        rows = slice(g * K, (g + 1) * K)
        damp = (nu_ref[0:1, g : g + 1] * flagged) * basis_ref[rows].astype(F32)
        out_ref[rows] = (image_ref[rows] + image[rows]) + damp


def face_scratch(count):
    return [pltpu.VMEM((rows, 2 * count * BLOCK), BF) for rows in (C, FK, WIDE)]


def face_cost(count):
    return pl.CostEstimate(flops=count * 1_250_000_000, bytes_accessed=2_000_000, transcendentals=0)


def early_call(nu, basis, diag, pair, jacobian, flags, cells, coords):
    return pl.pallas_call(
        early_kernel,
        out_shape=(
            jax.ShapeDtypeStruct((WIDE, C), F32),
            jax.ShapeDtypeStruct((C, 256), BF),
            jax.ShapeDtypeStruct((16, K), BF),
        ),
        in_specs=vmem(8),
        out_specs=tuple(vmem(3)),
        scratch_shapes=face_scratch(EARLY),
        compiler_params=pltpu.CompilerParams(vmem_limit_bytes=VMEM_LIMIT),
        cost_estimate=face_cost(EARLY),
        name="early_faces",
    )(nu, basis, diag, pair, jacobian, flags, cells, coords)


def late_call(nu, basis, pair, jacobian, flags, image):
    return pl.pallas_call(
        late_kernel,
        out_shape=jax.ShapeDtypeStruct((FK, C), F32),
        in_specs=vmem(6),
        out_specs=vmem(1)[0],
        scratch_shapes=face_scratch(LATE),
        compiler_params=pltpu.CompilerParams(vmem_limit_bytes=VMEM_LIMIT),
        cost_estimate=face_cost(LATE),
        name="late_faces",
    )(nu, basis, pair, jacobian, flags, image)


ROWS = 128
PACK = 56
MID = K // 2


def grids(rows, first=0):
    row = lax.broadcasted_iota(jnp.int32, (rows, 128), 0) + first
    return row, lax.broadcasted_iota(jnp.int32, (rows, 128), 1)


def pack_gram(gram):
    row, lane = grids(MID)
    lower = pltpu.roll(gram[MID:K], 128 - MID, 1)
    upper = jnp.where((lane < MID) & (lane < row), lower, gram[:MID])
    row, lane = grids(MID, MID)
    diagonal = jnp.sum(jnp.where(row == lane, gram[MID:K], 0.0), axis=0, keepdims=True)
    row, lane = grids(8)
    tail = jnp.where(row == 0, gram[K : K + 1], jnp.where(row == 1, diagonal, 0.0))
    return jnp.concatenate([upper, tail], axis=0)


def unpack_gram(packed, work):
    flipped = packed.T
    row, lane = grids(MID)
    first = packed[:MID]
    turned = jnp.concatenate([flipped, jnp.zeros((128, 128 - PACK), F32)], axis=1)
    work[:MID] = jnp.where((lane < MID) & (lane < row), turned[:MID], first)
    half = jnp.where(lane < row, first, turned[:MID])
    half = pltpu.roll(jnp.where(lane < MID, half, turned[MID:K]), MID, 1)
    half = jnp.where(lane < MID, turned[MID:K], half)
    work[MID:K] = jnp.where(lane == row + MID, packed[MID + 1 : MID + 2], half)
    row, lane = grids(8)
    work[K : K + 8] = jnp.where(row == 0, packed[MID : MID + 1], 0.0)


def finish_kernel(row_scale, image_ref, row_a, row_b, col_a, col_b, hot_ref, coef_ref, base_ref,
                  test_ref, gram_ref, arrive, stack):
    low = lax.broadcasted_iota(jnp.int32, (1, 128), 1) < 64
    for tile, first, second in ((0, row_a, row_b), (1, col_a, col_b)):
        here = slice(tile * 128, (tile + 1) * 128)
        one, two = first[...].astype(F32), second[...].astype(F32)
        arrive[:HALF, here] = jnp.where(low, one, pltpu.roll(two, 64, 1)).astype(BF)
        arrive[HALF:, here] = jnp.where(low, pltpu.roll(one, 64, 1), two).astype(BF)
    test = (image_ref[...] + dot_nt(arrive[...], hot_ref[...])).astype(BF)
    coef = coef_ref[...]
    first_row = lax.broadcasted_iota(jnp.int32, (ROWS - K, C), 0) == 0
    for f in range(F):
        part = test[f * K : (f + 1) * K]
        here = slice(f * C, (f + 1) * C)
        test_ref[f] = part
        stack[:K, here] = part
        product = dot_nn(coef, part)
        value = base_ref[f : f + 1] + row_scale * (product[0:1] + product[1:2])
        stack[K:ROWS, here] = jnp.where(first_row, value, 0.0).astype(BF)
    whole = stack[...]
    gram = dot_nt(whole, whole) * (row_scale * row_scale)
    gram_ref[...] = pack_gram(gram)


def finish_call(row_scale, image, row_a, row_b, col_a, col_b, hot, coef, base):
    return pl.pallas_call(
        functools.partial(finish_kernel, row_scale),
        out_shape=(jax.ShapeDtypeStruct((F, K, C), BF), jax.ShapeDtypeStruct((PACK, 128), F32)),
        in_specs=vmem(8),
        out_specs=tuple(vmem(2)),
        scratch_shapes=[pltpu.VMEM((FK, 256), BF), pltpu.VMEM((ROWS, F * C), BF)],
        compiler_params=pltpu.CompilerParams(vmem_limit_bytes=VMEM_LIMIT),
        name="finish",
    )(image, row_a, row_b, col_a, col_b, hot, coef, base)


TILES = 13


def solve_kernel(row_scale, one_ref, three_ref, two_ref, own_ref, test_ref, factor_ref, step_ref, out_hbm, work, sem):
    copy = pltpu.make_async_copy(test_ref, out_hbm, sem.at[0])
    copy.start()
    unpack_gram((one_ref[...] + three_ref[...]) + (two_ref[...] + own_ref[...]), work)
    lane = lax.broadcasted_iota(jnp.int32, (8, 128), 1)
    sub = lax.broadcasted_iota(jnp.int32, (8, 128), 0)

    def spread_row(tile, p):
        return jnp.broadcast_to(tile[p : p + 1], (8, 128))

    def spread_lane(tile, j):
        place = jnp.full((8, 128), j, jnp.int32)
        return jnp.take_along_axis(tile, place, axis=1, mode="promise_in_bounds")

    tiles = [work[8 * t : 8 * t + 8] for t in range(TILES)]
    for panel in range(12):
        start = 8 * panel
        here = tiles[panel]
        columns = [[spread_lane(tiles[t], start + p) for p in range(8)] for t in range(TILES)]
        rows = [spread_row(here, p) for p in range(8)]
        d = {(p, q): spread_row(columns[panel][q], p) for p in range(8) for q in range(p, 8)}
        m = {}
        inverse = []
        for p in range(8):
            recip = 1.0 / d[p, p]
            inverse.append(recip)
            for q in range(p + 1, 8):
                m[p, q] = d[p, q] * recip
            for q in range(p + 1, 8):
                rows[q] = rows[q] - m[p, q] * rows[p]
                for r in range(q, 8):
                    d[q, r] = d[q, r] - m[p, q] * d[p, r]
        out = jnp.zeros((8, 128), F32)
        for p in range(8):
            out = jnp.where(sub == p, rows[p] * lax.rsqrt(d[p, p]), out)
        out = jnp.where(lane >= start + sub, out, 0.0)
        factor_ref[start : start + 8, :] = out[:, :97]
        for p in range(7, -1, -1):
            rows[p] = rows[p] * inverse[p]
            for q in range(p + 1, 8):
                rows[p] = rows[p] - m[p, q] * rows[q]
        order = [panel + 1] + [t for t in range(TILES) if t not in (panel, panel + 1)]
        for t in order:
            product = [columns[t][p] * rows[p] for p in range(8)]
            while len(product) > 1:
                product = [product[i] + product[i + 1] for i in range(0, len(product), 2)]
            tiles[t] = tiles[t] - product[0]
        new = rows[0]
        for p in range(1, 8):
            new = jnp.where(sub == p, rows[p], new)
        tiles[panel] = new
    last = tiles[12]
    factor_ref[96:97, :] = jnp.where(lane[:1] == 96, jnp.sqrt(last[0:1]), 0.0)[:, :97]
    step = jnp.zeros((1, 128), F32)
    for t in range(12):
        column = spread_lane(tiles[t], 96)
        step = step + jnp.sum(jnp.where(lane == 8 * t + sub, column, 0.0), axis=0, keepdims=True)
    step_ref[...] = step[:, :96] * (-1.0 / row_scale)
    copy.wait()


def solve_call(row_scale, *terms):
    return pl.pallas_call(
        functools.partial(solve_kernel, row_scale),
        out_shape=(
            jax.ShapeDtypeStruct((97, 97), F32),
            jax.ShapeDtypeStruct((1, 96), F32),
            jax.ShapeDtypeStruct((F, K, C), BF),
        ),
        in_specs=vmem(5),
        out_specs=tuple(vmem(2)) + (pl.BlockSpec(memory_space=pltpu.MemorySpace.HBM),),
        scratch_shapes=[pltpu.VMEM((104, 128), F32), pltpu.SemaphoreType.DMA((1,))],
        compiler_params=pltpu.CompilerParams(vmem_limit_bytes=VMEM_LIMIT),
        name="solve",
    )(*terms)


def swap(x, axis, step):
    count = lax.axis_size(axis)
    return lax.ppermute(x, axis, [(i, i ^ step) for i in range(count)])


def cross(x, axis, step):
    pairs = [(2 * i + c, 2 * (i ^ step) + 1 - c) for i in range(lax.axis_size(axis)) for c in range(2)]
    return lax.ppermute(x, (axis, "col_1"), pairs)


def swap_odd(x, axis):
    count = lax.axis_size(axis)
    return lax.ppermute(x, axis, [(i, (i + 1) % count if i % 2 else (i - 1) % count) for i in range(count)])


def local(
    reduced_basis,
    cell_jacobian,
    face_cells,
    face_jacobian,
    limiter_flags,
    viscosity,
    ghost_cells,
    ghost_jacobian,
    ghost_counts,
    receive_cells,
    coordinates,
    base_residual,
):
    devices = lax.axis_size(ROW) * lax.axis_size(COL)
    row_scale = (F * C * devices) ** (-0.5)
    basis = reduced_basis.reshape(FK, C)
    jacobian = face_jacobian.transpose(1, 2, 0, 3)
    flags = limiter_flags.reshape(1, N)
    row_a, row_b, col_a, col_b, basis, pair, flags, jacobian, diag, arrive, coords, base, nu = ghost_call(
        ghost_counts.reshape(1, 8), ghost_cells.reshape(1, S), ghost_jacobian,
        basis, face_cells, flags, jacobian, cell_jacobian, receive_cells.reshape(1, S),
        coordinates.reshape(1, K), base_residual, viscosity.reshape(1, F),
    )
    row_a = swap(row_a, ROW, 1)
    row_b = swap_odd(row_b, ROW)
    image, hot, coef = early_call(
        nu, basis, diag, pair, jacobian, flags, arrive, coords
    )
    group = (lax.broadcasted_iota(jnp.int32, (HALF, 128), 1) % 64) // 8
    corner = row_a + row_b
    col_a = jnp.where((group == 4) | (group == 6), corner, col_a)
    col_b = jnp.where((group == 5) | (group == 7), corner, col_b)
    col_a = swap(col_a, COL, 1)
    col_b = swap_odd(col_b, COL)
    image = late_call(nu, basis, pair, jacobian, flags, image)
    test, gram = finish_call(row_scale, image, row_a, row_b, col_a, col_b, hot, coef, base)
    gram = gram + swap(gram, "col_1", 1)
    for axis in ("col_0", "row_1", "row_0"):
        one, three, two = (cross(gram, axis, k) for k in (1, 3, 2))
        terms = (one, three, two, gram)
        gram = (one + three) + (two + gram)
    factor, step, test = solve_call(row_scale, *terms, test)
    return (test, factor, step.reshape(K))


def solution(mesh):
    torus = Mesh(mesh.devices.reshape(4, 4, 4, 2), ("row_0", "row_1", "col_0", "col_1"))
    in_specs = (
        P(None, None, ROW_COL),
        P(None, None, ROW_COL),
        P(None, ROW_COL),
        P(None, None, None, ROW_COL),
        P(ROW_COL),
        P(),
        P(ROW_COL),
        P(None, None, ROW_COL),
        P(ROW_COL),
        P(ROW_COL),
        P(),
        P(None, ROW_COL),
    )
    out_specs = (P(None, None, ROW_COL), P(), P())
    return jax.shard_map(local, mesh=torus, in_specs=in_specs, out_specs=out_specs, check_vma=False)
```
